256 devices in a mesh: comp: 8 (over y, core), patch: 32 (over x, z).
Axes of the slice: x: 4, y: 4, z: 8, core: 2. Of those that a mesh axis runs over, the one named last changes fastest.
Arguments:
- load_cases: float32 [32, 786432], P(None, ('comp', 'patch')), may hold values from -6 to 6
- mass_diag: float32 [786432], P(('comp', 'patch')), may hold values from 0.5 to 2
- stiffness: float32 [12288, 64, 256], P(('comp', 'patch')), may hold values from -0.375 to 0.375
- block_cols: int32 [12288, 4], P(('comp', 'patch')), may hold values from 0 to 47
- trace_dofs: int32 [262144], P(('comp', 'patch')), may hold values from 0 to 3071
- penalty: float32 [262144], P(('comp', 'patch')), may hold values from 0.5 to 2
- cell_partials: float32 [32, 131072], P(None, ('comp', 'patch')), may hold values from -6 to 6
- cell_owner: int32 [131072, 1], P(('comp', 'patch')), may hold values from 0 to 31; in each aligned block of 512 rows (0 to 511, 512 to 1023, ...) at most 64 rows name the same one
- cell_dof: int32 [131072], P(('comp', 'patch')), may hold values from 0 to 3071
Outputs:
- solution: float32 [32, 786432], P(None, ('comp', 'patch'))
- residual: float32 [32, 786432], P(None, ('comp', 'patch'))
The draws below stay inside these ranges and needn't reach their ends.
Inputs may be any that keep to these rules, and one draw needn't show every extreme that they name: `cell_owner`: no more than 64 trimmed cells of one patch name the same owner, a bound that some block reaches of them.
All inputs are finite; a program needn't handle non-finite values.
Results may differ from the reference program's by a relative error of at most 0.0003.
Values sent between devices are 32-bit elements; how exact they have to be, the bound alone decides.
A program may use at most 64 MiB of HBM per device.

```python
import math
import jax
import jax.numpy as jnp
import numpy as np
from jax import lax

CASES = 32
BLK = 64
KNB = 4
NB = 48
TR = 1024
NCELL = 512
ITERS = 2
CAP = 64
DOFS = 786432
N_PATCH = 32
DEVICES = 256


def touch_ends(array, key, low, largest):
    shape = array.shape
    place = [jax.random.randint(jax.random.fold_in(key, axis), (), 0, shape[axis]) for axis in range(len(shape))]
    array = array.at[tuple(place)].set(low)
    longest = shape.index(max(shape))
    place[longest] = (place[longest] + 1) % shape[longest]
    return array.at[tuple(place)].set(largest)


def shard_levels(stream_key, shape, cuts, least, largest):
    def one(position, parts):
        steps = jax.random.uniform(jax.random.fold_in(jax.random.fold_in(stream_key, 6), position), (parts,), jnp.float32, least / len(cuts), largest / len(cuts))
        return jnp.repeat(jnp.exp(steps), shape[position] // parts).reshape((-1,) + (1,) * (len(shape) - position - 1))

    factor_of = one(*cuts[0])
    for cut in cuts[1:]:
        factor_of = factor_of * one(*cut)
    return factor_of


def deal_out(own_key, own, number, rows, number_of, top, limit, lean):
    order = jax.random.permutation(own_key, number_of)
    heavy_load, usual = portions_of(number_of, rows * top, limit, lean, True), portions_of(number_of, rows * top, limit, lean, False)
    places = jnp.arange(number_of)

    def named(tallies, offset_by):
        used = int((tallies > 0).sum())
        fixed = max(1, used // 4)
        passed = fixed + (places - fixed + offset_by * (used - fixed)) % max(1, number_of - fixed)
        return jnp.zeros((number_of,), jnp.int32).at[order[jnp.where(places < fixed, places, passed)]].set(jnp.asarray(tallies, jnp.int32))

    tallies = jnp.where(number % 4 == 0, named(heavy_load, number // 4), named(usual, number - number // 4 - 1))
    mixed = jax.random.permutation(jax.random.fold_in(own, 3), number_of)
    donor, receiver = mixed[0:number_of // 2 * 2:2], mixed[1:number_of // 2 * 2:2]
    room = jnp.minimum(tallies[donor] - 1, limit - tallies[receiver]) // 2
    room = jnp.where((donor == order[0]) | (receiver == order[0]) | (tallies[receiver] == 0), 0, jnp.maximum(room, 0))
    passed = jax.random.randint(jax.random.fold_in(own, 4), (number_of // 2,), 0, 1 << 20) % (room + 1)
    tallies = tallies.at[donor].add(-passed).at[receiver].add(passed)
    labels = jnp.searchsorted(jnp.cumsum(tallies), jnp.arange(rows * top), side="right").astype(jnp.int32)
    listing = labels.reshape(top, rows).T
    listing = listing[jax.random.permutation(jax.random.fold_in(own, 1), rows)]
    offset_by = jax.random.randint(jax.random.fold_in(own, 2), (rows, 1), 0, top)
    return jnp.take_along_axis(listing, (jnp.arange(top)[None, :] + offset_by) % top, axis=1)


def portions_of(number_of, total, bound, lean, full):
    portions = [(1 << 20) // math.isqrt(grade ** lean) + 1 for grade in range(1, number_of + 1)]
    largest = bound if full else min(bound, max(-(-total // number_of), total * portions[0] // sum(portions)))
    least = 1 if total - largest >= number_of - 1 else 0
    holding, surplus = [largest] + [least] * (number_of - 1), total - largest - least * (number_of - 1)
    while surplus > 0:
        candidates = [i for i in range(1, number_of) if holding[i] < largest] or [i for i in range(1, number_of) if holding[i] < bound]
        mass, budget = sum([portions[i] for i in candidates]), surplus
        for i in candidates:
            extra = min(bound - holding[i], max(1, budget * portions[i] // mass), surplus)
            holding[i] = holding[i] + extra
            surplus = surplus - extra
    return np.array(holding)


def normal_values(stream_key, extent, spread, bound, pieces=(), kind=jnp.bfloat16):
    array = jax.random.normal(stream_key, extent, jnp.float32) * spread
    if len(pieces) > 0:
        array = shard_levels(stream_key, extent, pieces, -0.22, 0.18) * array
    return jnp.clip(array, min=-bound, max=bound).astype(kind)


def setup_inputs(seed: int = 0) -> dict:
    key_list = jax.random.split(jax.random.key(seed), 10)
    load_cases = normal_values(key_list[0], (CASES, DOFS), 1.0, 6.0, ((1, 256),), jnp.float32)
    mass_diag = jnp.clip(0.5 + 1.5 * jax.random.uniform(key_list[1], (DOFS,), jnp.float32) ** shard_levels(key_list[1], (DOFS,), ((0, 256),), -0.2, 0.2), 0.5, 2.0)
    stiffness = normal_values(key_list[2], (DEVICES * NB, BLK, KNB * BLK), (KNB * BLK) ** -0.5, 0.375, ((0, 256),), jnp.float32)
    block_cols = touch_ends(jax.random.randint(key_list[3], (DEVICES * NB, KNB), 0, NB), jax.random.fold_in(key_list[3], 1), 0, NB - 1).astype(jnp.int32)
    trace_dofs = touch_ends(jax.random.randint(key_list[4], (DEVICES * TR,), 0, NB * BLK), jax.random.fold_in(key_list[4], 1), 0, (NB * BLK) - 1).astype(jnp.int32)
    penalty = jnp.clip(jnp.exp(math.log(2.0) - 1.3862944 * jax.random.uniform(key_list[5], (DEVICES * TR,), jnp.float32) ** shard_levels(key_list[5], (DEVICES * TR,), ((0, 256),), -0.2, 0.2)), 0.5, 2.0)
    cell_partials = normal_values(key_list[6], (CASES, DEVICES * NCELL), 1.0, 6.0, ((1, 256),), jnp.float32)
    cell_owner_keys = jax.random.split(jax.random.fold_in(key_list[7], 1), (DEVICES * NCELL) // NCELL)
    cell_owner_turns = jax.random.permutation(jax.random.fold_in(key_list[7], 3), (DEVICES * NCELL) // NCELL)
    cell_owner = jax.vmap(lambda own, number: deal_out(jax.random.fold_in(key_list[7], 2), own, number, NCELL, N_PATCH, 1, CAP, 2))(cell_owner_keys, cell_owner_turns).reshape((DEVICES * NCELL, 1))
    cell_dof = touch_ends(jax.random.randint(key_list[8], (DEVICES * NCELL,), 0, NB * BLK), jax.random.fold_in(key_list[8], 1), 0, (NB * BLK) - 1).astype(jnp.int32)
    return dict(load_cases=load_cases, mass_diag=mass_diag, stiffness=stiffness, block_cols=block_cols, trace_dofs=trace_dofs, penalty=penalty, cell_partials=cell_partials, cell_owner=cell_owner, cell_dof=cell_dof)


def gram_matrix(first, second):
    return jnp.dot(first.astype(jnp.float32), second.T.astype(jnp.float32), precision=lax.Precision.HIGHEST, preferred_element_type=jnp.float32)

def small_solve(matrix, target):
    factor = jnp.linalg.cholesky(matrix)
    return jax.scipy.linalg.cho_solve((factor, True), target)

def local_blocks(inputs):
    field_dev, stiff_dev, cols_dev = inputs
    blocks = field_dev.reshape(CASES, NB, BLK)
    neighbour_vals = blocks[:, cols_dev, :].reshape(CASES, NB, KNB * BLK)
    strain = jnp.einsum('cnk,nrk->cnr', neighbour_vals, stiff_dev, precision=lax.Precision.HIGHEST)
    transposed = jnp.einsum('cnr,nrk->cnk', strain, stiff_dev, precision=lax.Precision.HIGHEST)
    transposed = transposed.reshape(CASES, NB * KNB, BLK)
    folded = jnp.zeros((CASES, NB, BLK), jnp.float32).at[:, cols_dev.reshape(-1), :].add(transposed)
    return folded.reshape(CASES, NB * BLK)

def add_jump(totals, indices, jump_term):
    return totals.at[:, indices].add(jump_term)

def apply_operator(field, mass_diag, stiff_all, cols_all, trace_all, pen_all):
    per_device = field.reshape(CASES, DEVICES, NB * BLK).transpose(1, 0, 2)
    folded = lax.map(local_blocks, (per_device, stiff_all, cols_all))
    own_trace = jnp.take_along_axis(per_device, trace_all[:, None, :], axis=2)
    device_ids = jnp.arange(DEVICES, dtype=jnp.int32)
    partner_ids = device_ids // N_PATCH * N_PATCH + (device_ids % N_PATCH + N_PATCH // 2) % N_PATCH
    weight = pen_all * pen_all[partner_ids]
    jump_term = weight[:, None, :] * (own_trace - own_trace[partner_ids])
    folded = jax.vmap(add_jump)(folded, trace_all, jump_term)
    return mass_diag[None, :] * field + folded.transpose(1, 0, 2).reshape(CASES, DEVICES * NB * BLK)

def reference(load_cases, mass_diag, stiffness, block_cols, trace_dofs, penalty, cell_partials, cell_owner, cell_dof):
    cell_device = jnp.arange(DEVICES * NCELL, dtype=jnp.int32) // NCELL
    target_device = cell_device // N_PATCH * N_PATCH + cell_owner[:, 0].astype(jnp.int32)
    flat_target = target_device * (NB * BLK) + cell_dof.astype(jnp.int32)
    right_side = load_cases.at[:, flat_target].add(cell_partials)
    stiff_all = stiffness.reshape(DEVICES, NB, BLK, KNB * BLK)
    cols_all = block_cols.reshape(DEVICES, NB, KNB)
    trace_all = trace_dofs.reshape(DEVICES, TR)
    pen_all = penalty.reshape(DEVICES, TR)
    solution = jnp.zeros_like(right_side)
    residual = right_side
    direction = right_side
    norm_now = gram_matrix(residual, residual)
    for turn_index in range(ITERS):
        image_field = apply_operator(direction, mass_diag, stiff_all, cols_all, trace_all, pen_all)
        curvature = gram_matrix(direction, image_field)
        step_size = small_solve(curvature, norm_now)
        solution = solution + jnp.dot(step_size.T.astype(jnp.float32), direction.astype(jnp.float32), precision=lax.Precision.HIGHEST, preferred_element_type=jnp.float32)
        residual = residual - jnp.dot(step_size.T.astype(jnp.float32), image_field.astype(jnp.float32), precision=lax.Precision.HIGHEST, preferred_element_type=jnp.float32)
        if turn_index + 1 < ITERS:
            norm_next = gram_matrix(residual, residual)
            correction = small_solve(norm_now, norm_next)
            direction = residual + jnp.dot(correction.T.astype(jnp.float32), direction.astype(jnp.float32), precision=lax.Precision.HIGHEST, preferred_element_type=jnp.float32)
            norm_now = norm_next
    return (solution, residual)
```

```python
import functools

import jax
import jax.numpy as jnp
from jax import lax
from jax.experimental import pallas as pl
from jax.experimental.pallas import tpu as pltpu
from jax.sharding import PartitionSpec as P

CAP = 64
GROUP = 256
F32, BF16, I32 = jnp.float32, jnp.bfloat16, jnp.int32
NT = (((1,), (1,)), ((), ()))
NN = (((1,), (0,)), ((), ()))
MESH = pl.DeviceIdType.MESH


def mm(a, b, dims=NN):
    return lax.dot_general(a, b, dims, preferred_element_type=F32)


def split(x):
    hi = x.astype(BF16)
    return hi, (x - hi.astype(F32)).astype(BF16)


def split_rows(x):
    return jnp.concatenate(split(x), axis=0)


def iota(shape, dim):
    return lax.broadcasted_iota(I32, shape, dim)


def ones_where(mask):
    return jnp.where(mask, 1.0, 0.0)


def swap(x):
    return pltpu.roll(x, 64, 1)


def kernel(
    z_size, load_hbm, mass_ref, stiff_hbm, cols_ref, cols_smem, trace_ref, pen_ref, cells_ref, owner_ref,
    cdof_ref, sol_ref, res_ref,
    load, stiff, kk, send, recv, colp, csr_i, csr_f, csr_is, csr_fs, hot, own, part, pen_other,
    r_ref, q_ref, t_ref, s3, vab, ss, tp, run, acc, pay, rc, rx, rz,
    in_sem, a2a_send, a2a_recv, tr_send, tr_recv, red_send, red_recv,
):
    patches, comps = lax.axis_size("patch"), lax.axis_size("comp")
    me, mine = lax.axis_index("patch"), lax.axis_index("comp")
    cases, dofs = load.shape
    groups = dofs // GROUP
    ncell = cells_ref.shape[1]
    traces = trace_ref.shape[1]
    chunks = traces // GROUP
    rows = stiff.shape[0]
    entries = rows * 4
    pairs = rows // 2
    left = iota((1, 128), 1) < 64
    left16 = iota((16, 128), 1) < 64
    left32 = iota((32, 128), 1) < 64

    get_stiff = pltpu.make_async_copy(stiff_hbm, stiff, in_sem.at[0])
    get_load = pltpu.make_async_copy(load_hbm, load, in_sem.at[1])
    get_stiff.start()
    get_load.start()

    barrier = pltpu.get_barrier_semaphore()

    def greet_patch(d, _):
        pl.semaphore_signal(barrier, inc=1, device_id={"patch": lax.rem(me + d, patches)}, device_id_type=MESH)
        return 0

    def greet_comp(d, _):
        pl.semaphore_signal(barrier, inc=1, device_id={"comp": lax.rem(mine + d, comps)}, device_id_type=MESH)
        return 0

    lax.fori_loop(1, patches, greet_patch, 0)
    lax.fori_loop(1, comps, greet_comp, 0)

    owner = owner_ref[...]
    hit = owner == iota((patches, ncell), 0)
    tri = ones_where(iota((ncell, ncell), 0) < iota((ncell, ncell), 1)).astype(BF16)
    before = mm(ones_where(hit).astype(BF16), tri)
    pos = jnp.sum(jnp.where(hit, before, 0.0), axis=0, keepdims=True).astype(I32)
    slot = (owner & 3) * CAP + pos
    slot_hot = ones_where(iota((GROUP, ncell), 0) == slot).astype(BF16)
    cdof = cdof_ref[...]
    row16 = iota((16, ncell), 0)
    dof_rows = jnp.where(row16 == 0, cdof >> 8, jnp.where(row16 == 1, cdof & 255, 0)).astype(F32)
    cell_hi, cell_lo = split(cells_ref[...])
    cell_rows = jnp.concatenate([cell_hi, cell_lo, dof_rows.astype(BF16)], axis=0)
    for g in range(patches // 4):
        mask = jnp.broadcast_to(ones_where((owner >> 2) == g), (16, ncell)).astype(BF16)
        mask = jnp.concatenate([mask] * 5, axis=0)
        packed = mm(cell_rows * mask, slot_hot, NT)
        values = packed[0:32] + packed[32:64]
        places = packed[64:72]
        for half in range(2):
            tile = values[:, half * 128:(half + 1) * 128]
            top, bottom = tile[0:16], tile[16:32]
            place = places[:, half * 128:(half + 1) * 128]
            place_hi, place_lo = place[0:1], place[1:2]
            even = g * 4 + half * 2
            send[even, 0:16] = jnp.where(left16, top, swap(bottom))
            send[even + 1, 0:16] = jnp.where(left16, swap(top), bottom)
            send[even, 16:17] = jnp.where(left, place_hi, swap(place_lo))
            send[even + 1, 16:17] = jnp.where(left, swap(place_hi), place_lo)
    recv[0] = send[me]

    pl.semaphore_wait(barrier, patches + comps - 2)

    other = lax.rem(me + patches // 2, patches)

    def cell_copy(d):
        to = lax.rem(me + d, patches)
        return pltpu.make_async_remote_copy(
            src_ref=send.at[to], dst_ref=recv.at[d], send_sem=a2a_send.at[d], recv_sem=a2a_recv.at[d],
            device_id={"patch": to}, device_id_type=MESH,
        )

    def start_cell(d, _):
        cell_copy(d).start()
        return 0

    pen_copy = pltpu.make_async_remote_copy(
        src_ref=pen_ref, dst_ref=pen_other, send_sem=a2a_send.at[0], recv_sem=a2a_recv.at[0],
        device_id={"patch": other}, device_id_type=MESH,
    )
    lax.fori_loop(1, patches, start_cell, 0)
    pen_copy.start()

    colp[...] = jnp.full((1, GROUP), 255, I32)
    colp[:, 0:entries] = cols_ref[...]
    col = colp[...]
    i0, i1 = iota((GROUP, GROUP), 0), iota((GROUP, GROUP), 1)
    col_of = jnp.transpose(jnp.broadcast_to(col, (GROUP, GROUP)))
    ahead = (col_of < col) | ((col_of == col) & (i0 < i1))
    rank = jnp.sum(jnp.where(ahead, 1, 0), axis=0, keepdims=True)
    at_rank = jnp.transpose(jnp.broadcast_to(rank, (GROUP, GROUP))) == i1
    order = jnp.sum(jnp.where(at_rank, i0, 0), axis=0, keepdims=True)
    ocol = jnp.sum(jnp.where(at_rank, col_of, 0), axis=0, keepdims=True)
    upto = jnp.sum(jnp.where(col_of <= i1, 1, 0), axis=0, keepdims=True)
    same = jnp.sum(jnp.where(col_of == i1, 1, 0), axis=0, keepdims=True)
    lane = iota((1, GROUP), 1)
    csr_i[0:1, :] = jnp.minimum(order, entries - 1)
    csr_i[1:2, :] = jnp.clip(upto - 1, 0, entries - 1)
    csr_f[0:1, :] = ones_where((ocol == pltpu.roll(ocol, 1, 1)) & (lane > 0))
    csr_f[1:2, :] = ones_where(same > 0)
    put_i = pltpu.make_async_copy(csr_i, csr_is, in_sem.at[2])
    put_f = pltpu.make_async_copy(csr_f, csr_fs, in_sem.at[3])
    put_i.start()
    put_f.start()

    for c in range(chunks):
        t_lo = trace_ref[:, c * GROUP:(c + 1) * GROUP] & 255
        hot[c] = ones_where(i0 == t_lo).astype(BF16)

    get_stiff.wait()

    def halve(n, _):
        hi, lo = split(stiff[n])
        kk[n, 0:64] = hi
        kk[n, 64:128] = lo
        return 0

    lax.fori_loop(0, rows, halve, 0)
    put_i.wait()
    put_f.wait()
    get_load.wait()

    def masked_groups(data, high):
        parts = []
        for h in range(groups):
            mask = jnp.broadcast_to(ones_where(high == h), (16, GROUP)).astype(BF16)
            parts.append(data * jnp.concatenate([mask] * 4, axis=0))
        return jnp.concatenate(parts, axis=0)

    acc[...] = jnp.zeros(acc.shape, F32)

    def place_cells(k, _):
        data, highs, lows = [], [], []
        for i in range(2):
            tiles = []
            for j in range(2):
                d = k * 4 + i * 2 + j

                @pl.when(d > 0)
                def _():
                    cell_copy(d).wait_recv()

                tiles.append(recv[d])
            a, b = tiles
            at, bt, ap, bp = a[0:16], b[0:16], a[16:17], b[16:17]
            data.append(jnp.concatenate(
                [jnp.where(left16, at, swap(bt)), jnp.where(left16, swap(at), bt)], axis=0))
            highs.append(jnp.where(left, ap, swap(bp)))
            lows.append(jnp.where(left, swap(ap), bp))
        data = split_rows(jnp.concatenate(data, axis=1))
        high = jnp.concatenate(highs, axis=1).astype(I32)
        low = jnp.concatenate(lows, axis=1).astype(I32)
        low_hot = ones_where(i0 == low).astype(BF16)
        acc[...] += mm(masked_groups(data, high), low_hot, NT)
        return 0

    lax.fori_loop(0, patches // 4, place_cells, 0)
    for h in range(groups):
        lanes = slice(h * GROUP, (h + 1) * GROUP)
        r_ref[:, lanes] = load[:, lanes] + acc[h * 64:h * 64 + 32] + acc[h * 64 + 32:h * 64 + 64]

    def trace_copy(turn, c):
        return pltpu.make_async_remote_copy(
            src_ref=own.at[turn, c], dst_ref=part.at[turn, c], send_sem=tr_send.at[turn, c],
            recv_sem=tr_recv.at[turn, c], device_id={"patch": other}, device_id_type=MESH,
        )

    def halves_of(v_ref, base):
        for h in range(groups):
            lanes = slice(h * GROUP, (h + 1) * GROUP)
            s3[base:base + 64, lanes] = split_rows(v_ref[:, lanes])

    def send_trace(turn, base):
        stacked = jnp.concatenate([s3[base:base + 64, h * GROUP:(h + 1) * GROUP] for h in range(groups)], axis=0)
        for c in range(chunks):
            picked = mm(stacked, hot[c])
            high = trace_ref[:, c * GROUP:(c + 1) * GROUP] >> 8
            total = jnp.zeros((32, GROUP), F32)
            for h in range(groups):
                total += jnp.where(high == h, picked[h * 64:h * 64 + 32] + picked[h * 64 + 32:h * 64 + 64], 0.0)
            own[turn, c] = total
            trace_copy(turn, c).start()

    def strain_energy(v_ref, out_ref):
        for i in range(pairs):
            tile = v_ref[:, i * 128:(i + 1) * 128]
            turned = swap(tile)
            vab[4 * i] = split_rows(jnp.where(left32, tile, 0.0))
            vab[4 * i + 1] = split_rows(jnp.where(left32, 0.0, turned))
            vab[4 * i + 2] = split_rows(jnp.where(left32, turned, 0.0))
            vab[4 * i + 3] = split_rows(jnp.where(left32, 0.0, tile))

        def forward(step, _):
            for u in range(4):
                n = step * 4 + u
                c0, c1, c2, c3 = (cols_smem[n * 4 + k] for k in range(4))
                x = jnp.concatenate(
                    [vab[2 * c0] + vab[2 * c1 + 1], vab[2 * c2] + vab[2 * c3 + 1]], axis=1)
                o = mm(x, kk[n], NT)
                o = o[0:32] + o[32:64]
                ss[n] = split_rows(o + swap(o))
            return 0

        def backward(step, _):
            for u in range(4):
                n = step * 4 + u
                o = mm(ss[n], kk[n])
                o = o[0:32] + o[32:64]
                for half in range(2):
                    tile = o[:, half * 128:(half + 1) * 128]
                    top, bottom = tile[0:16], tile[16:32]
                    tp[n * 4 + 2 * half] = jnp.where(left16, top, swap(bottom))
                    tp[n * 4 + 2 * half + 1] = jnp.where(left16, swap(top), bottom)
            return 0

        def add_up(step, total):
            for u in range(8):
                i = step * 8 + u
                total = total * csr_fs[0, i] + tp[csr_is[0, i]]
                run[i] = total
            return total

        lax.fori_loop(0, rows // 4, forward, 0)
        lax.fori_loop(0, rows // 4, backward, 0)
        lax.fori_loop(0, entries // 8, add_up, jnp.zeros((16, 128), F32))
        for i in range(pairs):
            lanes = slice(i * 128, (i + 1) * 128)
            a = run[csr_is[1, 2 * i]] * csr_fs[1, 2 * i]
            b = run[csr_is[1, 2 * i + 1]] * csr_fs[1, 2 * i + 1]
            tile = jnp.concatenate(
                [jnp.where(left16, a, swap(b)), jnp.where(left16, swap(a), b)], axis=0)
            out_ref[:, lanes] = tile + mass_ref[:, lanes] * v_ref[:, lanes]

    def add_jump(turn, out_ref):
        acc[...] = jnp.zeros(acc.shape, F32)
        for c in range(chunks):
            lanes = slice(c * GROUP, (c + 1) * GROUP)
            trace_copy(turn, c).wait_recv()
            weight = pen_ref[:, lanes] * pen_other[:, lanes]
            jump = split_rows(weight * (own[turn, c] - part[turn, c]))
            acc[...] += mm(masked_groups(jump, trace_ref[:, lanes] >> 8), hot[c], NT)
        for h in range(groups):
            lanes = slice(h * GROUP, (h + 1) * GROUP)
            out_ref[:, lanes] += acc[h * 64:h * 64 + 32] + acc[h * 64 + 32:h * 64 + 64]

    def gram(base):
        def one(c, total):
            lanes = pl.ds(pl.multiple_of(c * GROUP, GROUP), GROUP)
            return total + mm(s3[base:base + 64, lanes], s3[base:base + 128, lanes], NT)
        o = lax.fori_loop(0, groups, one, jnp.zeros((64, 128), F32))
        o = o[0:32] + o[32:64]
        return o + pltpu.roll(o, 96, 1)

    halves_of(r_ref, 0)
    send_trace(0, 0)
    strain_energy(r_ref, q_ref)
    pen_copy.wait_recv()
    add_jump(0, q_ref)
    halves_of(q_ref, 64)
    send_trace(1, 64)
    gram_a = gram(0)
    strain_energy(q_ref, t_ref)
    add_jump(1, t_ref)
    halves_of(t_ref, 128)
    gram_b = gram(64)
    lane4 = iota((32, 128), 1)
    pay[0] = jnp.where(
        lane4 < 32, gram_a, jnp.where(lane4 < 64, pltpu.roll(gram_a, 96, 1),
                                      jnp.where(lane4 < 96, swap(gram_b), pltpu.roll(gram_b, 32, 1))))

    x_size = patches // z_size
    sent = []

    def reduce(stage, slots, count, place, base):
        copies = []
        for j in range(1, count):
            copies.append(pltpu.make_async_remote_copy(
                src_ref=pay.at[stage], dst_ref=slots.at[j - 1], send_sem=red_send.at[base + j],
                recv_sem=red_recv.at[base + j], device_id=place(j), device_id_type=MESH))
            copies[-1].start()
        total = pay[stage]
        for j, copy in enumerate(copies):
            copy.wait_recv()
            total += slots[j]
        sent.extend(copies)
        return total

    pay[1] = reduce(0, rc, comps, lambda j: {"comp": lax.rem(mine + j, comps)}, 0)
    pay[2] = reduce(1, rx, x_size, lambda j: {"patch": lax.rem(me + j * z_size, patches)}, comps)
    z_first = (me // z_size) * z_size
    grams = reduce(
        2, rz, z_size, lambda j: {"patch": z_first + lax.rem(lax.rem(me, z_size) + j, z_size)}, comps + x_size)

    system = jnp.concatenate([pltpu.roll(grams, 96, 1), pltpu.roll(grams, 64, 1)], axis=0)
    place = iota((64, 128), 0)
    for k in range(64):
        pivot_row = system[k:k + 1]
        scaled = pivot_row / pivot_row[:, k:k + 1]
        system = jnp.where(place == k, scaled, system - system[:, k:k + 1] * scaled)
    mixed = jnp.concatenate([system[0:32], system[0:32], system[32:64], system[32:64]], axis=0)
    weights = split_rows(jnp.transpose(mixed)[96:128])

    def outputs(c, _):
        lanes = pl.ds(pl.multiple_of(c * GROUP, GROUP), GROUP)
        o = mm(weights, s3[0:128, lanes])
        sol_ref[:, lanes] = o[0:32] + o[32:64]
        o = mm(weights, s3[64:192, lanes])
        res_ref[:, lanes] = r_ref[:, lanes] - (o[0:32] + o[32:64])
        return 0

    lax.fori_loop(0, groups, outputs, 0)

    def drain(d, _):
        cell_copy(d).wait_send()
        return 0

    lax.fori_loop(1, patches, drain, 0)
    pen_copy.wait_send()
    for turn in range(2):
        for c in range(chunks):
            trace_copy(turn, c).wait_send()
    for copy in sent:
        copy.wait_send()


def shards(z_size, load_cases, mass_diag, stiffness, block_cols, trace_dofs, penalty, cell_partials, cell_owner, cell_dof):
    cases, dofs = load_cases.shape
    rows = stiffness.shape[0]
    traces, ncell = trace_dofs.shape[0], cell_dof.shape[0]
    patches, comps = lax.axis_size("patch"), lax.axis_size("comp")
    groups, chunks = dofs // GROUP, traces // GROUP
    entries = rows * 4
    vm = pl.BlockSpec(memory_space=pltpu.VMEM)
    hbm = pl.BlockSpec(memory_space=pl.ANY)
    sm = pl.BlockSpec(memory_space=pltpu.SMEM)
    field = jax.ShapeDtypeStruct((cases, dofs), F32)
    x_size = patches // z_size
    stages = comps + x_size + z_size
    return pl.pallas_call(
        functools.partial(kernel, z_size),
        out_shape=(field, field),
        in_specs=[hbm, vm, hbm, vm, sm, vm, vm, vm, vm, vm],
        out_specs=(vm, vm),
        scratch_shapes=[
            pltpu.VMEM((cases, dofs), F32),
            pltpu.VMEM(stiffness.shape, F32),
            pltpu.VMEM((rows, 128, 256), BF16),
            pltpu.VMEM((patches, 17, 128), F32),
            pltpu.VMEM((patches, 17, 128), F32),
            pltpu.VMEM((1, GROUP), I32),
            pltpu.VMEM((2, GROUP), I32),
            pltpu.VMEM((2, GROUP), F32),
            pltpu.SMEM((2, GROUP), I32),
            pltpu.SMEM((2, GROUP), F32),
            pltpu.VMEM((chunks, GROUP, GROUP), BF16),
            pltpu.VMEM((2, chunks, cases, GROUP), F32),
            pltpu.VMEM((2, chunks, cases, GROUP), F32),
            pltpu.VMEM((1, traces), F32),
            pltpu.VMEM((cases, dofs), F32),
            pltpu.VMEM((cases, dofs), F32),
            pltpu.VMEM((cases, dofs), F32),
            pltpu.VMEM((6 * cases, dofs), BF16),
            pltpu.VMEM((2 * rows, 64, 128), BF16),
            pltpu.VMEM((rows, 64, 128), BF16),
            pltpu.VMEM((entries, 16, 128), F32),
            pltpu.VMEM((entries, 16, 128), F32),
            pltpu.VMEM((groups * 64, GROUP), F32),
            pltpu.VMEM((3, cases, 128), F32),
            pltpu.VMEM((comps - 1, cases, 128), F32),
            pltpu.VMEM((x_size - 1, cases, 128), F32),
            pltpu.VMEM((z_size - 1, cases, 128), F32),
            pltpu.SemaphoreType.DMA((4,)),
            pltpu.SemaphoreType.DMA((patches,)),
            pltpu.SemaphoreType.DMA((patches,)),
            pltpu.SemaphoreType.DMA((2, chunks)),
            pltpu.SemaphoreType.DMA((2, chunks)),
            pltpu.SemaphoreType.DMA((stages,)),
            pltpu.SemaphoreType.DMA((stages,)),
        ],
        compiler_params=pltpu.CompilerParams(
            collective_id=0, has_side_effects=True, vmem_limit_bytes=60 * 1024 * 1024),
    )(
        load_cases, mass_diag.reshape(1, -1), stiffness, block_cols.reshape(1, -1), block_cols.reshape(-1),
        trace_dofs.reshape(1, -1), penalty.reshape(1, -1), cell_partials, cell_owner.reshape(1, -1),
        cell_dof.reshape(1, -1),
    )


def solution(mesh):
    patches = mesh.shape["patch"]
    z_size = 8 if patches == 32 else patches // 2
    both = ("comp", "patch")
    return jax.shard_map(
        functools.partial(shards, z_size),
        mesh=mesh,
        in_specs=(
            P(None, both), P(both), P(both, None, None), P(both, None), P(both), P(both), P(None, both),
            P(both, None), P(both),
        ),
        out_specs=(P(None, both), P(None, both)),
        check_vma=False,
    )
```

```python
import functools

import jax
import jax.numpy as jnp
from jax import lax
from jax.experimental import pallas as pl
from jax.experimental.pallas import tpu as pltpu
from jax.sharding import PartitionSpec as P

CAP = 64
GROUP = 256
F32, BF16, I32 = jnp.float32, jnp.bfloat16, jnp.int32
NT = (((1,), (1,)), ((), ()))
NN = (((1,), (0,)), ((), ()))
MESH = pl.DeviceIdType.MESH


def mm(a, b, dims=NN):
    return lax.dot_general(a, b, dims, preferred_element_type=F32)


def split(x):
    hi = x.astype(BF16)
    return hi, (x - hi.astype(F32)).astype(BF16)


def split_rows(x):
    return jnp.concatenate(split(x), axis=0)


def iota(shape, dim):
    return lax.broadcasted_iota(I32, shape, dim)


def ones_where(mask):
    return jnp.where(mask, 1.0, 0.0)


def swap(x):
    return pltpu.roll(x, 64, 1)


def pack4(x, slot):
    band = iota((8, 128), 1) >> 5
    out = jnp.zeros((8, 128), F32)
    for g in range(4):
        out = jnp.where(band == g, pltpu.roll(x[8 * g:8 * g + 8], (32 * (g - slot)) % 128, 1), out)
    return out


def unpack4(x, slot):
    band = iota((8, 128), 1) >> 5
    return jnp.concatenate(
        [jnp.where(band == slot, pltpu.roll(x, (32 * (slot - g)) % 128, 1), 0.0) for g in range(4)], axis=0)


def eliminate(system, first, last):
    place = iota((64, 128), 0)
    for k in range(first, last, 2):
        row_a, row_b = system[k:k + 1], system[k + 1:k + 2]
        col_a, col_b = system[:, k:k + 1], system[:, k + 1:k + 2]
        aa, ab = row_a[:, k:k + 1], row_a[:, k + 1:k + 2]
        ba, bb = row_b[:, k:k + 1], row_b[:, k + 1:k + 2]
        inverse = 1.0 / (aa * bb - ab * ba)
        new_a = (bb * row_a - ab * row_b) * inverse
        new_b = (aa * row_b - ba * row_a) * inverse
        system = jnp.where(
            place == k, new_a, jnp.where(place == k + 1, new_b, system - col_a * new_a - col_b * new_b))
    return system


def kernel(
    z_size, load_hbm, mass_hbm, stiff_hbm, cols_hbm, trace_hbm, pen_hbm, cells_hbm, owner_hbm,
    cdof_hbm, sol_ref, res_ref,
    load, mass_ref, stiff, cols_ref, cols_smem, trace_ref, pen_ref, cells_ref, owner_ref, cdof_ref,
    kk, send, recv, colp, csr_i, csr_f, csr_is, csr_fs, hot, own, part, pen_other,
    r_ref, q_ref, t_ref, s3, vab, ss, tp, run, acc, fold, pay_a, rc_a, rx_a, rz_a, pay_b, rc_b, rx_b, rz_b,
    in_sem, a2a_send, a2a_recv, tr_send, tr_recv, red_send, red_recv,
):
    patches, comps = lax.axis_size("patch"), lax.axis_size("comp")
    me, mine = lax.axis_index("patch"), lax.axis_index("comp")
    cases, dofs = load.shape
    groups = dofs // GROUP
    ncell = cells_ref.shape[1]
    traces = trace_ref.shape[1]
    chunks = traces // GROUP
    rows = stiff.shape[0]
    entries = rows * 4
    spare = 64 - rows
    pairs = rows // 2
    left = iota((1, 128), 1) < 64
    left16 = iota((16, 128), 1) < 64
    left32 = iota((32, 128), 1) < 64

    get_stiff = pltpu.make_async_copy(stiff_hbm, stiff, in_sem.at[0])
    get_load = pltpu.make_async_copy(load_hbm, load, in_sem.at[1])
    small = [
        pltpu.make_async_copy(src, dst, in_sem.at[4 + i]) for i, (src, dst) in enumerate((
            (owner_hbm, owner_ref), (cdof_hbm, cdof_ref), (cells_hbm, cells_ref), (cols_hbm, cols_ref),
            (cols_hbm, cols_smem), (trace_hbm, trace_ref), (pen_hbm, pen_ref), (mass_hbm, mass_ref)))
    ]

    barrier = pltpu.get_barrier_semaphore()

    def greet_patch(d, _):
        pl.semaphore_signal(barrier, inc=1, device_id={"patch": lax.rem(me + d, patches)}, device_id_type=MESH)
        return 0

    def greet_comp(d, _):
        pl.semaphore_signal(barrier, inc=1, device_id={"comp": lax.rem(mine + d, comps)}, device_id_type=MESH)
        return 0

    lax.fori_loop(1, patches, greet_patch, 0)
    lax.fori_loop(1, comps, greet_comp, 0)

    for copy in small:
        copy.start()
    get_stiff.start()
    get_load.start()
    for copy in small:
        copy.wait()

    owner = owner_ref[...]
    hit = owner == iota((patches, ncell), 0)
    tri = ones_where(iota((ncell, ncell), 0) < iota((ncell, ncell), 1)).astype(BF16)
    before = mm(ones_where(hit).astype(BF16), tri)
    pos = jnp.sum(jnp.where(hit, before, 0.0), axis=0, keepdims=True).astype(I32)
    slot = (owner & 3) * CAP + pos
    slot_hot = ones_where(iota((GROUP, ncell), 0) == slot).astype(BF16)
    cdof = cdof_ref[...]
    row16 = iota((16, ncell), 0)
    dof_rows = jnp.where(row16 == 0, cdof >> 8, jnp.where(row16 == 1, cdof & 255, 0)).astype(F32)
    cell_hi, cell_lo = split(cells_ref[...])
    cell_rows = jnp.concatenate([cell_hi, cell_lo, dof_rows.astype(BF16)], axis=0)
    for g in range(patches // 4):
        mask = jnp.broadcast_to(ones_where((owner >> 2) == g), (16, ncell)).astype(BF16)
        mask = jnp.concatenate([mask] * 5, axis=0)
        packed = mm(cell_rows * mask, slot_hot, NT)
        values = packed[0:32] + packed[32:64]
        places = packed[64:72]
        for half in range(2):
            tile = values[:, half * 128:(half + 1) * 128]
            top, bottom = tile[0:16], tile[16:32]
            place = places[:, half * 128:(half + 1) * 128]
            place_hi, place_lo = place[0:1], place[1:2]
            even = g * 4 + half * 2
            send[even, 0:16] = jnp.where(left16, top, swap(bottom))
            send[even + 1, 0:16] = jnp.where(left16, swap(top), bottom)
            send[even, 16:17] = jnp.where(left, place_hi, swap(place_lo))
            send[even + 1, 16:17] = jnp.where(left, swap(place_hi), place_lo)
    recv[0] = send[me]

    pl.semaphore_wait(barrier, patches + comps - 2)

    other = lax.rem(me + patches // 2, patches)

    def cell_copy(d):
        to = lax.rem(me + d, patches)
        return pltpu.make_async_remote_copy(
            src_ref=send.at[to], dst_ref=recv.at[d], send_sem=a2a_send.at[d], recv_sem=a2a_recv.at[d],
            device_id={"patch": to}, device_id_type=MESH,
        )

    def start_cell(d, _):
        cell_copy(d).start()
        return 0

    pen_copy = pltpu.make_async_remote_copy(
        src_ref=pen_ref, dst_ref=pen_other, send_sem=a2a_send.at[0], recv_sem=a2a_recv.at[0],
        device_id={"patch": other}, device_id_type=MESH,
    )
    x_size = patches // z_size
    for x in [x_size // 2] + list(range(1, x_size // 2)) + list(range(x_size // 2 + 1, x_size)) + [0]:
        lax.fori_loop(max(1, x * z_size), (x + 1) * z_size, start_cell, 0)
    pen_copy.start()

    i0, i1 = iota((GROUP, GROUP), 0), iota((GROUP, GROUP), 1)
    colp[...] = jnp.full((4, 128), 255, I32)
    colp[:, 0:rows] = cols_ref[...]
    quad = colp[...]
    turned = pltpu.roll(quad, 64, 1)
    col = jnp.concatenate(
        [jnp.where(left, quad[0:1], turned[1:2]), jnp.where(left, quad[2:3], turned[3:4])], axis=1)
    col_of = jnp.transpose(jnp.broadcast_to(col, (GROUP, GROUP)))
    ahead = (col_of < col) | ((col_of == col) & (i0 < i1))
    rank = jnp.sum(jnp.where(ahead, 1, 0), axis=0, keepdims=True)
    at_rank = jnp.transpose(jnp.broadcast_to(rank, (GROUP, GROUP))) == i1
    order = jnp.sum(jnp.where(at_rank, i0, 0), axis=0, keepdims=True)
    ocol = jnp.sum(jnp.where(at_rank, col_of, 0), axis=0, keepdims=True)
    upto = jnp.sum(jnp.where(col_of <= i1, 1, 0), axis=0, keepdims=True)
    same = jnp.sum(jnp.where(col_of == i1, 1, 0), axis=0, keepdims=True)
    lane = iota((1, GROUP), 1)
    csr_i[0:1, :] = jnp.minimum((order & 63) * 4 + (order >> 6), entries - 1)
    csr_i[1:2, :] = jnp.clip(upto - 1, 0, entries - 1)
    csr_f[0:1, :] = ones_where((ocol == pltpu.roll(ocol, 1, 1)) & (lane > 0))
    csr_f[1:2, :] = ones_where(same > 0)
    put_i = pltpu.make_async_copy(csr_i, csr_is, in_sem.at[2])
    put_f = pltpu.make_async_copy(csr_f, csr_fs, in_sem.at[3])
    put_i.start()
    put_f.start()

    for c in range(chunks):
        t_lo = trace_ref[:, c * GROUP:(c + 1) * GROUP] & 255
        hot[c] = ones_where(i0 == t_lo).astype(BF16)

    get_stiff.wait()

    def halve(n, _):
        hi, lo = split(stiff[n])
        kk[n, 0:64] = hi
        kk[n, 64:128] = lo
        return 0

    lax.fori_loop(0, rows, halve, 0)
    put_i.wait()
    put_f.wait()
    get_load.wait()

    def masked_groups(data, high):
        parts = []
        for h in range(groups):
            mask = jnp.broadcast_to(ones_where(high == h), (16, GROUP)).astype(BF16)
            parts.append(data * jnp.concatenate([mask] * 4, axis=0))
        return jnp.concatenate(parts, axis=0)

    acc[...] = jnp.zeros(acc.shape, F32)

    def place_cells(k, _):
        data, highs, lows = [], [], []
        k = (k // 4) * 4 + (k % 4 + 2 * (k // 4)) % 4
        for i in range(2):
            tiles = []
            for j in range(2):
                d = k * 4 + i * 2 + j

                @pl.when(d > 0)
                def _():
                    cell_copy(d).wait_recv()

                tiles.append(recv[d])
            a, b = tiles
            at, bt, ap, bp = a[0:16], b[0:16], a[16:17], b[16:17]
            data.append(jnp.concatenate(
                [jnp.where(left16, at, swap(bt)), jnp.where(left16, swap(at), bt)], axis=0))
            highs.append(jnp.where(left, ap, swap(bp)))
            lows.append(jnp.where(left, swap(ap), bp))
        data = split_rows(jnp.concatenate(data, axis=1))
        high = jnp.concatenate(highs, axis=1).astype(I32)
        low = jnp.concatenate(lows, axis=1).astype(I32)
        low_hot = ones_where(i0 == low).astype(BF16)
        acc[...] += mm(masked_groups(data, high), low_hot, NT)
        return 0

    lax.fori_loop(0, patches // 4, place_cells, 0)
    for h in range(groups):
        lanes = slice(h * GROUP, (h + 1) * GROUP)
        r_ref[:, lanes] = load[:, lanes] + acc[h * 64:h * 64 + 32] + acc[h * 64 + 32:h * 64 + 64]

    def trace_copy(turn, c):
        return pltpu.make_async_remote_copy(
            src_ref=own.at[turn, c], dst_ref=part.at[turn, c], send_sem=tr_send.at[turn, c],
            recv_sem=tr_recv.at[turn, c], device_id={"patch": other}, device_id_type=MESH,
        )

    def halves_of(v_ref, base):
        for h in range(groups):
            lanes = slice(h * GROUP, (h + 1) * GROUP)
            s3[base:base + 64, lanes] = split_rows(v_ref[:, lanes])

    def send_trace(turn, base):
        stacked = jnp.concatenate([s3[base:base + 64, h * GROUP:(h + 1) * GROUP] for h in range(groups)], axis=0)
        for c in range(chunks):
            picked = mm(stacked, hot[c])
            high = trace_ref[:, c * GROUP:(c + 1) * GROUP] >> 8
            total = jnp.zeros((32, GROUP), F32)
            for h in range(groups):
                total += jnp.where(high == h, picked[h * 64:h * 64 + 32] + picked[h * 64 + 32:h * 64 + 64], 0.0)
            own[turn, c] = total
            trace_copy(turn, c).start()

    def strains(v_ref):
        for i in range(pairs):
            tile = v_ref[:, i * 128:(i + 1) * 128]
            turned = swap(tile)
            vab[4 * i] = split_rows(jnp.where(left32, tile, 0.0))
            vab[4 * i + 1] = split_rows(jnp.where(left32, 0.0, turned))
            vab[4 * i + 2] = split_rows(jnp.where(left32, turned, 0.0))
            vab[4 * i + 3] = split_rows(jnp.where(left32, 0.0, tile))

        def forward(step, _):
            for u in range(4):
                n = step * 4 + u
                c0, c1, c2, c3 = (cols_smem[k, n] for k in range(4))
                x = jnp.concatenate(
                    [vab[2 * c0] + vab[2 * c1 + 1], vab[2 * c2] + vab[2 * c3 + 1]], axis=1)
                o = mm(x, kk[n], NT)
                o = o[0:32] + o[32:64]
                ss[n] = split_rows(o + swap(o))
            return 0

        lax.fori_loop(0, rows // 4, forward, 0)

    def forces():
        def backward(step, _):
            for u in range(4):
                n = step * 4 + u
                o = mm(ss[n], kk[n])
                o = o[0:32] + o[32:64]
                for half in range(2):
                    tile = o[:, half * 128:(half + 1) * 128]
                    top, bottom = tile[0:16], tile[16:32]
                    tp[n * 4 + 2 * half] = jnp.where(left16, top, swap(bottom))
                    tp[n * 4 + 2 * half + 1] = jnp.where(left16, swap(top), bottom)
            return 0

        lax.fori_loop(0, rows // 4, backward, 0)

    def gather_forces(v_ref, out_ref):
        def add_up(step, total):
            for u in range(8):
                i = step * 8 + u
                total = total * csr_fs[0, i] + tp[csr_is[0, i]]
                run[i] = total
            return total

        lax.fori_loop(0, entries // 8, add_up, jnp.zeros((16, 128), F32))
        for i in range(pairs):
            lanes = slice(i * 128, (i + 1) * 128)
            a = run[csr_is[1, 2 * i]] * csr_fs[1, 2 * i]
            b = run[csr_is[1, 2 * i + 1]] * csr_fs[1, 2 * i + 1]
            tile = jnp.concatenate(
                [jnp.where(left16, a, swap(b)), jnp.where(left16, swap(a), b)], axis=0)
            out_ref[:, lanes] = tile + mass_ref[:, lanes] * v_ref[:, lanes]

    def take_jumps(turn):
        for c in range(chunks):
            trace_copy(turn, c).wait_recv()
            part[turn, c] = own[turn, c] - part[turn, c]

    def weight_of(c):
        lanes = slice(c * GROUP, (c + 1) * GROUP)
        return pen_ref[:, lanes] * pen_other[:, lanes]

    def add_jump(turn, out_ref):
        total = jnp.zeros((groups * 64, GROUP), F32)
        for c in range(chunks):
            lanes = slice(c * GROUP, (c + 1) * GROUP)
            jump = split_rows(weight_of(c) * part[turn, c])
            total += mm(masked_groups(jump, trace_ref[:, lanes] >> 8), hot[c], NT)
        for h in range(groups):
            lanes = slice(h * GROUP, (h + 1) * GROUP)
            out_ref[:, lanes] += total[h * 64:h * 64 + 32] + total[h * 64 + 32:h * 64 + 64]

    sent = []

    def stage(pay, index, slots, count, place, base):
        copies = []
        for j in range(1, count):
            copies.append(pltpu.make_async_remote_copy(
                src_ref=pay.at[index], dst_ref=slots.at[j - 1], send_sem=red_send.at[base + j],
                recv_sem=red_recv.at[base + j], device_id=place(j), device_id_type=MESH))
            copies[-1].start()
        sent.extend(copies)

        def finish():
            total = pay[index]
            for j, copy in enumerate(copies):
                copy.wait_recv()
                total += slots[j]
            return total

        return finish

    z_first = (me // z_size) * z_size
    span = comps + x_size + z_size

    def along_comp(j):
        return {"comp": lax.rem(mine + j, comps)}

    def along_x(j):
        return {"patch": lax.rem(me + j * z_size, patches)}

    def along_z(j):
        return {"patch": z_first + lax.rem(lax.rem(me, z_size) + j, z_size)}

    halves_of(r_ref, 0)
    send_trace(0, 0)
    strains(r_ref)
    forces()
    gather_forces(r_ref, q_ref)
    pen_copy.wait_recv()
    take_jumps(0)
    add_jump(0, q_ref)
    halves_of(q_ref, 64)
    send_trace(1, 64)

    def gram_part(c, total):
        lanes = pl.ds(pl.multiple_of(c * GROUP, GROUP), GROUP)
        both = s3[0:128, lanes]
        return total + mm(both, both, NT)

    o = lax.fori_loop(0, groups, gram_part, jnp.zeros((128, 128), F32))
    first, second = o[0:32] + o[32:64], o[64:96] + o[96:128]
    first, second = first + pltpu.roll(first, 96, 1), second + pltpu.roll(second, 96, 1)
    pay_a[0] = jnp.concatenate([pack4(first, 0), pack4(first, 2), pack4(second, 2)], axis=0)
    a_comp = stage(pay_a, 0, rc_a, comps, along_comp, 0)
    strains(q_ref)

    def strain_part(n, total):
        both = jnp.concatenate([ss[2 * n], ss[2 * n + 1]], axis=1)
        return total + mm(both, both, NT)

    def mass_part(c, total):
        lanes = pl.ds(pl.multiple_of(c * GROUP, GROUP), GROUP)
        return total + mm(split_rows(mass_ref[:, lanes] * q_ref[:, lanes]), s3[64:128, lanes], NT)

    energy = lax.fori_loop(0, rows // 2, strain_part, jnp.zeros((64, 64), F32)) * 0.5
    energy = lax.fori_loop(0, groups, mass_part, energy)
    pay_a[1] = a_comp()
    a_x = stage(pay_a, 1, rx_a, x_size, along_x, comps)
    take_jumps(1)
    for c in range(chunks):
        jump = part[1, c]
        energy += mm(split_rows(0.5 * weight_of(c) * jump), split_rows(jump), NT)
    fold[...] = jnp.zeros((32, 128), F32)
    fold[:, 0:64] = energy[0:32] + energy[32:64]
    third = fold[...]
    third = third + pltpu.roll(third, 96, 1)
    pay_b[0] = pack4(third, 0)
    b_comp = stage(pay_b, 0, rc_b, comps, along_comp, span)

    forces()
    pay_a[2] = a_x()
    a_z = stage(pay_a, 2, rz_a, z_size, along_z, comps + x_size)
    pay_b[1] = b_comp()
    b_x = stage(pay_b, 1, rx_b, x_size, along_x, span + comps)
    gather_forces(q_ref, t_ref)
    add_jump(1, t_ref)
    pay_b[2] = b_x()
    b_z = stage(pay_b, 2, rz_b, z_size, along_z, span + comps + x_size)
    halves_of(t_ref, 128)

    total = a_z()
    m0, m1, m2 = total[0:8], total[8:16], total[16:24]
    upper = unpack4(m1, 0) + unpack4(m2, 1) + unpack4(m0, 2)
    lower = unpack4(m2, 0) + unpack4(m1, 2)
    system = eliminate(jnp.concatenate([upper, lower], axis=0), 0, 32)
    lower = system[32:64] + unpack4(b_z(), 1)
    system = eliminate(jnp.concatenate([system[0:32], lower], axis=0), 32, 64)
    mixed = jnp.concatenate([system[0:32], system[0:32], system[32:64], system[32:64]], axis=0)
    weights = split_rows(jnp.transpose(mixed)[64:96])

    def outputs(c, _):
        lanes = pl.ds(pl.multiple_of(c * GROUP, GROUP), GROUP)
        o = mm(weights, s3[0:128, lanes])
        sol_ref[:, lanes] = o[0:32] + o[32:64]
        o = mm(weights, s3[64:192, lanes])
        res_ref[:, lanes] = r_ref[:, lanes] - (o[0:32] + o[32:64])
        return 0

    lax.fori_loop(0, groups, outputs, 0)

    def drain(d, _):
        cell_copy(d).wait_send()
        return 0

    lax.fori_loop(1, patches, drain, 0)
    pen_copy.wait_send()
    for turn in range(2):
        for c in range(chunks):
            trace_copy(turn, c).wait_send()
    for copy in sent:
        copy.wait_send()


def shards(z_size, load_cases, mass_diag, stiffness, block_cols, trace_dofs, penalty, cell_partials, cell_owner, cell_dof):
    cases, dofs = load_cases.shape
    rows = stiffness.shape[0]
    traces, ncell = trace_dofs.shape[0], cell_dof.shape[0]
    patches, comps = lax.axis_size("patch"), lax.axis_size("comp")
    groups, chunks = dofs // GROUP, traces // GROUP
    entries = rows * 4
    vm = pl.BlockSpec(memory_space=pltpu.VMEM)
    hbm = pl.BlockSpec(memory_space=pltpu.HBM)
    field = jax.ShapeDtypeStruct((cases, dofs), F32)
    x_size = patches // z_size
    stages = comps + x_size + z_size

    def sums(tall):
        return [
            pltpu.VMEM((3, tall, 128), F32),
            pltpu.VMEM((comps - 1, tall, 128), F32),
            pltpu.VMEM((x_size - 1, tall, 128), F32),
            pltpu.VMEM((z_size - 1, tall, 128), F32),
        ]

    return pl.pallas_call(
        functools.partial(kernel, z_size),
        out_shape=(field, field),
        in_specs=[hbm] * 9,
        out_specs=(vm, vm),
        scratch_shapes=[
            pltpu.VMEM((cases, dofs), F32),
            pltpu.VMEM((1, dofs), F32),
            pltpu.VMEM(stiffness.shape, F32),
            pltpu.VMEM((4, rows), I32),
            pltpu.SMEM((4, rows), I32),
            pltpu.VMEM((1, traces), I32),
            pltpu.VMEM((1, traces), F32),
            pltpu.VMEM((cases, ncell), F32),
            pltpu.VMEM((1, ncell), I32),
            pltpu.VMEM((1, ncell), I32),
            pltpu.VMEM((rows, 128, 256), BF16),
            pltpu.VMEM((patches, 17, 128), F32),
            pltpu.VMEM((patches, 17, 128), F32),
            pltpu.VMEM((4, 128), I32),
            pltpu.VMEM((2, GROUP), I32),
            pltpu.VMEM((2, GROUP), F32),
            pltpu.SMEM((2, GROUP), I32),
            pltpu.SMEM((2, GROUP), F32),
            pltpu.VMEM((chunks, GROUP, GROUP), BF16),
            pltpu.VMEM((2, chunks, cases, GROUP), F32),
            pltpu.VMEM((2, chunks, cases, GROUP), F32),
            pltpu.VMEM((1, traces), F32),
            pltpu.VMEM((cases, dofs), F32),
            pltpu.VMEM((cases, dofs), F32),
            pltpu.VMEM((cases, dofs), F32),
            pltpu.VMEM((6 * cases, dofs), BF16),
            pltpu.VMEM((2 * rows, 64, 128), BF16),
            pltpu.VMEM((rows, 64, 128), BF16),
            pltpu.VMEM((entries, 16, 128), F32),
            pltpu.VMEM((entries, 16, 128), F32),
            pltpu.VMEM((groups * 64, GROUP), F32),
            pltpu.VMEM((cases, 128), F32),
            *sums(24),
            *sums(8),
            pltpu.SemaphoreType.DMA((12,)),
            pltpu.SemaphoreType.DMA((patches,)),
            pltpu.SemaphoreType.DMA((patches,)),
            pltpu.SemaphoreType.DMA((2, chunks)),
            pltpu.SemaphoreType.DMA((2, chunks)),
            pltpu.SemaphoreType.DMA((2 * stages,)),
            pltpu.SemaphoreType.DMA((2 * stages,)),
        ],
        compiler_params=pltpu.CompilerParams(
            collective_id=0, has_side_effects=True, vmem_limit_bytes=40 * 1024 * 1024),
    )(
        *(pltpu.with_memory_space_constraint(x, pltpu.HBM) for x in (
            load_cases, mass_diag.reshape(1, -1), stiffness, block_cols.T, trace_dofs.reshape(1, -1),
            penalty.reshape(1, -1), cell_partials, cell_owner.reshape(1, -1), cell_dof.reshape(1, -1)))
    )


def solution(mesh):
    patches = mesh.shape["patch"]
    z_size = 8 if patches == 32 else patches // 2
    both = ("comp", "patch")
    return jax.shard_map(
        functools.partial(shards, z_size),
        mesh=mesh,
        in_specs=(
            P(None, both), P(both), P(both, None, None), P(both, None), P(both), P(both), P(None, both),
            P(both, None), P(both),
        ),
        out_specs=(P(None, both), P(None, both)),
        check_vma=False,
    )
```

```python
import functools

import jax
import jax.numpy as jnp
from jax import lax
from jax.experimental import pallas as pl
from jax.experimental.pallas import tpu as pltpu
from jax.sharding import PartitionSpec as P

CAP = 64
GROUP = 256
F32, BF16, I32 = jnp.float32, jnp.bfloat16, jnp.int32
NT = (((1,), (1,)), ((), ()))
NN = (((1,), (0,)), ((), ()))
MESH = pl.DeviceIdType.MESH


def mm(a, b, dims=NN):
    return lax.dot_general(a, b, dims, preferred_element_type=F32)


def split(x):
    hi = x.astype(BF16)
    return hi, (x - hi.astype(F32)).astype(BF16)


def split_rows(x):
    return jnp.concatenate(split(x), axis=0)


def iota(shape, dim):
    return lax.broadcasted_iota(I32, shape, dim)


def ones_where(mask):
    return jnp.where(mask, 1.0, 0.0)


def swap(x):
    return pltpu.roll(x, 64, 1)


def pack4(x, slot):
    band = iota((8, 128), 1) >> 5
    out = jnp.zeros((8, 128), F32)
    for g in range(4):
        out = jnp.where(band == g, pltpu.roll(x[8 * g:8 * g + 8], (32 * (g - slot)) % 128, 1), out)
    return out


def unpack4(x, slot):
    band = iota((8, 128), 1) >> 5
    return jnp.concatenate(
        [jnp.where(band == slot, pltpu.roll(x, (32 * (slot - g)) % 128, 1), 0.0) for g in range(4)], axis=0)


def eliminate(system, first, last):
    place = iota((64, 128), 0)
    for start in range(first, last, 8):
        wide = [jnp.broadcast_to(system[:, start + j:start + j + 1], (64, 128)) for j in range(8)]
        for j in range(8):
            k = start + j
            here = place == k
            inverse = 1.0 / wide[j][k:k + 1]
            factor = wide[j] * inverse
            row = system[k:k + 1]
            system = jnp.where(here, row * inverse, system - factor * row)
            for i in range(j + 1, 8):
                entry = wide[i][k:k + 1]
                wide[i] = jnp.where(here, entry * inverse, wide[i] - factor * entry)
    return system


def kernel(
    z_size, load_hbm, mass_hbm, stiff_hbm, cols_hbm, trace_hbm, pen_hbm, cells_hbm, owner_hbm,
    cdof_hbm, sol_ref, res_ref,
    load, mass_ref, stiff, cols_ref, cols_smem, trace_ref, pen_ref, cells_ref, owner_ref, cdof_ref,
    kk, send, recv, colp, csr_i, csr_f, csr_is, csr_fs, hot, own, part, pen_other,
    r_ref, q_ref, t_ref, s3, vab, ss, tp, run, acc, fold, pay_a, rc_a, rx_a, rz_a, pay_b, rc_b, rx_b, rz_b,
    in_sem, a2a_send, a2a_recv, tr_send, tr_recv, red_send, red_recv,
):
    patches, comps = lax.axis_size("patch"), lax.axis_size("comp")
    me, mine = lax.axis_index("patch"), lax.axis_index("comp")
    cases, dofs = load.shape
    groups = dofs // GROUP
    ncell = cells_ref.shape[1]
    traces = trace_ref.shape[1]
    chunks = traces // GROUP
    rows = stiff.shape[0]
    entries = rows * 4
    spare = 64 - rows
    pairs = rows // 2
    left = iota((1, 128), 1) < 64
    left16 = iota((16, 128), 1) < 64
    left32 = iota((32, 128), 1) < 64

    get_stiff = pltpu.make_async_copy(stiff_hbm, stiff, in_sem.at[0])
    get_load = pltpu.make_async_copy(load_hbm, load, in_sem.at[1])
    small = [
        pltpu.make_async_copy(src, dst, in_sem.at[4 + i]) for i, (src, dst) in enumerate((
            (owner_hbm, owner_ref), (cdof_hbm, cdof_ref), (cells_hbm, cells_ref), (cols_hbm, cols_ref),
            (cols_hbm, cols_smem), (trace_hbm, trace_ref), (pen_hbm, pen_ref), (mass_hbm, mass_ref)))
    ]

    barrier = pltpu.get_barrier_semaphore()

    def greet_patch(d, _):
        pl.semaphore_signal(barrier, inc=1, device_id={"patch": lax.rem(me + d, patches)}, device_id_type=MESH)
        return 0

    def greet_comp(d, _):
        pl.semaphore_signal(barrier, inc=1, device_id={"comp": lax.rem(mine + d, comps)}, device_id_type=MESH)
        return 0

    lax.fori_loop(1, patches, greet_patch, 0)
    lax.fori_loop(1, comps, greet_comp, 0)

    for copy in small:
        copy.start()
    get_stiff.start()
    get_load.start()
    for copy in small:
        copy.wait()

    owner = owner_ref[...]
    hit = owner == iota((patches, ncell), 0)
    tri = ones_where(iota((ncell, ncell), 0) < iota((ncell, ncell), 1)).astype(BF16)
    before = mm(ones_where(hit).astype(BF16), tri)
    pos = jnp.sum(jnp.where(hit, before, 0.0), axis=0, keepdims=True).astype(I32)
    slot = (owner & 3) * CAP + pos
    slot_hot = ones_where(iota((GROUP, ncell), 0) == slot).astype(BF16)
    cdof = cdof_ref[...]
    row16 = iota((16, ncell), 0)
    dof_rows = jnp.where(row16 == 0, cdof >> 8, jnp.where(row16 == 1, cdof & 255, 0)).astype(F32)
    cell_hi, cell_lo = split(cells_ref[...])
    cell_rows = jnp.concatenate([cell_hi, cell_lo, dof_rows.astype(BF16)], axis=0)
    for g in range(patches // 4):
        mask = jnp.broadcast_to(ones_where((owner >> 2) == g), (16, ncell)).astype(BF16)
        mask = jnp.concatenate([mask] * 5, axis=0)
        packed = mm(cell_rows * mask, slot_hot, NT)
        values = packed[0:32] + packed[32:64]
        places = packed[64:72]
        for half in range(2):
            tile = values[:, half * 128:(half + 1) * 128]
            top, bottom = tile[0:16], tile[16:32]
            place = places[:, half * 128:(half + 1) * 128]
            place_hi, place_lo = place[0:1], place[1:2]
            even = g * 4 + half * 2
            send[even, 0:16] = jnp.where(left16, top, swap(bottom))
            send[even + 1, 0:16] = jnp.where(left16, swap(top), bottom)
            send[even, 16:17] = jnp.where(left, place_hi, swap(place_lo))
            send[even + 1, 16:17] = jnp.where(left, swap(place_hi), place_lo)
    recv[0] = send[me]

    pl.semaphore_wait(barrier, patches + comps - 2)

    other = lax.rem(me + patches // 2, patches)

    def cell_copy(d):
        to = lax.rem(me + d, patches)
        return pltpu.make_async_remote_copy(
            src_ref=send.at[to], dst_ref=recv.at[d], send_sem=a2a_send.at[d], recv_sem=a2a_recv.at[d],
            device_id={"patch": to}, device_id_type=MESH,
        )

    def start_cell(d, _):
        cell_copy(d).start()
        return 0

    pen_copy = pltpu.make_async_remote_copy(
        src_ref=pen_ref, dst_ref=pen_other, send_sem=a2a_send.at[0], recv_sem=a2a_recv.at[0],
        device_id={"patch": other}, device_id_type=MESH,
    )
    x_size = patches // z_size
    for x in [x_size // 2] + list(range(1, x_size // 2)) + list(range(x_size // 2 + 1, x_size)) + [0]:
        lax.fori_loop(max(1, x * z_size), (x + 1) * z_size, start_cell, 0)
    pen_copy.start()

    i0, i1 = iota((GROUP, GROUP), 0), iota((GROUP, GROUP), 1)
    colp[...] = jnp.full((4, 128), 255, I32)
    colp[:, 0:rows] = cols_ref[...]
    quad = colp[...]
    turned = pltpu.roll(quad, 64, 1)
    col = jnp.concatenate(
        [jnp.where(left, quad[0:1], turned[1:2]), jnp.where(left, quad[2:3], turned[3:4])], axis=1)
    col_of = jnp.transpose(jnp.broadcast_to(col, (GROUP, GROUP)))
    ahead = (col_of < col) | ((col_of == col) & (i0 < i1))
    rank = jnp.sum(jnp.where(ahead, 1, 0), axis=0, keepdims=True)
    at_rank = jnp.transpose(jnp.broadcast_to(rank, (GROUP, GROUP))) == i1
    order = jnp.sum(jnp.where(at_rank, i0, 0), axis=0, keepdims=True)
    ocol = jnp.sum(jnp.where(at_rank, col_of, 0), axis=0, keepdims=True)
    upto = jnp.sum(jnp.where(col_of <= i1, 1, 0), axis=0, keepdims=True)
    same = jnp.sum(jnp.where(col_of == i1, 1, 0), axis=0, keepdims=True)
    lane = iota((1, GROUP), 1)
    csr_i[0:1, :] = jnp.minimum((order & 63) * 4 + (order >> 6), entries - 1)
    csr_i[1:2, :] = jnp.clip(upto - 1, 0, entries - 1)
    csr_f[0:1, :] = ones_where((ocol == pltpu.roll(ocol, 1, 1)) & (lane > 0))
    csr_f[1:2, :] = ones_where(same > 0)
    put_i = pltpu.make_async_copy(csr_i, csr_is, in_sem.at[2])
    put_f = pltpu.make_async_copy(csr_f, csr_fs, in_sem.at[3])
    put_i.start()
    put_f.start()

    for c in range(chunks):
        t_lo = trace_ref[:, c * GROUP:(c + 1) * GROUP] & 255
        hot[c] = ones_where(i0 == t_lo).astype(BF16)

    get_stiff.wait()

    def halve(n, _):
        hi, lo = split(stiff[n])
        kk[n, 0:64] = hi
        kk[n, 64:128] = lo
        return 0

    lax.fori_loop(0, rows, halve, 0)
    put_i.wait()
    put_f.wait()
    get_load.wait()

    def masked_groups(data, high):
        parts = []
        for h in range(groups):
            mask = jnp.broadcast_to(ones_where(high == h), (16, GROUP)).astype(BF16)
            parts.append(data * jnp.concatenate([mask] * 4, axis=0))
        return jnp.concatenate(parts, axis=0)

    acc[...] = jnp.zeros(acc.shape, F32)

    def place_cells(k, _):
        data, highs, lows = [], [], []
        k = (k // 4) * 4 + (k % 4 + 2 * (k // 4)) % 4
        for i in range(2):
            tiles = []
            for j in range(2):
                d = k * 4 + i * 2 + j

                @pl.when(d > 0)
                def _():
                    cell_copy(d).wait_recv()

                tiles.append(recv[d])
            a, b = tiles
            at, bt, ap, bp = a[0:16], b[0:16], a[16:17], b[16:17]
            data.append(jnp.concatenate(
                [jnp.where(left16, at, swap(bt)), jnp.where(left16, swap(at), bt)], axis=0))
            highs.append(jnp.where(left, ap, swap(bp)))
            lows.append(jnp.where(left, swap(ap), bp))
        data = split_rows(jnp.concatenate(data, axis=1))
        high = jnp.concatenate(highs, axis=1).astype(I32)
        low = jnp.concatenate(lows, axis=1).astype(I32)
        low_hot = ones_where(i0 == low).astype(BF16)
        acc[...] += mm(masked_groups(data, high), low_hot, NT)
        return 0

    lax.fori_loop(0, patches // 4, place_cells, 0)
    for h in range(groups):
        lanes = slice(h * GROUP, (h + 1) * GROUP)
        r_ref[:, lanes] = load[:, lanes] + acc[h * 64:h * 64 + 32] + acc[h * 64 + 32:h * 64 + 64]

    def trace_copy(turn, c):
        return pltpu.make_async_remote_copy(
            src_ref=own.at[turn, c], dst_ref=part.at[turn, c], send_sem=tr_send.at[turn, c],
            recv_sem=tr_recv.at[turn, c], device_id={"patch": other}, device_id_type=MESH,
        )

    def halves_of(v_ref, base):
        for h in range(groups):
            lanes = slice(h * GROUP, (h + 1) * GROUP)
            s3[base:base + 64, lanes] = split_rows(v_ref[:, lanes])

    def send_trace(turn, base):
        stacked = jnp.concatenate([s3[base:base + 64, h * GROUP:(h + 1) * GROUP] for h in range(groups)], axis=0)
        for c in range(chunks):
            picked = mm(stacked, hot[c])
            high = trace_ref[:, c * GROUP:(c + 1) * GROUP] >> 8
            total = jnp.zeros((32, GROUP), F32)
            for h in range(groups):
                total += jnp.where(high == h, picked[h * 64:h * 64 + 32] + picked[h * 64 + 32:h * 64 + 64], 0.0)
            own[turn, c] = total
            trace_copy(turn, c).start()

    def strains(v_ref):
        for i in range(pairs):
            tile = v_ref[:, i * 128:(i + 1) * 128]
            turned = swap(tile)
            vab[4 * i] = split_rows(jnp.where(left32, tile, 0.0))
            vab[4 * i + 1] = split_rows(jnp.where(left32, 0.0, turned))
            vab[4 * i + 2] = split_rows(jnp.where(left32, turned, 0.0))
            vab[4 * i + 3] = split_rows(jnp.where(left32, 0.0, tile))

        for n in range(rows):
            c0, c1, c2, c3 = (cols_smem[k, n] for k in range(4))
            x = jnp.concatenate(
                [vab[2 * c0] + vab[2 * c1 + 1], vab[2 * c2] + vab[2 * c3 + 1]], axis=1)
            o = mm(x, kk[n], NT)
            o = o[0:32] + o[32:64]
            ss[:, n * 128:(n + 1) * 128] = split_rows(o + swap(o))

    def forces():
        for n in range(rows):
            o = mm(ss[:, n * 128:(n + 1) * 128], kk[n])
            o = o[0:32] + o[32:64]
            for half in range(2):
                tile = o[:, half * 128:(half + 1) * 128]
                top, bottom = tile[0:16], tile[16:32]
                tp[n * 4 + 2 * half] = jnp.where(left16, top, swap(bottom))
                tp[n * 4 + 2 * half + 1] = jnp.where(left16, swap(top), bottom)

    def gather_forces(v_ref, out_ref):
        def add_up(step, total):
            for u in range(8):
                i = step * 8 + u
                total = total * csr_fs[0, i] + tp[csr_is[0, i]]
                run[i] = total
            return total

        lax.fori_loop(0, entries // 8, add_up, jnp.zeros((16, 128), F32))
        for i in range(pairs):
            lanes = slice(i * 128, (i + 1) * 128)
            a = run[csr_is[1, 2 * i]] * csr_fs[1, 2 * i]
            b = run[csr_is[1, 2 * i + 1]] * csr_fs[1, 2 * i + 1]
            tile = jnp.concatenate(
                [jnp.where(left16, a, swap(b)), jnp.where(left16, swap(a), b)], axis=0)
            out_ref[:, lanes] = tile + mass_ref[:, lanes] * v_ref[:, lanes]

    def take_jumps(turn):
        for c in range(chunks):
            trace_copy(turn, c).wait_recv()
            part[turn, c] = own[turn, c] - part[turn, c]

    def weight_of(c):
        lanes = slice(c * GROUP, (c + 1) * GROUP)
        return pen_ref[:, lanes] * pen_other[:, lanes]

    def add_jump(turn, out_ref):
        total = jnp.zeros((groups * 64, GROUP), F32)
        for c in range(chunks):
            lanes = slice(c * GROUP, (c + 1) * GROUP)
            jump = split_rows(weight_of(c) * part[turn, c])
            total += mm(masked_groups(jump, trace_ref[:, lanes] >> 8), hot[c], NT)
        for h in range(groups):
            lanes = slice(h * GROUP, (h + 1) * GROUP)
            out_ref[:, lanes] += total[h * 64:h * 64 + 32] + total[h * 64 + 32:h * 64 + 64]

    sent = []

    def stage(pay, index, slots, count, place, base):
        copies = []
        for j in range(1, count):
            copies.append(pltpu.make_async_remote_copy(
                src_ref=pay.at[index], dst_ref=slots.at[j - 1], send_sem=red_send.at[base + j],
                recv_sem=red_recv.at[base + j], device_id=place(j), device_id_type=MESH))
            copies[-1].start()
        sent.extend(copies)

        def finish():
            total = pay[index]
            for j, copy in enumerate(copies):
                copy.wait_recv()
                total += slots[j]
            return total

        return finish

    z_first = (me // z_size) * z_size
    span = comps + x_size + z_size

    def along_comp(j):
        return {"comp": lax.rem(mine + j, comps)}

    def along_x(j):
        return {"patch": lax.rem(me + j * z_size, patches)}

    def along_z(j):
        return {"patch": z_first + lax.rem(lax.rem(me, z_size) + j, z_size)}

    halves_of(r_ref, 0)
    send_trace(0, 0)
    strains(r_ref)
    forces()
    gather_forces(r_ref, q_ref)
    pen_copy.wait_recv()
    take_jumps(0)
    add_jump(0, q_ref)
    halves_of(q_ref, 64)
    send_trace(1, 64)

    both = s3[0:128]
    o = mm(both, both, NT)
    first, second = o[0:32] + o[32:64], o[64:96] + o[96:128]
    first, second = first + pltpu.roll(first, 96, 1), second + pltpu.roll(second, 96, 1)
    pay_a[0] = jnp.concatenate([pack4(first, 0), pack4(first, 2), pack4(second, 2)], axis=0)
    a_comp = stage(pay_a, 0, rc_a, comps, along_comp, 0)
    strains(q_ref)

    strain = ss[...]
    energy = mm(strain, strain, NT) * 0.5 + mm(split_rows(mass_ref[...] * q_ref[...]), s3[64:128], NT)
    pay_a[1] = a_comp()
    a_x = stage(pay_a, 1, rx_a, x_size, along_x, comps)
    take_jumps(1)
    for c in range(chunks):
        jump = part[1, c]
        energy += mm(split_rows(0.5 * weight_of(c) * jump), split_rows(jump), NT)
    fold[...] = jnp.zeros((32, 128), F32)
    fold[:, 0:64] = energy[0:32] + energy[32:64]
    third = fold[...]
    third = third + pltpu.roll(third, 96, 1)
    pay_b[0] = pack4(third, 0)
    b_comp = stage(pay_b, 0, rc_b, comps, along_comp, span)

    forces()
    pay_a[2] = a_x()
    a_z = stage(pay_a, 2, rz_a, z_size, along_z, comps + x_size)
    pay_b[1] = b_comp()
    b_x = stage(pay_b, 1, rx_b, x_size, along_x, span + comps)
    gather_forces(q_ref, t_ref)
    add_jump(1, t_ref)
    pay_b[2] = b_x()
    b_z = stage(pay_b, 2, rz_b, z_size, along_z, span + comps + x_size)
    halves_of(t_ref, 128)

    total = a_z()
    m0, m1, m2 = total[0:8], total[8:16], total[16:24]
    upper = unpack4(m1, 0) + unpack4(m2, 1) + unpack4(m0, 2)
    lower = unpack4(m2, 0) + unpack4(m1, 2)
    system = eliminate(jnp.concatenate([upper, lower], axis=0), 0, 32)
    lower = system[32:64] + unpack4(b_z(), 1)
    system = eliminate(jnp.concatenate([system[0:32], lower], axis=0), 32, 64)
    mixed = jnp.concatenate([system[0:32], system[0:32], system[32:64], system[32:64]], axis=0)
    weights = split_rows(jnp.transpose(mixed)[64:96])

    for h in range(groups):
        lanes = slice(h * GROUP, (h + 1) * GROUP)
        o = mm(weights, s3[0:128, lanes])
        sol_ref[:, lanes] = o[0:32] + o[32:64]
        o = mm(weights, s3[64:192, lanes])
        res_ref[:, lanes] = r_ref[:, lanes] - (o[0:32] + o[32:64])

    def drain(d, _):
        cell_copy(d).wait_send()
        return 0

    lax.fori_loop(1, patches, drain, 0)
    pen_copy.wait_send()
    for turn in range(2):
        for c in range(chunks):
            trace_copy(turn, c).wait_send()
    for copy in sent:
        copy.wait_send()


def shards(z_size, load_cases, mass_diag, stiffness, block_cols, trace_dofs, penalty, cell_partials, cell_owner, cell_dof):
    cases, dofs = load_cases.shape
    rows = stiffness.shape[0]
    traces, ncell = trace_dofs.shape[0], cell_dof.shape[0]
    patches, comps = lax.axis_size("patch"), lax.axis_size("comp")
    groups, chunks = dofs // GROUP, traces // GROUP
    entries = rows * 4
    vm = pl.BlockSpec(memory_space=pltpu.VMEM)
    hbm = pl.BlockSpec(memory_space=pltpu.HBM)
    field = jax.ShapeDtypeStruct((cases, dofs), F32)
    x_size = patches // z_size
    stages = comps + x_size + z_size

    def sums(tall):
        return [
            pltpu.VMEM((3, tall, 128), F32),
            pltpu.VMEM((comps - 1, tall, 128), F32),
            pltpu.VMEM((x_size - 1, tall, 128), F32),
            pltpu.VMEM((z_size - 1, tall, 128), F32),
        ]

    return pl.pallas_call(
        functools.partial(kernel, z_size),
        out_shape=(field, field),
        in_specs=[hbm] * 9,
        out_specs=(vm, vm),
        scratch_shapes=[
            pltpu.VMEM((cases, dofs), F32),
            pltpu.VMEM((1, dofs), F32),
            pltpu.VMEM(stiffness.shape, F32),
            pltpu.VMEM((4, rows), I32),
            pltpu.SMEM((4, rows), I32),
            pltpu.VMEM((1, traces), I32),
            pltpu.VMEM((1, traces), F32),
            pltpu.VMEM((cases, ncell), F32),
            pltpu.VMEM((1, ncell), I32),
            pltpu.VMEM((1, ncell), I32),
            pltpu.VMEM((rows, 128, 256), BF16),
            pltpu.VMEM((patches, 17, 128), F32),
            pltpu.VMEM((patches, 17, 128), F32),
            pltpu.VMEM((4, 128), I32),
            pltpu.VMEM((2, GROUP), I32),
            pltpu.VMEM((2, GROUP), F32),
            pltpu.SMEM((2, GROUP), I32),
            pltpu.SMEM((2, GROUP), F32),
            pltpu.VMEM((chunks, GROUP, GROUP), BF16),
            pltpu.VMEM((2, chunks, cases, GROUP), F32),
            pltpu.VMEM((2, chunks, cases, GROUP), F32),
            pltpu.VMEM((1, traces), F32),
            pltpu.VMEM((cases, dofs), F32),
            pltpu.VMEM((cases, dofs), F32),
            pltpu.VMEM((cases, dofs), F32),
            pltpu.VMEM((6 * cases, dofs), BF16),
            pltpu.VMEM((2 * rows, 64, 128), BF16),
            pltpu.VMEM((64, rows * 128), BF16),
            pltpu.VMEM((entries, 16, 128), F32),
            pltpu.VMEM((entries, 16, 128), F32),
            pltpu.VMEM((groups * 64, GROUP), F32),
            pltpu.VMEM((cases, 128), F32),
            *sums(24),
            *sums(8),
            pltpu.SemaphoreType.DMA((12,)),
            pltpu.SemaphoreType.DMA((patches,)),
            pltpu.SemaphoreType.DMA((patches,)),
            pltpu.SemaphoreType.DMA((2, chunks)),
            pltpu.SemaphoreType.DMA((2, chunks)),
            pltpu.SemaphoreType.DMA((2 * stages,)),
            pltpu.SemaphoreType.DMA((2 * stages,)),
        ],
        compiler_params=pltpu.CompilerParams(
            collective_id=0, has_side_effects=True, vmem_limit_bytes=40 * 1024 * 1024),
    )(
        *(pltpu.with_memory_space_constraint(x, pltpu.HBM) for x in (
            load_cases, mass_diag.reshape(1, -1), stiffness, block_cols.T, trace_dofs.reshape(1, -1),
            penalty.reshape(1, -1), cell_partials, cell_owner.reshape(1, -1), cell_dof.reshape(1, -1)))
    )


def solution(mesh):
    patches = mesh.shape["patch"]
    z_size = 8 if patches == 32 else patches // 2
    both = ("comp", "patch")
    return jax.shard_map(
        functools.partial(shards, z_size),
        mesh=mesh,
        in_specs=(
            P(None, both), P(both), P(both, None, None), P(both, None), P(both), P(both), P(None, both),
            P(both, None), P(both),
        ),
        out_specs=(P(None, both), P(None, both)),
        check_vma=False,
    )
```

```python
import functools

import jax
import jax.numpy as jnp
from jax import lax
from jax.experimental import pallas as pl
from jax.experimental.pallas import tpu as pltpu
from jax.sharding import PartitionSpec as P

CAP = 64
GROUP = 256
F32, BF16, I32 = jnp.float32, jnp.bfloat16, jnp.int32
NT = (((1,), (1,)), ((), ()))
NN = (((1,), (0,)), ((), ()))
MESH = pl.DeviceIdType.MESH


def mm(a, b, dims=NN):
    return lax.dot_general(a, b, dims, preferred_element_type=F32)


def split(x):
    hi = x.astype(BF16)
    return hi, (x - hi.astype(F32)).astype(BF16)


def split_rows(x):
    return jnp.concatenate(split(x), axis=0)


def iota(shape, dim):
    return lax.broadcasted_iota(I32, shape, dim)


def ones_where(mask):
    return jnp.where(mask, 1.0, 0.0)


def swap(x):
    return pltpu.roll(x, 64, 1)


def pack4(x, slot):
    band = iota((8, 128), 1) >> 5
    out = jnp.zeros((8, 128), F32)
    for g in range(4):
        out = jnp.where(band == g, pltpu.roll(x[8 * g:8 * g + 8], (32 * (g - slot)) % 128, 1), out)
    return out


def unpack4(x, slot):
    band = iota((8, 128), 1) >> 5
    return jnp.concatenate(
        [jnp.where(band == slot, pltpu.roll(x, (32 * (slot - g)) % 128, 1), 0.0) for g in range(4)], axis=0)


def eliminate(system, first, last):
    place = iota((64, 128), 0)
    for start in range(first, last, 8):
        wide = [jnp.broadcast_to(system[:, start + j:start + j + 1], (64, 128)) for j in range(8)]
        for j in range(8):
            k = start + j
            here = place == k
            inverse = 1.0 / wide[j][k:k + 1]
            factor = wide[j] * inverse
            row = system[k:k + 1]
            system = jnp.where(here, row * inverse, system - factor * row)
            for i in range(j + 1, 8):
                entry = wide[i][k:k + 1]
                wide[i] = jnp.where(here, entry * inverse, wide[i] - factor * entry)
    return system


def kernel(
    z_size, load_hbm, mass_hbm, stiff_hbm, cols_hbm, trace_hbm, pen_hbm, cells_hbm, owner_hbm,
    cdof_hbm, sol_ref, res_ref,
    load, mass_ref, stiff, cols_ref, cols_smem, trace_ref, pen_ref, cells_ref, owner_ref, cdof_ref,
    kk, send, recv, colp, csr_i, csr_f, csr_is, csr_fs, hot, own, part, pen_other, trace_other, twins,
    r_ref, q_ref, t_ref, s3, vab, ss, tp, run, fold, pay_a, rc_a, rx_a, rz_a, pay_b, rc_b, rx_b, rz_b,
    in_sem, a2a_send, a2a_recv, tr_send, tr_recv, red_send, red_recv,
):
    patches, comps = lax.axis_size("patch"), lax.axis_size("comp")
    me, mine = lax.axis_index("patch"), lax.axis_index("comp")
    cases, dofs = load.shape
    groups = dofs // GROUP
    ncell = cells_ref.shape[1]
    traces = trace_ref.shape[1]
    chunks = traces // GROUP
    rows = stiff.shape[0]
    entries = rows * 4
    spare = 64 - rows
    pairs = rows // 2
    left = iota((1, 128), 1) < 64
    left16 = iota((16, 128), 1) < 64
    left32 = iota((32, 128), 1) < 64

    get_stiff = pltpu.make_async_copy(stiff_hbm, stiff, in_sem.at[0])
    get_load = pltpu.make_async_copy(load_hbm, load, in_sem.at[1])
    small = [
        pltpu.make_async_copy(src, dst, in_sem.at[4 + i]) for i, (src, dst) in enumerate((
            (owner_hbm, owner_ref), (cdof_hbm, cdof_ref), (cells_hbm, cells_ref), (cols_hbm, cols_ref),
            (cols_hbm, cols_smem), (trace_hbm, trace_ref), (pen_hbm, pen_ref), (mass_hbm, mass_ref)))
    ]

    for copy in small:
        copy.start()
    barrier = pltpu.get_barrier_semaphore()

    def greet_patch(d, _):
        pl.semaphore_signal(barrier, inc=1, device_id={"patch": lax.rem(me + d, patches)}, device_id_type=MESH)
        return 0

    def greet_comp(d, _):
        pl.semaphore_signal(barrier, inc=1, device_id={"comp": lax.rem(mine + d, comps)}, device_id_type=MESH)
        return 0

    lax.fori_loop(1, patches, greet_patch, 0)
    lax.fori_loop(1, comps, greet_comp, 0)
    get_stiff.start()
    get_load.start()

    tri = ones_where(iota((ncell, ncell), 0) < iota((ncell, ncell), 1)).astype(BF16)
    for copy in small[0:3]:
        copy.wait()

    owner = owner_ref[...]
    hit = owner == iota((patches, ncell), 0)
    before = mm(ones_where(hit).astype(BF16), tri)
    pos = jnp.sum(jnp.where(hit, before, 0.0), axis=0, keepdims=True).astype(I32)
    slot = (owner & 3) * CAP + pos
    slot_hot = ones_where(iota((GROUP, ncell), 0) == slot).astype(BF16)
    cdof = cdof_ref[...]
    row16 = iota((16, ncell), 0)
    dof_rows = jnp.where(row16 == 0, cdof >> 8, jnp.where(row16 == 1, cdof & 255, 0)).astype(F32)
    cell_hi, cell_lo = split(cells_ref[...])
    cell_rows = jnp.concatenate([cell_hi, cell_lo, dof_rows.astype(BF16)], axis=0)
    for g in range(patches // 4):
        mask = jnp.broadcast_to(ones_where((owner >> 2) == g), (16, ncell)).astype(BF16)
        mask = jnp.concatenate([mask] * 5, axis=0)
        packed = mm(cell_rows * mask, slot_hot, NT)
        values = packed[0:32] + packed[32:64]
        places = packed[64:72]
        for half in range(2):
            tile = values[:, half * 128:(half + 1) * 128]
            top, bottom = tile[0:16], tile[16:32]
            place = places[:, half * 128:(half + 1) * 128]
            place_hi, place_lo = place[0:1], place[1:2]
            even = g * 4 + half * 2
            send[even, 0:16] = jnp.where(left16, top, swap(bottom))
            send[even + 1, 0:16] = jnp.where(left16, swap(top), bottom)
            send[even, 16:17] = jnp.where(left, place_hi, swap(place_lo))
            send[even + 1, 16:17] = jnp.where(left, swap(place_hi), place_lo)
    recv[0] = send[me]

    for copy in small[3:]:
        copy.wait()

    pl.semaphore_wait(barrier, patches + comps - 2)

    other = lax.rem(me + patches // 2, patches)

    def cell_copy(d):
        to = lax.rem(me + d, patches)
        return pltpu.make_async_remote_copy(
            src_ref=send.at[to], dst_ref=recv.at[d], send_sem=a2a_send.at[d], recv_sem=a2a_recv.at[d],
            device_id={"patch": to}, device_id_type=MESH,
        )

    def start_cell(d, _):
        cell_copy(d).start()
        return 0

    pen_copy = pltpu.make_async_remote_copy(
        src_ref=pen_ref, dst_ref=pen_other, send_sem=a2a_send.at[0], recv_sem=a2a_recv.at[0],
        device_id={"patch": other}, device_id_type=MESH,
    )
    other_copy = pltpu.make_async_remote_copy(
        src_ref=trace_ref, dst_ref=trace_other, send_sem=tr_send.at[2], recv_sem=tr_recv.at[2],
        device_id={"patch": other}, device_id_type=MESH,
    )
    x_size = patches // z_size
    pen_copy.start()
    other_copy.start()
    for x in [x_size // 2] + list(range(1, x_size // 2)) + list(range(x_size // 2 + 1, x_size)) + [0]:
        lax.fori_loop(max(1, x * z_size), (x + 1) * z_size, start_cell, 0)

    i0, i1 = iota((GROUP, GROUP), 0), iota((GROUP, GROUP), 1)
    colp[...] = jnp.full((4, 128), 255, I32)
    colp[:, 0:rows] = cols_ref[...]
    quad = colp[...]
    turned = pltpu.roll(quad, 64, 1)
    col = jnp.concatenate(
        [jnp.where(left, quad[0:1], turned[1:2]), jnp.where(left, quad[2:3], turned[3:4])], axis=1)
    col_of = jnp.transpose(jnp.broadcast_to(col, (GROUP, GROUP)))
    ahead = (col_of < col) | ((col_of == col) & (i0 < i1))
    rank = jnp.sum(jnp.where(ahead, 1, 0), axis=0, keepdims=True)
    at_rank = jnp.transpose(jnp.broadcast_to(rank, (GROUP, GROUP))) == i1
    order = jnp.sum(jnp.where(at_rank, i0, 0), axis=0, keepdims=True)
    ocol = jnp.sum(jnp.where(at_rank, col_of, 0), axis=0, keepdims=True)
    upto = jnp.sum(jnp.where(col_of <= i1, 1, 0), axis=0, keepdims=True)
    same = jnp.sum(jnp.where(col_of == i1, 1, 0), axis=0, keepdims=True)
    lane = iota((1, GROUP), 1)
    csr_i[0:1, :] = jnp.minimum((order & 63) * 4 + (order >> 6), entries - 1)
    csr_i[1:2, :] = jnp.clip(upto - 1, 0, entries - 1)
    csr_f[0:1, :] = ones_where((ocol == pltpu.roll(ocol, 1, 1)) & (lane > 0))
    csr_f[1:2, :] = ones_where(same > 0)
    put_i = pltpu.make_async_copy(csr_i, csr_is, in_sem.at[2])
    put_f = pltpu.make_async_copy(csr_f, csr_fs, in_sem.at[3])
    put_i.start()
    put_f.start()

    for c in range(chunks):
        lanes = slice(c * GROUP, (c + 1) * GROUP)
        hot[:, lanes] = ones_where(i0 == trace_ref[:, lanes] & 255).astype(BF16)

    get_stiff.wait()

    def halve(n, _):
        hi, lo = split(stiff[n])
        kk[n, 0:64] = hi
        kk[n, 64:128] = lo
        return 0

    lax.fori_loop(0, rows, halve, 0)
    put_i.wait()
    put_f.wait()

    pen_copy.wait_recv()
    other_copy.wait_recv()
    for c in range(chunks):
        lanes = slice(c * GROUP, (c + 1) * GROUP)
        mine_of = jnp.transpose(jnp.broadcast_to(trace_ref[:, lanes], (GROUP, GROUP)))
        other_of = jnp.transpose(jnp.broadcast_to(trace_other[:, lanes], (GROUP, GROUP)))
        for e in range(chunks):
            across = slice(e * GROUP, (e + 1) * GROUP)
            twins[lanes, across] = (
                ones_where(mine_of == trace_ref[:, across]) + ones_where(other_of == trace_other[:, across])
            ).astype(BF16)
    get_load.wait()

    def masked_groups(data, high):
        parts = []
        for h in range(groups):
            mask = jnp.broadcast_to(ones_where(high == h), (16, data.shape[1])).astype(BF16)
            parts.append(data * jnp.concatenate([mask] * 4, axis=0))
        return jnp.concatenate(parts, axis=0)

    def add_groups(total, base_ref, out_ref):
        for h in range(groups):
            lanes = slice(h * GROUP, (h + 1) * GROUP)
            out_ref[:, lanes] = base_ref[:, lanes] + total[h * 64:h * 64 + 32] + total[h * 64 + 32:h * 64 + 64]

    def arrive(d, _):
        cell_copy(d).wait_recv()
        return 0

    lax.fori_loop(1, patches, arrive, 0)
    data, highs, lows = [], [], []
    for d in range(0, patches, 2):
        a, b = recv[d], recv[d + 1]
        at, bt, ap, bp = a[0:16], b[0:16], a[16:17], b[16:17]
        data.append(split_rows(jnp.concatenate(
            [jnp.where(left16, at, swap(bt)), jnp.where(left16, swap(at), bt)], axis=0)))
        highs.append(jnp.where(left, ap, swap(bp)))
        lows.append(jnp.where(left, swap(ap), bp))
    data, high = jnp.concatenate(data, axis=1), jnp.concatenate(highs, axis=1)
    low_hot = jnp.concatenate(
        [ones_where(iota((GROUP, 128), 0) == x.astype(I32)).astype(BF16) for x in lows], axis=1)
    add_groups(mm(masked_groups(data, high.astype(I32)), low_hot, NT), load, r_ref)

    def trace_copy(turn):
        return pltpu.make_async_remote_copy(
            src_ref=own.at[turn], dst_ref=part.at[turn], send_sem=tr_send.at[turn], recv_sem=tr_recv.at[turn],
            device_id={"patch": other}, device_id_type=MESH,
        )

    def halves_of(v_ref, base):
        for h in range(groups):
            lanes = slice(h * GROUP, (h + 1) * GROUP)
            s3[base:base + 64, lanes] = split_rows(v_ref[:, lanes])

    def send_trace(turn, base):
        stacked = jnp.concatenate([s3[base:base + 64, h * GROUP:(h + 1) * GROUP] for h in range(groups)], axis=0)
        for c in range(chunks):
            lanes = slice(c * GROUP, (c + 1) * GROUP)
            picked = mm(stacked, hot[:, lanes])
            high = trace_ref[:, lanes] >> 8
            total = jnp.zeros((32, GROUP), F32)
            for h in range(groups):
                total = jnp.where(high == h, picked[h * 64:h * 64 + 32] + picked[h * 64 + 32:h * 64 + 64], total)
            own[turn, :, lanes] = total
        trace_copy(turn).start()

    def strains(v_ref):
        for i in range(pairs):
            tile = v_ref[:, i * 128:(i + 1) * 128]
            turned = swap(tile)
            vab[4 * i] = split_rows(jnp.where(left32, tile, 0.0))
            vab[4 * i + 1] = split_rows(jnp.where(left32, 0.0, turned))
            vab[4 * i + 2] = split_rows(jnp.where(left32, turned, 0.0))
            vab[4 * i + 3] = split_rows(jnp.where(left32, 0.0, tile))

        for n in range(rows):
            c0, c1, c2, c3 = (cols_smem[k, n] for k in range(4))
            x = jnp.concatenate(
                [vab[2 * c0] + vab[2 * c1 + 1], vab[2 * c2] + vab[2 * c3 + 1]], axis=1)
            o = mm(x, kk[n], NT)
            o = o[0:32] + o[32:64]
            ss[:, n * 128:(n + 1) * 128] = split_rows(o + swap(o))

    def forces():
        for n in range(rows):
            o = mm(ss[:, n * 128:(n + 1) * 128], kk[n])
            o = o[0:32] + o[32:64]
            for half in range(2):
                tile = o[:, half * 128:(half + 1) * 128]
                top, bottom = tile[0:16], tile[16:32]
                tp[n * 4 + 2 * half] = jnp.where(left16, top, swap(bottom))
                tp[n * 4 + 2 * half + 1] = jnp.where(left16, swap(top), bottom)

    def gather_forces(v_ref, out_ref):
        def add_up(step, total):
            for u in range(8):
                i = step * 8 + u
                total = total * csr_fs[0, i] + tp[csr_is[0, i]]
                run[i] = total
            return total

        lax.fori_loop(0, entries // 8, add_up, jnp.zeros((16, 128), F32))
        for i in range(pairs):
            lanes = slice(i * 128, (i + 1) * 128)
            a = run[csr_is[1, 2 * i]] * csr_fs[1, 2 * i]
            b = run[csr_is[1, 2 * i + 1]] * csr_fs[1, 2 * i + 1]
            tile = jnp.concatenate(
                [jnp.where(left16, a, swap(b)), jnp.where(left16, swap(a), b)], axis=0)
            out_ref[:, lanes] = tile + mass_ref[:, lanes] * v_ref[:, lanes]

    def add_jump(jump, out_ref):
        add_groups(mm(masked_groups(jump, trace_ref[...] >> 8), hot[...], NT), out_ref, out_ref)

    sent = []

    def stage(pay, index, slots, count, place, base):
        copies = []
        for j in range(1, count):
            copies.append(pltpu.make_async_remote_copy(
                src_ref=pay.at[index], dst_ref=slots.at[j - 1], send_sem=red_send.at[base + j],
                recv_sem=red_recv.at[base + j], device_id=place(j), device_id_type=MESH))
            copies[-1].start()
        sent.extend(copies)

        def finish():
            total = pay[index]
            for j, copy in enumerate(copies):
                copy.wait_recv()
                total += slots[j]
            return total

        return finish

    z_first = (me // z_size) * z_size
    span = comps + x_size + z_size

    def along_comp(j):
        return {"comp": lax.rem(mine + j, comps)}

    def along_x(j):
        return {"patch": lax.rem(me + j * z_size, patches)}

    def along_z(j):
        return {"patch": z_first + lax.rem(lax.rem(me, z_size) + j, z_size)}

    weight = pen_ref[...] * pen_other[...]
    halves_of(r_ref, 0)
    send_trace(0, 0)
    strains(r_ref)
    forces()
    gather_forces(r_ref, q_ref)
    halves_of(q_ref, 64)
    send_trace(1, 64)
    trace_copy(0).wait_recv()
    first_jump = split_rows(weight * (own[0] - part[0]))
    add_jump(first_jump, q_ref)
    halves_of(q_ref, 64)

    both = s3[0:128]
    o = mm(both, both, NT)
    first, second = o[0:32] + o[32:64], o[64:96] + o[96:128]
    first, second = first + pltpu.roll(first, 96, 1), second + pltpu.roll(second, 96, 1)
    pay_a[0] = jnp.concatenate([pack4(first, 0), pack4(first, 2), pack4(second, 2)], axis=0)
    a_comp = stage(pay_a, 0, rc_a, comps, along_comp, 0)
    strains(q_ref)

    strain = ss[...]
    energy = mm(strain, strain, NT) * 0.5 + mm(split_rows(mass_ref[...] * q_ref[...]), s3[64:128], NT)
    turn = mm(first_jump, twins[...])
    trace_copy(1).wait_recv()
    jump = own[1] - part[1] + turn[0:32] + turn[32:64]
    energy += mm(split_rows(0.5 * weight * jump), split_rows(jump), NT)
    fold[...] = jnp.zeros((32, 128), F32)
    fold[:, 0:64] = energy[0:32] + energy[32:64]
    third = fold[...]
    third = third + pltpu.roll(third, 96, 1)
    pay_b[0] = pack4(third, 0)
    b_comp = stage(pay_b, 0, rc_b, comps, along_comp, span)

    pay_a[1] = a_comp()
    a_x = stage(pay_a, 1, rx_a, x_size, along_x, comps)
    forces()
    pay_b[1] = b_comp()
    b_x = stage(pay_b, 1, rx_b, x_size, along_x, span + comps)
    gather_forces(q_ref, t_ref)
    add_jump(split_rows(weight * jump), t_ref)
    pay_a[2] = a_x()
    a_z = stage(pay_a, 2, rz_a, z_size, along_z, comps + x_size)
    pay_b[2] = b_x()
    b_z = stage(pay_b, 2, rz_b, z_size, along_z, span + comps + x_size)
    halves_of(t_ref, 128)

    total = a_z()
    m0, m1, m2 = total[0:8], total[8:16], total[16:24]
    upper = unpack4(m1, 0) + unpack4(m2, 1) + unpack4(m0, 2)
    lower = unpack4(m2, 0) + unpack4(m1, 2)
    system = eliminate(jnp.concatenate([upper, lower], axis=0), 0, 32)
    lower = system[32:64] + unpack4(b_z(), 1)
    system = eliminate(jnp.concatenate([system[0:32], lower], axis=0), 32, 64)
    mixed = jnp.concatenate([system[0:32], system[0:32], system[32:64], system[32:64]], axis=0)
    weights = split_rows(jnp.transpose(mixed)[64:96])

    for h in range(groups):
        lanes = slice(h * GROUP, (h + 1) * GROUP)
        o = mm(weights, s3[0:128, lanes])
        sol_ref[:, lanes] = o[0:32] + o[32:64]
        o = mm(weights, s3[64:192, lanes])
        res_ref[:, lanes] = r_ref[:, lanes] - (o[0:32] + o[32:64])

    def drain(d, _):
        cell_copy(d).wait_send()
        return 0

    lax.fori_loop(1, patches, drain, 0)
    pen_copy.wait_send()
    other_copy.wait_send()
    trace_copy(0).wait_send()
    trace_copy(1).wait_send()
    for copy in sent:
        copy.wait_send()


def shards(z_size, load_cases, mass_diag, stiffness, block_cols, trace_dofs, penalty, cell_partials, cell_owner, cell_dof):
    cases, dofs = load_cases.shape
    rows = stiffness.shape[0]
    traces, ncell = trace_dofs.shape[0], cell_dof.shape[0]
    patches, comps = lax.axis_size("patch"), lax.axis_size("comp")
    groups = dofs // GROUP
    entries = rows * 4
    vm = pl.BlockSpec(memory_space=pltpu.VMEM)
    hbm = pl.BlockSpec(memory_space=pltpu.HBM)
    field = jax.ShapeDtypeStruct((cases, dofs), F32)
    x_size = patches // z_size
    stages = comps + x_size + z_size

    def sums(tall):
        return [
            pltpu.VMEM((3, tall, 128), F32),
            pltpu.VMEM((comps - 1, tall, 128), F32),
            pltpu.VMEM((x_size - 1, tall, 128), F32),
            pltpu.VMEM((z_size - 1, tall, 128), F32),
        ]

    return pl.pallas_call(
        functools.partial(kernel, z_size),
        out_shape=(field, field),
        in_specs=[hbm] * 9,
        out_specs=(vm, vm),
        scratch_shapes=[
            pltpu.VMEM((cases, dofs), F32),
            pltpu.VMEM((1, dofs), F32),
            pltpu.VMEM(stiffness.shape, F32),
            pltpu.VMEM((4, rows), I32),
            pltpu.SMEM((4, rows), I32),
            pltpu.VMEM((1, traces), I32),
            pltpu.VMEM((1, traces), F32),
            pltpu.VMEM((cases, ncell), F32),
            pltpu.VMEM((1, ncell), I32),
            pltpu.VMEM((1, ncell), I32),
            pltpu.VMEM((rows, 128, 256), BF16),
            pltpu.VMEM((patches, 17, 128), F32),
            pltpu.VMEM((patches, 17, 128), F32),
            pltpu.VMEM((4, 128), I32),
            pltpu.VMEM((2, GROUP), I32),
            pltpu.VMEM((2, GROUP), F32),
            pltpu.SMEM((2, GROUP), I32),
            pltpu.SMEM((2, GROUP), F32),
            pltpu.VMEM((GROUP, traces), BF16),
            pltpu.VMEM((2, cases, traces), F32),
            pltpu.VMEM((2, cases, traces), F32),
            pltpu.VMEM((1, traces), F32),
            pltpu.VMEM((1, traces), I32),
            pltpu.VMEM((traces, traces), BF16),
            pltpu.VMEM((cases, dofs), F32),
            pltpu.VMEM((cases, dofs), F32),
            pltpu.VMEM((cases, dofs), F32),
            pltpu.VMEM((6 * cases, dofs), BF16),
            pltpu.VMEM((2 * rows, 64, 128), BF16),
            pltpu.VMEM((64, rows * 128), BF16),
            pltpu.VMEM((entries, 16, 128), F32),
            pltpu.VMEM((entries, 16, 128), F32),
            pltpu.VMEM((cases, 128), F32),
            *sums(24),
            *sums(8),
            pltpu.SemaphoreType.DMA((12,)),
            pltpu.SemaphoreType.DMA((patches,)),
            pltpu.SemaphoreType.DMA((patches,)),
            pltpu.SemaphoreType.DMA((3,)),
            pltpu.SemaphoreType.DMA((3,)),
            pltpu.SemaphoreType.DMA((2 * stages,)),
            pltpu.SemaphoreType.DMA((2 * stages,)),
        ],
        compiler_params=pltpu.CompilerParams(
            collective_id=0, has_side_effects=True, vmem_limit_bytes=40 * 1024 * 1024),
    )(
        *(pltpu.with_memory_space_constraint(x, pltpu.HBM) for x in (
            load_cases, mass_diag.reshape(1, -1), stiffness, block_cols.T, trace_dofs.reshape(1, -1),
            penalty.reshape(1, -1), cell_partials, cell_owner.reshape(1, -1), cell_dof.reshape(1, -1)))
    )


def solution(mesh):
    patches = mesh.shape["patch"]
    z_size = 8 if patches == 32 else patches // 2
    both = ("comp", "patch")
    return jax.shard_map(
        functools.partial(shards, z_size),
        mesh=mesh,
        in_specs=(
            P(None, both), P(both), P(both, None, None), P(both, None), P(both), P(both), P(None, both),
            P(both, None), P(both),
        ),
        out_specs=(P(None, both), P(None, both)),
        check_vma=False,
    )
```

```python
import functools

import jax
import jax.numpy as jnp
from jax import lax
from jax.experimental import pallas as pl
from jax.experimental.pallas import tpu as pltpu
from jax.sharding import PartitionSpec as P

CAP = 64
GROUP = 256
F32, BF16, I32 = jnp.float32, jnp.bfloat16, jnp.int32
NT = (((1,), (1,)), ((), ()))
NN = (((1,), (0,)), ((), ()))
MESH = pl.DeviceIdType.MESH


def mm(a, b, dims=NN):
    return lax.dot_general(a, b, dims, preferred_element_type=F32)


def split(x):
    hi = x.astype(BF16)
    return hi, (x - hi.astype(F32)).astype(BF16)


def split_rows(x):
    return jnp.concatenate(split(x), axis=0)


def iota(shape, dim):
    return lax.broadcasted_iota(I32, shape, dim)


def ones_where(mask):
    return jnp.where(mask, 1.0, 0.0)


def swap(x):
    return pltpu.roll(x, 64, 1)


def pack4(x, slot):
    band = iota((8, 128), 1) >> 5
    out = jnp.zeros((8, 128), F32)
    for g in range(4):
        out = jnp.where(band == g, pltpu.roll(x[8 * g:8 * g + 8], (32 * (g - slot)) % 128, 1), out)
    return out


def unpack4(x, slot):
    band = iota((8, 128), 1) >> 5
    return jnp.concatenate(
        [jnp.where(band == slot, pltpu.roll(x, (32 * (slot - g)) % 128, 1), 0.0) for g in range(4)], axis=0)


def eliminate(system, first, last):
    place = iota((64, 128), 0)
    for start in range(first, last, 8):
        wide = [jnp.broadcast_to(system[:, start + j:start + j + 1], (64, 128)) for j in range(8)]
        for j in range(8):
            k = start + j
            here = place == k
            inverse = 1.0 / wide[j][k:k + 1]
            factor = wide[j] * inverse
            row = system[k:k + 1]
            system = jnp.where(here, row * inverse, system - factor * row)
            for i in range(j + 1, 8):
                entry = wide[i][k:k + 1]
                wide[i] = jnp.where(here, entry * inverse, wide[i] - factor * entry)
    return system


def kernel(
    z_size, load_hbm, mass_hbm, stiff_hbm, cols_hbm, trace_hbm, pen_hbm, cells_hbm, owner_hbm,
    cdof_hbm, r_ref, s3, weights_ref,
    load, mass_ref, stiff, cols_ref, cols_smem, trace_ref, pen_ref, cells_ref, owner_ref, cdof_ref,
    kk, send, recv, colp, csr_i, csr_f, csr_is, csr_fs, hot, own, part, pen_other, trace_other, twins,
    q_ref, t_ref, vab, ss, tp, run, fold, pay_a, rc_a, rx_a, rz_a, pay_b, rc_b, rx_b, rz_b,
    in_sem, a2a_send, a2a_recv, tr_send, tr_recv, red_send, red_recv,
):
    patches, comps = lax.axis_size("patch"), lax.axis_size("comp")
    me, mine = lax.axis_index("patch"), lax.axis_index("comp")
    cases, dofs = load.shape
    groups = dofs // GROUP
    ncell = cells_ref.shape[1]
    traces = trace_ref.shape[1]
    chunks = traces // GROUP
    rows = stiff.shape[0]
    entries = rows * 4
    spare = 64 - rows
    pairs = rows // 2
    left = iota((1, 128), 1) < 64
    left16 = iota((16, 128), 1) < 64
    left32 = iota((32, 128), 1) < 64

    get_stiff = pltpu.make_async_copy(stiff_hbm, stiff, in_sem.at[0])
    get_load = pltpu.make_async_copy(load_hbm, load, in_sem.at[1])
    small = [
        pltpu.make_async_copy(src, dst, in_sem.at[4 + i]) for i, (src, dst) in enumerate((
            (owner_hbm, owner_ref), (cdof_hbm, cdof_ref), (cells_hbm, cells_ref), (cols_hbm, cols_ref),
            (cols_hbm, cols_smem), (trace_hbm, trace_ref), (pen_hbm, pen_ref), (mass_hbm, mass_ref)))
    ]

    for copy in small:
        copy.start()
    barrier = pltpu.get_barrier_semaphore()

    def greet_patch(d, _):
        pl.semaphore_signal(barrier, inc=1, device_id={"patch": lax.rem(me + d, patches)}, device_id_type=MESH)
        return 0

    def greet_comp(d, _):
        pl.semaphore_signal(barrier, inc=1, device_id={"comp": lax.rem(mine + d, comps)}, device_id_type=MESH)
        return 0

    lax.fori_loop(1, patches, greet_patch, 0)
    lax.fori_loop(1, comps, greet_comp, 0)
    get_stiff.start()
    get_load.start()

    tri = ones_where(iota((ncell, ncell), 0) < iota((ncell, ncell), 1)).astype(BF16)
    for copy in small[0:3]:
        copy.wait()

    owner = owner_ref[...]
    hit = owner == iota((patches, ncell), 0)
    before = mm(ones_where(hit).astype(BF16), tri)
    pos = jnp.sum(jnp.where(hit, before, 0.0), axis=0, keepdims=True).astype(I32)
    slot = (owner & 3) * CAP + pos
    slot_hot = ones_where(iota((GROUP, ncell), 0) == slot).astype(BF16)
    cdof = cdof_ref[...]
    row16 = iota((16, ncell), 0)
    dof_rows = jnp.where(row16 == 0, cdof >> 8, jnp.where(row16 == 1, cdof & 255, 0)).astype(F32)
    cell_hi, cell_lo = split(cells_ref[...])
    cell_rows = jnp.concatenate([cell_hi, cell_lo, dof_rows.astype(BF16)], axis=0)
    masked = []
    for g in range(patches // 4):
        mask = jnp.broadcast_to(ones_where((owner >> 2) == g), (16, ncell)).astype(BF16)
        masked.append(cell_rows * jnp.concatenate([mask] * 5, axis=0))
    packed = mm(jnp.concatenate(masked, axis=0), slot_hot, NT)
    for g in range(patches // 4):
        values = packed[g * 80:g * 80 + 32] + packed[g * 80 + 32:g * 80 + 64]
        places = packed[g * 80 + 64:g * 80 + 72]
        for half in range(2):
            tile = values[:, half * 128:(half + 1) * 128]
            top, bottom = tile[0:16], tile[16:32]
            place = places[:, half * 128:(half + 1) * 128]
            place_hi, place_lo = place[0:1], place[1:2]
            even = g * 4 + half * 2
            send[even, 0:16] = jnp.where(left16, top, swap(bottom))
            send[even + 1, 0:16] = jnp.where(left16, swap(top), bottom)
            send[even, 16:17] = jnp.where(left, place_hi, swap(place_lo))
            send[even + 1, 16:17] = jnp.where(left, swap(place_hi), place_lo)
    recv[0] = send[me]

    for copy in small[3:]:
        copy.wait()

    pl.semaphore_wait(barrier, patches + comps - 2)

    other = lax.rem(me + patches // 2, patches)

    def cell_copy(d):
        to = lax.rem(me + d, patches)
        return pltpu.make_async_remote_copy(
            src_ref=send.at[to], dst_ref=recv.at[d], send_sem=a2a_send.at[d], recv_sem=a2a_recv.at[d],
            device_id={"patch": to}, device_id_type=MESH,
        )

    def start_cell(d, _):
        cell_copy(d).start()
        return 0

    pen_copy = pltpu.make_async_remote_copy(
        src_ref=pen_ref, dst_ref=pen_other, send_sem=a2a_send.at[0], recv_sem=a2a_recv.at[0],
        device_id={"patch": other}, device_id_type=MESH,
    )
    other_copy = pltpu.make_async_remote_copy(
        src_ref=trace_ref, dst_ref=trace_other, send_sem=tr_send.at[2], recv_sem=tr_recv.at[2],
        device_id={"patch": other}, device_id_type=MESH,
    )
    x_size = patches // z_size
    pen_copy.start()
    other_copy.start()
    far_first = [x_size // 2] + list(range(1, x_size // 2)) + list(range(x_size // 2 + 1, x_size)) + [0]
    for x in far_first:
        lax.fori_loop(max(1, x * z_size), (x + 1) * z_size, start_cell, 0)

    i0, i1 = iota((GROUP, GROUP), 0), iota((GROUP, GROUP), 1)
    colp[...] = jnp.full((4, 128), 255, I32)
    colp[:, 0:rows] = cols_ref[...]
    quad = colp[...]
    turned = pltpu.roll(quad, 64, 1)
    col = jnp.concatenate(
        [jnp.where(left, quad[0:1], turned[1:2]), jnp.where(left, quad[2:3], turned[3:4])], axis=1)
    col_of = jnp.transpose(jnp.broadcast_to(col, (GROUP, GROUP)))
    ahead = (col_of < col) | ((col_of == col) & (i0 < i1))
    rank = jnp.sum(jnp.where(ahead, 1, 0), axis=0, keepdims=True)
    at_rank = jnp.transpose(jnp.broadcast_to(rank, (GROUP, GROUP))) == i1
    order = jnp.sum(jnp.where(at_rank, i0, 0), axis=0, keepdims=True)
    ocol = jnp.sum(jnp.where(at_rank, col_of, 0), axis=0, keepdims=True)
    upto = jnp.sum(jnp.where(col_of <= i1, 1, 0), axis=0, keepdims=True)
    same = jnp.sum(jnp.where(col_of == i1, 1, 0), axis=0, keepdims=True)
    lane = iota((1, GROUP), 1)
    csr_i[0:1, :] = jnp.minimum((order & 63) * 4 + (order >> 6), entries - 1)
    csr_i[1:2, :] = jnp.clip(upto - 1, 0, entries - 1)
    csr_f[0:1, :] = ones_where((ocol == pltpu.roll(ocol, 1, 1)) & (lane > 0))
    csr_f[1:2, :] = ones_where(same > 0)
    put_i = pltpu.make_async_copy(csr_i, csr_is, in_sem.at[2])
    put_f = pltpu.make_async_copy(csr_f, csr_fs, in_sem.at[3])
    put_i.start()
    put_f.start()

    for c in range(chunks):
        lanes = slice(c * GROUP, (c + 1) * GROUP)
        hot[:, lanes] = ones_where(i0 == trace_ref[:, lanes] & 255).astype(BF16)

    get_stiff.wait()

    def halve(n, _):
        hi, lo = split(stiff[n])
        kk[n, 0:64] = hi
        kk[n, 64:128] = lo
        return 0

    lax.fori_loop(0, rows, halve, 0)
    put_i.wait()
    put_f.wait()

    pen_copy.wait_recv()
    other_copy.wait_recv()
    for c in range(chunks):
        lanes = slice(c * GROUP, (c + 1) * GROUP)
        mine_of = jnp.transpose(jnp.broadcast_to(trace_ref[:, lanes], (GROUP, GROUP)))
        other_of = jnp.transpose(jnp.broadcast_to(trace_other[:, lanes], (GROUP, GROUP)))
        for e in range(chunks):
            across = slice(e * GROUP, (e + 1) * GROUP)
            twins[lanes, across] = (
                ones_where(mine_of == trace_ref[:, across]) + ones_where(other_of == trace_other[:, across])
            ).astype(BF16)
    get_load.wait()

    def masked_groups(data, high):
        parts = []
        for h in range(groups):
            mask = jnp.broadcast_to(ones_where(high == h), (16, data.shape[1])).astype(BF16)
            parts.append(data * jnp.concatenate([mask] * 4, axis=0))
        return jnp.concatenate(parts, axis=0)

    def add_groups(total, base_ref, out_ref):
        for h in range(groups):
            lanes = slice(h * GROUP, (h + 1) * GROUP)
            out_ref[:, lanes] = base_ref[:, lanes] + total[h * 64:h * 64 + 32] + total[h * 64 + 32:h * 64 + 64]

    def arrive(d, _):
        cell_copy(d).wait_recv()
        return 0

    def place(steps, base_ref):
        for x in steps:
            lax.fori_loop(max(1, x * z_size), (x + 1) * z_size, arrive, 0)
        data, highs, lows = [], [], []
        for x in steps:
            for d in range(x * z_size, (x + 1) * z_size, 2):
                a, b = recv[d], recv[d + 1]
                at, bt, ap, bp = a[0:16], b[0:16], a[16:17], b[16:17]
                data.append(split_rows(jnp.concatenate(
                    [jnp.where(left16, at, swap(bt)), jnp.where(left16, swap(at), bt)], axis=0)))
                highs.append(jnp.where(left, ap, swap(bp)).astype(I32))
                lows.append(jnp.where(left, swap(ap), bp).astype(I32))
        rows_of = iota((GROUP, 128), 0)
        low_hot = jnp.concatenate([ones_where(rows_of == low).astype(BF16) for low in lows], axis=1)
        data = masked_groups(jnp.concatenate(data, axis=1), jnp.concatenate(highs, axis=1))
        add_groups(mm(data, low_hot, NT), base_ref, r_ref)

    place(far_first[:x_size // 2], load)
    place(far_first[x_size // 2:], r_ref)

    def trace_copy(turn):
        return pltpu.make_async_remote_copy(
            src_ref=own.at[turn], dst_ref=part.at[turn], send_sem=tr_send.at[turn], recv_sem=tr_recv.at[turn],
            device_id={"patch": other}, device_id_type=MESH,
        )

    def halves_of(v_ref, base):
        for h in range(groups):
            lanes = slice(h * GROUP, (h + 1) * GROUP)
            s3[base:base + 64, lanes] = split_rows(v_ref[:, lanes])

    def send_trace(turn, base):
        stacked = jnp.concatenate([s3[base:base + 64, h * GROUP:(h + 1) * GROUP] for h in range(groups)], axis=0)
        for c in range(chunks):
            lanes = slice(c * GROUP, (c + 1) * GROUP)
            picked = mm(stacked, hot[:, lanes])
            high = trace_ref[:, lanes] >> 8
            total = jnp.zeros((32, GROUP), F32)
            for h in range(groups):
                total = jnp.where(high == h, picked[h * 64:h * 64 + 32] + picked[h * 64 + 32:h * 64 + 64], total)
            own[turn, :, lanes] = total
        trace_copy(turn).start()

    def strains(v_ref):
        for i in range(pairs):
            tile = v_ref[:, i * 128:(i + 1) * 128]
            turned = swap(tile)
            vab[4 * i] = split_rows(jnp.where(left32, tile, 0.0))
            vab[4 * i + 1] = split_rows(jnp.where(left32, 0.0, turned))
            vab[4 * i + 2] = split_rows(jnp.where(left32, turned, 0.0))
            vab[4 * i + 3] = split_rows(jnp.where(left32, 0.0, tile))

        for n in range(rows):
            c0, c1, c2, c3 = (cols_smem[k, n] for k in range(4))
            x = jnp.concatenate(
                [vab[2 * c0] + vab[2 * c1 + 1], vab[2 * c2] + vab[2 * c3 + 1]], axis=1)
            o = mm(x, kk[n], NT)
            o = o[0:32] + o[32:64]
            ss[:, n * 128:(n + 1) * 128] = split_rows(o + swap(o))

    def forces():
        for n in range(rows):
            o = mm(ss[:, n * 128:(n + 1) * 128], kk[n])
            o = o[0:32] + o[32:64]
            for half in range(2):
                tile = o[:, half * 128:(half + 1) * 128]
                top, bottom = tile[0:16], tile[16:32]
                tp[n * 4 + 2 * half] = jnp.where(left16, top, swap(bottom))
                tp[n * 4 + 2 * half + 1] = jnp.where(left16, swap(top), bottom)

    def gather_forces(v_ref, out_ref):
        def add_up(step, total):
            for u in range(8):
                i = step * 8 + u
                total = total * csr_fs[0, i] + tp[csr_is[0, i]]
                run[i] = total
            return total

        lax.fori_loop(0, entries // 8, add_up, jnp.zeros((16, 128), F32))
        for i in range(pairs):
            lanes = slice(i * 128, (i + 1) * 128)
            a = run[csr_is[1, 2 * i]] * csr_fs[1, 2 * i]
            b = run[csr_is[1, 2 * i + 1]] * csr_fs[1, 2 * i + 1]
            tile = jnp.concatenate(
                [jnp.where(left16, a, swap(b)), jnp.where(left16, swap(a), b)], axis=0)
            out_ref[:, lanes] = tile + mass_ref[:, lanes] * v_ref[:, lanes]

    def add_jump(jump, out_ref):
        add_groups(mm(masked_groups(jump, trace_ref[...] >> 8), hot[...], NT), out_ref, out_ref)

    sent = []

    def stage(pay, index, slots, count, place, base):
        copies = []
        for j in range(1, count):
            copies.append(pltpu.make_async_remote_copy(
                src_ref=pay.at[index], dst_ref=slots.at[j - 1], send_sem=red_send.at[base + j],
                recv_sem=red_recv.at[base + j], device_id=place(j), device_id_type=MESH))
            copies[-1].start()
        sent.extend(copies)

        def finish():
            total = pay[index]
            for j, copy in enumerate(copies):
                copy.wait_recv()
                total += slots[j]
            return total

        return finish

    z_first = (me // z_size) * z_size
    span = comps + x_size + z_size

    def along_comp(j):
        return {"comp": lax.rem(mine + j, comps)}

    def along_x(j):
        return {"patch": lax.rem(me + j * z_size, patches)}

    def along_z(j):
        return {"patch": z_first + lax.rem(lax.rem(me, z_size) + j, z_size)}

    weight = pen_ref[...] * pen_other[...]
    halves_of(r_ref, 0)
    send_trace(0, 0)
    strains(r_ref)
    forces()
    gather_forces(r_ref, q_ref)
    halves_of(q_ref, 64)
    send_trace(1, 64)
    trace_copy(0).wait_recv()
    first_jump = split_rows(weight * (own[0] - part[0]))
    add_jump(first_jump, q_ref)
    halves_of(q_ref, 64)

    both = s3[0:128]
    o = mm(both, both, NT)
    first, second = o[0:32] + o[32:64], o[64:96] + o[96:128]
    first, second = first + pltpu.roll(first, 96, 1), second + pltpu.roll(second, 96, 1)
    pay_a[0] = jnp.concatenate([pack4(first, 0), pack4(first, 2), pack4(second, 2)], axis=0)
    a_z = stage(pay_a, 0, rz_a, z_size, along_z, comps + x_size)
    strains(q_ref)

    strain = ss[...]
    energy = mm(strain, strain, NT) * 0.5 + mm(split_rows(mass_ref[...] * q_ref[...]), s3[64:128], NT)
    turn = mm(first_jump, twins[...])
    trace_copy(1).wait_recv()
    jump = own[1] - part[1] + turn[0:32] + turn[32:64]
    energy += mm(split_rows(0.5 * weight * jump), split_rows(jump), NT)
    fold[...] = jnp.zeros((32, 128), F32)
    fold[:, 0:64] = energy[0:32] + energy[32:64]
    third = fold[...]
    third = third + pltpu.roll(third, 96, 1)
    pay_b[0] = pack4(third, 0)
    b_comp = stage(pay_b, 0, rc_b, comps, along_comp, span)

    forces()
    gather_forces(q_ref, t_ref)
    add_jump(split_rows(weight * jump), t_ref)
    halves_of(t_ref, 128)
    pay_a[1] = a_z()
    a_x = stage(pay_a, 1, rx_a, x_size, along_x, comps)
    pay_b[1] = b_comp()
    b_x = stage(pay_b, 1, rx_b, x_size, along_x, span + comps)
    pay_a[2] = a_x()
    a_comp = stage(pay_a, 2, rc_a, comps, along_comp, 0)
    pay_b[2] = b_x()
    b_z = stage(pay_b, 2, rz_b, z_size, along_z, span + comps + x_size)

    def drain(d, _):
        cell_copy(d).wait_send()
        return 0

    lax.fori_loop(1, patches, drain, 0)
    pen_copy.wait_send()
    other_copy.wait_send()
    trace_copy(0).wait_send()
    trace_copy(1).wait_send()

    total = a_comp()
    m0, m1, m2 = total[0:8], total[8:16], total[16:24]
    upper = unpack4(m1, 0) + unpack4(m2, 1) + unpack4(m0, 2)
    lower = unpack4(m2, 0) + unpack4(m1, 2)
    system = eliminate(jnp.concatenate([upper, lower], axis=0), 0, 32)
    lower = system[32:64] + unpack4(b_z(), 1)
    system = eliminate(jnp.concatenate([system[0:32], lower], axis=0), 32, 64)
    mixed = jnp.concatenate([system[0:32], system[0:32], system[32:64], system[32:64]], axis=0)
    weights_ref[...] = split_rows(jnp.transpose(mixed)[64:96])
    for copy in sent:
        copy.wait_send()


def finish(weights_ref, s3, r_ref, sol_hbm, res_hbm, sol, res, sems):
    weights = weights_ref[...]
    dofs = sol.shape[1]
    width = dofs // 4
    copies = []
    for part in range(4):
        for h in range(width // GROUP):
            lanes = slice(part * width + h * GROUP, part * width + (h + 1) * GROUP)
            o = mm(weights, s3[0:128, lanes])
            sol[:, lanes] = o[0:32] + o[32:64]
            o = mm(weights, s3[64:192, lanes])
            res[:, lanes] = r_ref[:, lanes] - (o[0:32] + o[32:64])
        lanes = pl.ds(part * width, width)
        for i, (src, dst) in enumerate(((sol, sol_hbm), (res, res_hbm))):
            copies.append(pltpu.make_async_copy(src.at[:, lanes], dst.at[:, lanes], sems.at[part, i]))
            copies[-1].start()
    for copy in copies:
        copy.wait()


def shards(z_size, load_cases, mass_diag, stiffness, block_cols, trace_dofs, penalty, cell_partials, cell_owner, cell_dof):
    cases, dofs = load_cases.shape
    rows = stiffness.shape[0]
    traces, ncell = trace_dofs.shape[0], cell_dof.shape[0]
    patches, comps = lax.axis_size("patch"), lax.axis_size("comp")
    groups = dofs // GROUP
    entries = rows * 4
    vm = pl.BlockSpec(memory_space=pltpu.VMEM)
    hbm = pl.BlockSpec(memory_space=pltpu.HBM)
    field = jax.ShapeDtypeStruct((cases, dofs), F32)
    x_size = patches // z_size
    stages = comps + x_size + z_size

    def sums(tall):
        return [
            pltpu.VMEM((3, tall, 128), F32),
            pltpu.VMEM((comps - 1, tall, 128), F32),
            pltpu.VMEM((x_size - 1, tall, 128), F32),
            pltpu.VMEM((z_size - 1, tall, 128), F32),
        ]

    right_side, parts, weights = pl.pallas_call(
        functools.partial(kernel, z_size),
        out_shape=(
            field, jax.ShapeDtypeStruct((6 * cases, dofs), BF16), jax.ShapeDtypeStruct((2 * cases, 128), BF16)),
        in_specs=[hbm] * 9,
        out_specs=(vm, vm, vm),
        scratch_shapes=[
            pltpu.VMEM((cases, dofs), F32),
            pltpu.VMEM((1, dofs), F32),
            pltpu.VMEM(stiffness.shape, F32),
            pltpu.VMEM((4, rows), I32),
            pltpu.SMEM((4, rows), I32),
            pltpu.VMEM((1, traces), I32),
            pltpu.VMEM((1, traces), F32),
            pltpu.VMEM((cases, ncell), F32),
            pltpu.VMEM((1, ncell), I32),
            pltpu.VMEM((1, ncell), I32),
            pltpu.VMEM((rows, 128, 256), BF16),
            pltpu.VMEM((patches, 17, 128), F32),
            pltpu.VMEM((patches, 17, 128), F32),
            pltpu.VMEM((4, 128), I32),
            pltpu.VMEM((2, GROUP), I32),
            pltpu.VMEM((2, GROUP), F32),
            pltpu.SMEM((2, GROUP), I32),
            pltpu.SMEM((2, GROUP), F32),
            pltpu.VMEM((GROUP, traces), BF16),
            pltpu.VMEM((2, cases, traces), F32),
            pltpu.VMEM((2, cases, traces), F32),
            pltpu.VMEM((1, traces), F32),
            pltpu.VMEM((1, traces), I32),
            pltpu.VMEM((traces, traces), BF16),
            pltpu.VMEM((cases, dofs), F32),
            pltpu.VMEM((cases, dofs), F32),
            pltpu.VMEM((2 * rows, 64, 128), BF16),
            pltpu.VMEM((64, rows * 128), BF16),
            pltpu.VMEM((entries, 16, 128), F32),
            pltpu.VMEM((entries, 16, 128), F32),
            pltpu.VMEM((cases, 128), F32),
            *sums(24),
            *sums(8),
            pltpu.SemaphoreType.DMA((12,)),
            pltpu.SemaphoreType.DMA((patches,)),
            pltpu.SemaphoreType.DMA((patches,)),
            pltpu.SemaphoreType.DMA((3,)),
            pltpu.SemaphoreType.DMA((3,)),
            pltpu.SemaphoreType.DMA((2 * stages,)),
            pltpu.SemaphoreType.DMA((2 * stages,)),
        ],
        compiler_params=pltpu.CompilerParams(
            collective_id=0, has_side_effects=True, vmem_limit_bytes=40 * 1024 * 1024),
    )(
        *(pltpu.with_memory_space_constraint(x, pltpu.HBM) for x in (
            load_cases, mass_diag.reshape(1, -1), stiffness, block_cols.T, trace_dofs.reshape(1, -1),
            penalty.reshape(1, -1), cell_partials, cell_owner.reshape(1, -1), cell_dof.reshape(1, -1)))
    )
    return pl.pallas_call(
        finish,
        out_shape=(field, field),
        in_specs=[vm, vm, vm],
        out_specs=(hbm, hbm),
        scratch_shapes=[
            pltpu.VMEM((cases, dofs), F32),
            pltpu.VMEM((cases, dofs), F32),
            pltpu.SemaphoreType.DMA((4, 2)),
        ],
        compiler_params=pltpu.CompilerParams(vmem_limit_bytes=8 * 1024 * 1024),
    )(weights, parts, right_side)


def solution(mesh):
    patches = mesh.shape["patch"]
    z_size = 8 if patches == 32 else patches // 2
    both = ("comp", "patch")
    return jax.shard_map(
        functools.partial(shards, z_size),
        mesh=mesh,
        in_specs=(
            P(None, both), P(both), P(both, None, None), P(both, None), P(both), P(both), P(None, both),
            P(both, None), P(both),
        ),
        out_specs=(P(None, both), P(None, both)),
        check_vma=False,
    )
```

```python
import functools

import jax
import jax.numpy as jnp
from jax import lax
from jax.experimental import pallas as pl
from jax.experimental.pallas import tpu as pltpu
from jax.sharding import PartitionSpec as P

CAP = 64
GROUP = 256
F32, BF16, I32 = jnp.float32, jnp.bfloat16, jnp.int32
NT = (((1,), (1,)), ((), ()))
NN = (((1,), (0,)), ((), ()))
MESH = pl.DeviceIdType.MESH


def mm(a, b, dims=NN):
    return lax.dot_general(a, b, dims, preferred_element_type=F32)


def split(x):
    hi = x.astype(BF16)
    return hi, (x - hi.astype(F32)).astype(BF16)


def split_rows(x):
    return jnp.concatenate(split(x), axis=0)


def iota(shape, dim):
    return lax.broadcasted_iota(I32, shape, dim)


def ones_where(mask):
    return jnp.where(mask, 1.0, 0.0)


def swap(x):
    return pltpu.roll(x, 64, 1)


def pack4(x, slot):
    band = iota((8, 128), 1) >> 5
    out = jnp.zeros((8, 128), F32)
    for g in range(4):
        out = jnp.where(band == g, pltpu.roll(x[8 * g:8 * g + 8], (32 * (g - slot)) % 128, 1), out)
    return out


def unpack4(x, slot):
    band = iota((8, 128), 1) >> 5
    return jnp.concatenate(
        [jnp.where(band == slot, pltpu.roll(x, (32 * (slot - g)) % 128, 1), 0.0) for g in range(4)], axis=0)


def eliminate(system, first, last):
    place = iota((64, 128), 0)
    for start in range(first, last, 8):
        wide = [jnp.broadcast_to(system[:, start + j:start + j + 1], (64, 128)) for j in range(8)]
        for j in range(8):
            k = start + j
            here = place == k
            inverse = 1.0 / wide[j][k:k + 1]
            factor = wide[j] * inverse
            row = system[k:k + 1]
            system = jnp.where(here, row * inverse, system - factor * row)
            for i in range(j + 1, 8):
                entry = wide[i][k:k + 1]
                wide[i] = jnp.where(here, entry * inverse, wide[i] - factor * entry)
    return system


def kernel(
    z_size, load_hbm, mass_hbm, stiff_hbm, cols_hbm, trace_hbm, pen_hbm, cells_hbm, owner_hbm,
    cdof_hbm, r_ref, s3, weights_ref,
    load, mass_ref, stiff, cols_ref, cols_smem, trace_ref, pen_ref, cells_ref, owner_ref, cdof_ref,
    kk, kt, send, recv, colp, csr_i, csr_f, csr_is, csr_fs, hot, own, part, pen_other, trace_other, twins,
    q_ref, t_ref, vab, ss, tp, run, fold, pay_a, rc_a, rx_a, rz_a, pay_b, rc_b, rx_b, rz_b,
    in_sem, a2a_send, a2a_recv, tr_send, tr_recv, red_send, red_recv,
):
    patches, comps = lax.axis_size("patch"), lax.axis_size("comp")
    me, mine = lax.axis_index("patch"), lax.axis_index("comp")
    cases, dofs = load.shape
    groups = dofs // GROUP
    ncell = cells_ref.shape[1]
    traces = trace_ref.shape[1]
    chunks = traces // GROUP
    rows = stiff.shape[0]
    entries = rows * 4
    spare = 64 - rows
    pairs = rows // 2
    left = iota((1, 128), 1) < 64
    left16 = iota((16, 128), 1) < 64
    left32 = iota((32, 128), 1) < 64

    get_stiff = pltpu.make_async_copy(stiff_hbm, stiff, in_sem.at[0])
    get_load = pltpu.make_async_copy(load_hbm, load, in_sem.at[1])
    small = [
        pltpu.make_async_copy(src, dst, in_sem.at[4 + i]) for i, (src, dst) in enumerate((
            (owner_hbm, owner_ref), (cdof_hbm, cdof_ref), (cells_hbm, cells_ref), (cols_hbm, cols_ref),
            (cols_hbm, cols_smem), (trace_hbm, trace_ref), (pen_hbm, pen_ref), (mass_hbm, mass_ref)))
    ]

    for copy in small:
        copy.start()
    barrier = pltpu.get_barrier_semaphore()

    for d in range(1, patches):
        pl.semaphore_signal(barrier, inc=1, device_id={"patch": lax.rem(me + d, patches)}, device_id_type=MESH)
    for d in range(1, comps):
        pl.semaphore_signal(barrier, inc=1, device_id={"comp": lax.rem(mine + d, comps)}, device_id_type=MESH)
    get_stiff.start()
    get_load.start()

    tri = ones_where(iota((ncell, ncell), 0) < iota((ncell, ncell), 1)).astype(BF16)
    for copy in small[0:3]:
        copy.wait()

    owner = owner_ref[...]
    hit = owner == iota((patches, ncell), 0)
    before = mm(ones_where(hit).astype(BF16), tri)
    pos = jnp.sum(jnp.where(hit, before, 0.0), axis=0, keepdims=True).astype(I32)
    slot = (owner & 3) * CAP + pos
    slot_hot = ones_where(iota((GROUP, ncell), 0) == slot).astype(BF16)
    cdof = cdof_ref[...]
    row16 = iota((16, ncell), 0)
    dof_rows = jnp.where(row16 == 0, cdof >> 8, jnp.where(row16 == 1, cdof & 255, 0)).astype(F32)
    cell_hi, cell_lo = split(cells_ref[...])
    cell_rows = jnp.concatenate([cell_hi, cell_lo, dof_rows.astype(BF16)], axis=0)
    masked = []
    for g in range(patches // 4):
        mask = jnp.broadcast_to(ones_where((owner >> 2) == g), (16, ncell)).astype(BF16)
        masked.append(cell_rows * jnp.concatenate([mask] * 5, axis=0))
    packed = mm(jnp.concatenate(masked, axis=0), slot_hot, NT)
    for g in range(patches // 4):
        values = packed[g * 80:g * 80 + 32] + packed[g * 80 + 32:g * 80 + 64]
        places = packed[g * 80 + 64:g * 80 + 72]
        for half in range(2):
            tile = values[:, half * 128:(half + 1) * 128]
            top, bottom = tile[0:16], tile[16:32]
            place = places[:, half * 128:(half + 1) * 128]
            place_hi, place_lo = place[0:1], place[1:2]
            even = g * 4 + half * 2
            send[even, 0:16] = jnp.where(left16, top, swap(bottom))
            send[even + 1, 0:16] = jnp.where(left16, swap(top), bottom)
            send[even, 16:17] = jnp.where(left, place_hi, swap(place_lo))
            send[even + 1, 16:17] = jnp.where(left, swap(place_hi), place_lo)
    recv[0] = send[me]

    for copy in small[3:]:
        copy.wait()

    pl.semaphore_wait(barrier, patches + comps - 2)

    other = lax.rem(me + patches // 2, patches)

    def cell_copy(d):
        to = lax.rem(me + d, patches)
        return pltpu.make_async_remote_copy(
            src_ref=send.at[to], dst_ref=recv.at[d], send_sem=a2a_send.at[d], recv_sem=a2a_recv.at[d],
            device_id={"patch": to}, device_id_type=MESH,
        )

    pen_copy = pltpu.make_async_remote_copy(
        src_ref=pen_ref, dst_ref=pen_other, send_sem=a2a_send.at[0], recv_sem=a2a_recv.at[0],
        device_id={"patch": other}, device_id_type=MESH,
    )
    other_copy = pltpu.make_async_remote_copy(
        src_ref=trace_ref, dst_ref=trace_other, send_sem=tr_send.at[2], recv_sem=tr_recv.at[2],
        device_id={"patch": other}, device_id_type=MESH,
    )
    x_size = patches // z_size
    pen_copy.start()
    other_copy.start()
    near_first = sorted(range(x_size), key=lambda x: min(x, x_size - x))
    for x in near_first:
        for z in sorted(range(z_size), key=lambda z: min(z, z_size - z)):
            if x or z:
                cell_copy(x * z_size + z).start()

    i0, i1 = iota((GROUP, GROUP), 0), iota((GROUP, GROUP), 1)
    colp[...] = jnp.full((4, 128), 255, I32)
    colp[:, 0:rows] = cols_ref[...]
    quad = colp[...]
    turned = pltpu.roll(quad, 64, 1)
    col = jnp.concatenate(
        [jnp.where(left, quad[0:1], turned[1:2]), jnp.where(left, quad[2:3], turned[3:4])], axis=1)
    col_of = jnp.transpose(jnp.broadcast_to(col, (GROUP, GROUP)))
    ahead = (col_of < col) | ((col_of == col) & (i0 < i1))
    rank = jnp.sum(jnp.where(ahead, 1, 0), axis=0, keepdims=True)
    at_rank = jnp.transpose(jnp.broadcast_to(rank, (GROUP, GROUP))) == i1
    order = jnp.sum(jnp.where(at_rank, i0, 0), axis=0, keepdims=True)
    ocol = jnp.sum(jnp.where(at_rank, col_of, 0), axis=0, keepdims=True)
    upto = jnp.sum(jnp.where(col_of <= i1, 1, 0), axis=0, keepdims=True)
    same = jnp.sum(jnp.where(col_of == i1, 1, 0), axis=0, keepdims=True)
    lane = iota((1, GROUP), 1)
    csr_i[0:1, :] = jnp.minimum((order & 63) * 4 + (order >> 6), entries - 1)
    csr_i[1:2, :] = jnp.clip(upto - 1, 0, entries - 1)
    csr_f[0:1, :] = ones_where((ocol == pltpu.roll(ocol, 1, 1)) & (lane > 0))
    csr_f[1:2, :] = ones_where(same > 0)
    put_i = pltpu.make_async_copy(csr_i, csr_is, in_sem.at[2])
    put_f = pltpu.make_async_copy(csr_f, csr_fs, in_sem.at[3])
    put_i.start()
    put_f.start()

    for c in range(chunks):
        lanes = slice(c * GROUP, (c + 1) * GROUP)
        hot[:, lanes] = ones_where(i0 == trace_ref[:, lanes] & 255).astype(BF16)

    get_stiff.wait()

    def halve(n, _):
        hi, lo = split(stiff[n])
        kk[n, 0:64] = hi
        kk[n, 64:128] = lo
        return 0

    lax.fori_loop(0, rows, halve, 0)
    for n in range(rows):
        kt[n] = jnp.transpose(kk[n])
    fold[...] = jnp.zeros((128, 128), F32)
    put_i.wait()
    put_f.wait()

    pen_copy.wait_recv()
    other_copy.wait_recv()
    for c in range(chunks):
        lanes = slice(c * GROUP, (c + 1) * GROUP)
        mine_of = jnp.transpose(jnp.broadcast_to(trace_ref[:, lanes], (GROUP, GROUP)))
        other_of = jnp.transpose(jnp.broadcast_to(trace_other[:, lanes], (GROUP, GROUP)))
        for e in range(chunks):
            across = slice(e * GROUP, (e + 1) * GROUP)
            twins[lanes, across] = (
                ones_where(mine_of == trace_ref[:, across]) + ones_where(other_of == trace_other[:, across])
            ).astype(BF16)
    get_load.wait()

    def masked_groups(data, high):
        parts = []
        for h in range(groups):
            mask = jnp.broadcast_to(ones_where(high == h), (16, data.shape[1])).astype(BF16)
            parts.append(data * jnp.concatenate([mask] * 4, axis=0))
        return jnp.concatenate(parts, axis=0)

    def add_groups(total, base_ref, out_ref):
        for h in range(groups):
            lanes = slice(h * GROUP, (h + 1) * GROUP)
            out_ref[:, lanes] = base_ref[:, lanes] + total[h * 64:h * 64 + 32] + total[h * 64 + 32:h * 64 + 64]

    def arrive(d, _):
        cell_copy(d).wait_recv()
        return 0

    def place(steps, base_ref):
        for x in steps:
            lax.fori_loop(max(1, x * z_size), (x + 1) * z_size, arrive, 0)
        data, highs, lows = [], [], []
        for x in steps:
            for d in range(x * z_size, (x + 1) * z_size, 2):
                a, b = recv[d], recv[d + 1]
                at, bt, ap, bp = a[0:16], b[0:16], a[16:17], b[16:17]
                data.append(split_rows(jnp.concatenate(
                    [jnp.where(left16, at, swap(bt)), jnp.where(left16, swap(at), bt)], axis=0)))
                highs.append(jnp.where(left, ap, swap(bp)).astype(I32))
                lows.append(jnp.where(left, swap(ap), bp).astype(I32))
        rows_of = iota((GROUP, 128), 0)
        low_hot = jnp.concatenate([ones_where(rows_of == low).astype(BF16) for low in lows], axis=1)
        data = masked_groups(jnp.concatenate(data, axis=1), jnp.concatenate(highs, axis=1))
        add_groups(mm(data, low_hot, NT), base_ref, r_ref)

    place(near_first[:x_size // 2], load)
    place(near_first[x_size // 2:], r_ref)

    def trace_copy(turn):
        return pltpu.make_async_remote_copy(
            src_ref=own.at[turn], dst_ref=part.at[turn], send_sem=tr_send.at[turn], recv_sem=tr_recv.at[turn],
            device_id={"patch": other}, device_id_type=MESH,
        )

    def halves_of(v_ref, base):
        for h in range(groups):
            lanes = slice(h * GROUP, (h + 1) * GROUP)
            s3[base:base + 64, lanes] = split_rows(v_ref[:, lanes])

    def send_trace(turn, base):
        stacked = jnp.concatenate([s3[base:base + 64, h * GROUP:(h + 1) * GROUP] for h in range(groups)], axis=0)
        for c in range(chunks):
            lanes = slice(c * GROUP, (c + 1) * GROUP)
            picked = mm(stacked, hot[:, lanes])
            high = trace_ref[:, lanes] >> 8
            total = jnp.zeros((32, GROUP), F32)
            for h in range(groups):
                total = jnp.where(high == h, picked[h * 64:h * 64 + 32] + picked[h * 64 + 32:h * 64 + 64], total)
            own[turn, :, lanes] = total
        trace_copy(turn).start()

    def strains(v_ref):
        for i in range(pairs):
            tile = v_ref[:, i * 128:(i + 1) * 128]
            turned = swap(tile)
            vab[4 * i] = split_rows(jnp.where(left32, tile, 0.0))
            vab[4 * i + 1] = split_rows(jnp.where(left32, 0.0, turned))
            vab[4 * i + 2] = split_rows(jnp.where(left32, turned, 0.0))
            vab[4 * i + 3] = split_rows(jnp.where(left32, 0.0, tile))

        for n in range(rows):
            c0, c1, c2, c3 = (cols_smem[k, n] for k in range(4))
            x = jnp.concatenate(
                [vab[2 * c0] + vab[2 * c1 + 1], vab[2 * c2] + vab[2 * c3 + 1]], axis=1)
            o = mm(x, kt[n])
            o = o[0:32] + o[32:64]
            ss[:, n * 128:(n + 1) * 128] = split_rows(o + swap(o))

    def forces():
        for n in range(rows):
            o = mm(ss[:, n * 128:(n + 1) * 128], kk[n])
            o = o[0:32] + o[32:64]
            for half in range(2):
                tile = o[:, half * 128:(half + 1) * 128]
                top, bottom = tile[0:16], tile[16:32]
                tp[n * 4 + 2 * half] = jnp.where(left16, top, swap(bottom))
                tp[n * 4 + 2 * half + 1] = jnp.where(left16, swap(top), bottom)

    def gather_forces(v_ref, out_ref):
        def add_up(step, total):
            for u in range(8):
                i = step * 8 + u
                total = total * csr_fs[0, i] + tp[csr_is[0, i]]
                run[i] = total
            return total

        lax.fori_loop(0, entries // 8, add_up, jnp.zeros((16, 128), F32))
        for i in range(pairs):
            lanes = slice(i * 128, (i + 1) * 128)
            a = run[csr_is[1, 2 * i]] * csr_fs[1, 2 * i]
            b = run[csr_is[1, 2 * i + 1]] * csr_fs[1, 2 * i + 1]
            tile = jnp.concatenate(
                [jnp.where(left16, a, swap(b)), jnp.where(left16, swap(a), b)], axis=0)
            out_ref[:, lanes] = tile + mass_ref[:, lanes] * v_ref[:, lanes]

    def add_jump(jump, out_ref):
        add_groups(mm(masked_groups(jump, trace_ref[...] >> 8), hot[...], NT), out_ref, out_ref)

    sent = []

    def stage(pay, index, slots, count, place, base):
        copies = []
        for j in range(1, count):
            copies.append(pltpu.make_async_remote_copy(
                src_ref=pay.at[index], dst_ref=slots.at[j - 1], send_sem=red_send.at[base + j],
                recv_sem=red_recv.at[base + j], device_id=place(j), device_id_type=MESH))
            copies[-1].start()
        sent.extend(copies)

        def finish():
            total = pay[index]
            for j, copy in enumerate(copies):
                copy.wait_recv()
                total += slots[j]
            return total

        return finish

    z_first = (me // z_size) * z_size
    span = comps + x_size + z_size

    def along_comp(j):
        return {"comp": lax.rem(mine + j, comps)}

    def along_x(j):
        return {"patch": lax.rem(me + j * z_size, patches)}

    def along_z(j):
        return {"patch": z_first + lax.rem(lax.rem(me, z_size) + j, z_size)}

    weight = pen_ref[...] * pen_other[...]
    halves_of(r_ref, 0)
    send_trace(0, 0)
    strains(r_ref)
    forces()
    gather_forces(r_ref, q_ref)
    halves_of(q_ref, 64)
    send_trace(1, 64)
    o = mm(s3[0:64], s3[0:64], NT)
    fold[32:64, 0:64] = o[0:32] + o[32:64]
    trace_copy(0).wait_recv()
    first_jump = split_rows(weight * (own[0] - part[0]))
    add_jump(first_jump, q_ref)
    halves_of(q_ref, 64)

    o = mm(s3[0:128], s3[64:128], NT)
    fold[64:96, 0:64] = o[0:32] + o[32:64]
    fold[96:128, 0:64] = o[64:96] + o[96:128]
    early = fold[32:128]
    early = early + pltpu.roll(early, 96, 1)
    pay_a[0] = jnp.concatenate([pack4(early[32 * i:32 * i + 32], 0) for i in range(3)], axis=0)
    a_z = stage(pay_a, 0, rz_a, z_size, along_z, comps + x_size)
    strains(q_ref)

    strain = ss[...]
    energy = mm(strain, strain, NT) * 0.5 + mm(split_rows(mass_ref[...] * q_ref[...]), s3[64:128], NT)
    turn = mm(first_jump, twins[...])
    trace_copy(1).wait_recv()
    jump = own[1] - part[1] + turn[0:32] + turn[32:64]
    energy += mm(split_rows(0.5 * weight * jump), split_rows(jump), NT)
    fold[0:32, 0:64] = energy[0:32] + energy[32:64]
    third = fold[0:32]
    third = third + pltpu.roll(third, 96, 1)
    pay_b[0] = pack4(third, 0)
    b_comp = stage(pay_b, 0, rc_b, comps, along_comp, span)

    forces()
    gather_forces(q_ref, t_ref)
    add_jump(split_rows(weight * jump), t_ref)
    halves_of(t_ref, 128)
    pay_a[1] = a_z()
    a_x = stage(pay_a, 1, rx_a, x_size, along_x, comps)
    pay_b[1] = b_comp()
    b_x = stage(pay_b, 1, rx_b, x_size, along_x, span + comps)
    pay_a[2] = a_x()
    a_comp = stage(pay_a, 2, rc_a, comps, along_comp, 0)
    pay_b[2] = b_x()
    b_z = stage(pay_b, 2, rz_b, z_size, along_z, span + comps + x_size)

    def drain(d, _):
        cell_copy(d).wait_send()
        return 0

    lax.fori_loop(1, patches, drain, 0)
    pen_copy.wait_send()
    other_copy.wait_send()
    trace_copy(0).wait_send()
    trace_copy(1).wait_send()

    total = a_comp()
    m0, m1, m2 = total[0:8], total[8:16], total[16:24]
    upper = unpack4(m1, 0) + unpack4(m2, 1) + unpack4(m0, 2)
    lower = unpack4(m2, 0) + unpack4(m1, 2)
    system = eliminate(jnp.concatenate([upper, lower], axis=0), 0, 32)
    lower = system[32:64] + unpack4(b_z(), 1)
    system = eliminate(jnp.concatenate([system[0:32], lower], axis=0), 32, 64)
    mixed = jnp.concatenate([system[0:32], system[0:32], system[32:64], system[32:64]], axis=0)
    weights_ref[...] = split_rows(jnp.transpose(mixed)[64:96])
    for copy in sent:
        copy.wait_send()


def finish(weights_ref, s3, r_ref, sol_hbm, res_hbm, sol, res, sems):
    weights = weights_ref[...]
    dofs = sol.shape[1]
    width = dofs // 4
    copies = []
    for part in range(4):
        for h in range(width // GROUP):
            lanes = slice(part * width + h * GROUP, part * width + (h + 1) * GROUP)
            o = mm(weights, s3[0:128, lanes])
            sol[:, lanes] = o[0:32] + o[32:64]
            o = mm(weights, s3[64:192, lanes])
            res[:, lanes] = r_ref[:, lanes] - (o[0:32] + o[32:64])
        lanes = pl.ds(part * width, width)
        for i, (src, dst) in enumerate(((sol, sol_hbm), (res, res_hbm))):
            copies.append(pltpu.make_async_copy(src.at[:, lanes], dst.at[:, lanes], sems.at[part, i]))
            copies[-1].start()
    for copy in copies:
        copy.wait()


def shards(z_size, load_cases, mass_diag, stiffness, block_cols, trace_dofs, penalty, cell_partials, cell_owner, cell_dof):
    cases, dofs = load_cases.shape
    rows = stiffness.shape[0]
    traces, ncell = trace_dofs.shape[0], cell_dof.shape[0]
    patches, comps = lax.axis_size("patch"), lax.axis_size("comp")
    groups = dofs // GROUP
    entries = rows * 4
    vm = pl.BlockSpec(memory_space=pltpu.VMEM)
    hbm = pl.BlockSpec(memory_space=pltpu.HBM)
    field = jax.ShapeDtypeStruct((cases, dofs), F32)
    x_size = patches // z_size
    stages = comps + x_size + z_size

    def sums(tall):
        return [
            pltpu.VMEM((3, tall, 128), F32),
            pltpu.VMEM((comps - 1, tall, 128), F32),
            pltpu.VMEM((x_size - 1, tall, 128), F32),
            pltpu.VMEM((z_size - 1, tall, 128), F32),
        ]

    right_side, parts, weights = pl.pallas_call(
        functools.partial(kernel, z_size),
        out_shape=(
            field, jax.ShapeDtypeStruct((6 * cases, dofs), BF16), jax.ShapeDtypeStruct((2 * cases, 128), BF16)),
        in_specs=[hbm] * 9,
        out_specs=(vm, vm, vm),
        scratch_shapes=[
            pltpu.VMEM((cases, dofs), F32),
            pltpu.VMEM((1, dofs), F32),
            pltpu.VMEM(stiffness.shape, F32),
            pltpu.VMEM((4, rows), I32),
            pltpu.SMEM((4, rows), I32),
            pltpu.VMEM((1, traces), I32),
            pltpu.VMEM((1, traces), F32),
            pltpu.VMEM((cases, ncell), F32),
            pltpu.VMEM((1, ncell), I32),
            pltpu.VMEM((1, ncell), I32),
            pltpu.VMEM((rows, 128, 256), BF16),
            pltpu.VMEM((rows, 256, 128), BF16),
            pltpu.VMEM((patches, 17, 128), F32),
            pltpu.VMEM((patches, 17, 128), F32),
            pltpu.VMEM((4, 128), I32),
            pltpu.VMEM((2, GROUP), I32),
            pltpu.VMEM((2, GROUP), F32),
            pltpu.SMEM((2, GROUP), I32),
            pltpu.SMEM((2, GROUP), F32),
            pltpu.VMEM((GROUP, traces), BF16),
            pltpu.VMEM((2, cases, traces), F32),
            pltpu.VMEM((2, cases, traces), F32),
            pltpu.VMEM((1, traces), F32),
            pltpu.VMEM((1, traces), I32),
            pltpu.VMEM((traces, traces), BF16),
            pltpu.VMEM((cases, dofs), F32),
            pltpu.VMEM((cases, dofs), F32),
            pltpu.VMEM((2 * rows, 64, 128), BF16),
            pltpu.VMEM((64, rows * 128), BF16),
            pltpu.VMEM((entries, 16, 128), F32),
            pltpu.VMEM((entries, 16, 128), F32),
            pltpu.VMEM((4 * cases, 128), F32),
            *sums(24),
            *sums(8),
            pltpu.SemaphoreType.DMA((12,)),
            pltpu.SemaphoreType.DMA((patches,)),
            pltpu.SemaphoreType.DMA((patches,)),
            pltpu.SemaphoreType.DMA((3,)),
            pltpu.SemaphoreType.DMA((3,)),
            pltpu.SemaphoreType.DMA((2 * stages,)),
            pltpu.SemaphoreType.DMA((2 * stages,)),
        ],
        compiler_params=pltpu.CompilerParams(
            collective_id=0, has_side_effects=True, vmem_limit_bytes=40 * 1024 * 1024),
    )(
        *(pltpu.with_memory_space_constraint(x, pltpu.HBM) for x in (
            load_cases, mass_diag.reshape(1, -1), stiffness, block_cols.T, trace_dofs.reshape(1, -1),
            penalty.reshape(1, -1), cell_partials, cell_owner.reshape(1, -1), cell_dof.reshape(1, -1)))
    )
    return pl.pallas_call(
        finish,
        out_shape=(field, field),
        in_specs=[vm, vm, vm],
        out_specs=(hbm, hbm),
        scratch_shapes=[
            pltpu.VMEM((cases, dofs), F32),
            pltpu.VMEM((cases, dofs), F32),
            pltpu.SemaphoreType.DMA((4, 2)),
        ],
        compiler_params=pltpu.CompilerParams(vmem_limit_bytes=8 * 1024 * 1024),
    )(weights, parts, right_side)


def solution(mesh):
    patches = mesh.shape["patch"]
    z_size = 8 if patches == 32 else patches // 2
    both = ("comp", "patch")
    return jax.shard_map(
        functools.partial(shards, z_size),
        mesh=mesh,
        in_specs=(
            P(None, both), P(both), P(both, None, None), P(both, None), P(both), P(both), P(None, both),
            P(both, None), P(both),
        ),
        out_specs=(P(None, both), P(None, both)),
        check_vma=False,
    )
```

```python
import functools

import jax
import jax.numpy as jnp
from jax import lax
from jax.experimental import pallas as pl
from jax.experimental.pallas import tpu as pltpu
from jax.sharding import PartitionSpec as P

CAP = 64
GROUP = 256
F32, BF16, I32 = jnp.float32, jnp.bfloat16, jnp.int32
NT = (((1,), (1,)), ((), ()))
NN = (((1,), (0,)), ((), ()))
MESH = pl.DeviceIdType.MESH


def mm(a, b, dims=NN):
    return lax.dot_general(a, b, dims, preferred_element_type=F32)


def split(x):
    hi = x.astype(BF16)
    return hi, (x - hi.astype(F32)).astype(BF16)


def split_rows(x):
    return jnp.concatenate(split(x), axis=0)


def iota(shape, dim):
    return lax.broadcasted_iota(I32, shape, dim)


def ones_where(mask):
    return jnp.where(mask, 1.0, 0.0)


def swap(x):
    return pltpu.roll(x, 64, 1)


def pack4(x, slot):
    band = iota((8, 128), 1) >> 5
    out = jnp.zeros((8, 128), F32)
    for g in range(4):
        out = jnp.where(band == g, pltpu.roll(x[8 * g:8 * g + 8], (32 * (g - slot)) % 128, 1), out)
    return out


def unpack4(x, slot):
    band = iota((8, 128), 1) >> 5
    return jnp.concatenate(
        [jnp.where(band == slot, pltpu.roll(x, (32 * (slot - g)) % 128, 1), 0.0) for g in range(4)], axis=0)


def eliminate(system, first, last):
    place = iota((64, 128), 0)
    for start in range(first, last, 8):
        wide = [jnp.broadcast_to(system[:, start + j:start + j + 1], (64, 128)) for j in range(8)]
        for j in range(8):
            k = start + j
            here = place == k
            inverse = 1.0 / wide[j][k:k + 1]
            factor = wide[j] * inverse
            row = system[k:k + 1]
            system = jnp.where(here, row * inverse, system - factor * row)
            for i in range(j + 1, 8):
                entry = wide[i][k:k + 1]
                wide[i] = jnp.where(here, entry * inverse, wide[i] - factor * entry)
    return system


def kernel(
    z_size, load_hbm, mass_hbm, stiff_hbm, cols_hbm, trace_hbm, pen_hbm, cells_hbm, owner_hbm,
    cdof_hbm, r_ref, s3, weights_ref,
    load, mass_ref, stiff, cols_ref, cols_smem, trace_ref, pen_ref, cells_ref, owner_ref, cdof_ref,
    kk, kt, send, recv, colp, csr_i, csr_f, csr_is, csr_fs, hot, own, part, pen_other, trace_other, twins,
    q_ref, t_ref, vab, ss, tp, run, fold, pay_a, rc_a, rx_a, rz_a, pay_b, rc_b, rx_b, rz_b, pay_m, rc_m, rx_m, rz_m,
    in_sem, a2a_send, a2a_recv, tr_send, tr_recv, red_send, red_recv,
):
    patches, comps = lax.axis_size("patch"), lax.axis_size("comp")
    me, mine = lax.axis_index("patch"), lax.axis_index("comp")
    cases, dofs = load.shape
    groups = dofs // GROUP
    ncell = cells_ref.shape[1]
    traces = trace_ref.shape[1]
    chunks = traces // GROUP
    rows = stiff.shape[0]
    entries = rows * 4
    spare = 64 - rows
    pairs = rows // 2
    left = iota((1, 128), 1) < 64
    left16 = iota((16, 128), 1) < 64
    left32 = iota((32, 128), 1) < 64

    get_stiff = pltpu.make_async_copy(stiff_hbm, stiff, in_sem.at[0])
    get_load = pltpu.make_async_copy(load_hbm, load, in_sem.at[1])
    small = [
        pltpu.make_async_copy(src, dst, in_sem.at[4 + i]) for i, (src, dst) in enumerate((
            (owner_hbm, owner_ref), (cdof_hbm, cdof_ref), (cells_hbm, cells_ref), (cols_hbm, cols_ref),
            (cols_hbm, cols_smem), (trace_hbm, trace_ref), (pen_hbm, pen_ref), (mass_hbm, mass_ref)))
    ]

    for copy in small:
        copy.start()
    barrier = pltpu.get_barrier_semaphore()

    for d in range(1, patches):
        pl.semaphore_signal(barrier, inc=1, device_id={"patch": lax.rem(me + d, patches)}, device_id_type=MESH)
    for d in range(1, comps):
        pl.semaphore_signal(barrier, inc=1, device_id={"comp": lax.rem(mine + d, comps)}, device_id_type=MESH)
    get_stiff.start()
    get_load.start()

    tri = ones_where(iota((ncell, ncell), 0) < iota((ncell, ncell), 1)).astype(BF16)
    for copy in small[0:3]:
        copy.wait()

    owner = owner_ref[...]
    hit = owner == iota((patches, ncell), 0)
    before = mm(ones_where(hit).astype(BF16), tri)
    pos = jnp.sum(jnp.where(hit, before, 0.0), axis=0, keepdims=True).astype(I32)
    slot = (owner & 3) * CAP + pos
    slot_hot = ones_where(iota((GROUP, ncell), 0) == slot).astype(BF16)
    cdof = cdof_ref[...]
    row16 = iota((16, ncell), 0)
    dof_rows = jnp.where(row16 == 0, cdof >> 8, jnp.where(row16 == 1, cdof & 255, 0)).astype(F32)
    cell_hi, cell_lo = split(cells_ref[...])
    cell_rows = jnp.concatenate([cell_hi, cell_lo, dof_rows.astype(BF16)], axis=0)
    masked = []
    for g in range(patches // 4):
        mask = jnp.broadcast_to(ones_where((owner >> 2) == g), (16, ncell)).astype(BF16)
        masked.append(cell_rows * jnp.concatenate([mask] * 5, axis=0))
    packed = mm(jnp.concatenate(masked, axis=0), slot_hot, NT)
    for g in range(patches // 4):
        values = packed[g * 80:g * 80 + 32] + packed[g * 80 + 32:g * 80 + 64]
        places = packed[g * 80 + 64:g * 80 + 72]
        for half in range(2):
            tile = values[:, half * 128:(half + 1) * 128]
            top, bottom = tile[0:16], tile[16:32]
            place = places[:, half * 128:(half + 1) * 128]
            place_hi, place_lo = place[0:1], place[1:2]
            even = g * 4 + half * 2
            send[even, 0:16] = jnp.where(left16, top, swap(bottom))
            send[even + 1, 0:16] = jnp.where(left16, swap(top), bottom)
            send[even, 16:17] = jnp.where(left, place_hi, swap(place_lo))
            send[even + 1, 16:17] = jnp.where(left, swap(place_hi), place_lo)
    recv[0] = send[me]

    for copy in small[3:]:
        copy.wait()

    pl.semaphore_wait(barrier, patches + comps - 2)

    other = lax.rem(me + patches // 2, patches)

    def cell_copy(d):
        to = lax.rem(me + d, patches)
        return pltpu.make_async_remote_copy(
            src_ref=send.at[to], dst_ref=recv.at[d], send_sem=a2a_send.at[d], recv_sem=a2a_recv.at[d],
            device_id={"patch": to}, device_id_type=MESH,
        )

    pen_copy = pltpu.make_async_remote_copy(
        src_ref=pen_ref, dst_ref=pen_other, send_sem=a2a_send.at[0], recv_sem=a2a_recv.at[0],
        device_id={"patch": other}, device_id_type=MESH,
    )
    other_copy = pltpu.make_async_remote_copy(
        src_ref=trace_ref, dst_ref=trace_other, send_sem=tr_send.at[2, 0], recv_sem=tr_recv.at[2, 0],
        device_id={"patch": other}, device_id_type=MESH,
    )
    x_size = patches // z_size
    pen_copy.start()
    other_copy.start()
    far_first = [x_size // 2] + list(range(1, x_size // 2)) + list(range(x_size // 2 + 1, x_size)) + [0]
    for x in far_first:
        for z in range(z_size):
            if x or z:
                cell_copy(x * z_size + z).start()

    i0, i1 = iota((GROUP, GROUP), 0), iota((GROUP, GROUP), 1)
    colp[...] = jnp.full((4, 128), 255, I32)
    colp[:, 0:rows] = cols_ref[...]
    quad = colp[...]
    turned = pltpu.roll(quad, 64, 1)
    col = jnp.concatenate(
        [jnp.where(left, quad[0:1], turned[1:2]), jnp.where(left, quad[2:3], turned[3:4])], axis=1)
    col_of = jnp.transpose(jnp.broadcast_to(col, (GROUP, GROUP)))
    ahead = (col_of < col) | ((col_of == col) & (i0 < i1))
    rank = jnp.sum(jnp.where(ahead, 1, 0), axis=0, keepdims=True)
    at_rank = jnp.transpose(jnp.broadcast_to(rank, (GROUP, GROUP))) == i1
    order = jnp.sum(jnp.where(at_rank, i0, 0), axis=0, keepdims=True)
    ocol = jnp.sum(jnp.where(at_rank, col_of, 0), axis=0, keepdims=True)
    upto = jnp.sum(jnp.where(col_of <= i1, 1, 0), axis=0, keepdims=True)
    same = jnp.sum(jnp.where(col_of == i1, 1, 0), axis=0, keepdims=True)
    lane = iota((1, GROUP), 1)
    csr_i[0:1, :] = jnp.minimum((order & 63) * 4 + (order >> 6), entries - 1)
    csr_i[1:2, :] = jnp.clip(upto - 1, 0, entries - 1)
    csr_f[0:1, :] = ones_where((ocol == pltpu.roll(ocol, 1, 1)) & (lane > 0))
    csr_f[1:2, :] = ones_where(same > 0)
    put_i = pltpu.make_async_copy(csr_i, csr_is, in_sem.at[2])
    put_f = pltpu.make_async_copy(csr_f, csr_fs, in_sem.at[3])
    put_i.start()
    put_f.start()

    for c in range(chunks):
        lanes = slice(c * GROUP, (c + 1) * GROUP)
        hot[:, lanes] = ones_where(i0 == trace_ref[:, lanes] & 255).astype(BF16)

    get_stiff.wait()

    def halve(n, _):
        hi, lo = split(stiff[n])
        kk[n, 0:64] = hi
        kk[n, 64:128] = lo
        return 0

    lax.fori_loop(0, rows, halve, 0)
    for n in range(rows):
        kt[n] = jnp.transpose(kk[n])
    fold[...] = jnp.zeros((128, 128), F32)
    put_i.wait()
    put_f.wait()

    pen_copy.wait_recv()
    other_copy.wait_recv()
    for c in range(chunks):
        lanes = slice(c * GROUP, (c + 1) * GROUP)
        mine_of = jnp.transpose(jnp.broadcast_to(trace_ref[:, lanes], (GROUP, GROUP)))
        other_of = jnp.transpose(jnp.broadcast_to(trace_other[:, lanes], (GROUP, GROUP)))
        for e in range(chunks):
            across = slice(e * GROUP, (e + 1) * GROUP)
            twins[lanes, across] = (
                ones_where(mine_of == trace_ref[:, across]) + ones_where(other_of == trace_other[:, across])
            ).astype(BF16)
    get_load.wait()

    def masked_groups(data, high):
        parts = []
        for h in range(groups):
            mask = jnp.broadcast_to(ones_where(high == h), (16, data.shape[1])).astype(BF16)
            parts.append(data * jnp.concatenate([mask] * 4, axis=0))
        return jnp.concatenate(parts, axis=0)

    def add_groups(total, base_ref, out_ref):
        for h in range(groups):
            lanes = slice(h * GROUP, (h + 1) * GROUP)
            out_ref[:, lanes] = base_ref[:, lanes] + total[h * 64:h * 64 + 32] + total[h * 64 + 32:h * 64 + 64]

    def arrive(d, _):
        cell_copy(d).wait_recv()
        return 0

    def place(steps, base_ref):
        for x in steps:
            lax.fori_loop(max(1, x * z_size), (x + 1) * z_size, arrive, 0)
        data, highs, lows = [], [], []
        for x in steps:
            for d in range(x * z_size, (x + 1) * z_size, 2):
                a, b = recv[d], recv[d + 1]
                at, bt, ap, bp = a[0:16], b[0:16], a[16:17], b[16:17]
                data.append(split_rows(jnp.concatenate(
                    [jnp.where(left16, at, swap(bt)), jnp.where(left16, swap(at), bt)], axis=0)))
                highs.append(jnp.where(left, ap, swap(bp)).astype(I32))
                lows.append(jnp.where(left, swap(ap), bp).astype(I32))
        rows_of = iota((GROUP, 128), 0)
        low_hot = jnp.concatenate([ones_where(rows_of == low).astype(BF16) for low in lows], axis=1)
        data = masked_groups(jnp.concatenate(data, axis=1), jnp.concatenate(highs, axis=1))
        add_groups(mm(data, low_hot, NT), base_ref, r_ref)

    place(far_first[:x_size // 2], load)
    place(far_first[x_size // 2:], r_ref)

    def trace_copy(turn, half):
        lanes = pl.ds(half * (traces // 2), traces // 2)
        return pltpu.make_async_remote_copy(
            src_ref=own.at[turn, :, lanes], dst_ref=part.at[turn, :, lanes], send_sem=tr_send.at[turn, half],
            recv_sem=tr_recv.at[turn, half], device_id={"patch": other}, device_id_type=MESH,
        )

    def halves_of(v_ref, base):
        for h in range(groups):
            lanes = slice(h * GROUP, (h + 1) * GROUP)
            s3[base:base + 64, lanes] = split_rows(v_ref[:, lanes])

    def send_trace(turn, base):
        stacked = jnp.concatenate([s3[base:base + 64, h * GROUP:(h + 1) * GROUP] for h in range(groups)], axis=0)
        for c in range(chunks):
            lanes = slice(c * GROUP, (c + 1) * GROUP)
            picked = mm(stacked, hot[:, lanes])
            high = trace_ref[:, lanes] >> 8
            total = jnp.zeros((32, GROUP), F32)
            for h in range(groups):
                total = jnp.where(high == h, picked[h * 64:h * 64 + 32] + picked[h * 64 + 32:h * 64 + 64], total)
            own[turn, :, lanes] = total
            if turn == 0 and c + 1 == chunks // 2:
                trace_copy(turn, 0).start()
        if turn == 1:
            trace_copy(turn, 0).start()
        trace_copy(turn, 1).start()

    def strains(v_ref):
        for i in range(pairs):
            tile = v_ref[:, i * 128:(i + 1) * 128]
            turned = swap(tile)
            vab[4 * i] = split_rows(jnp.where(left32, tile, 0.0))
            vab[4 * i + 1] = split_rows(jnp.where(left32, 0.0, turned))
            vab[4 * i + 2] = split_rows(jnp.where(left32, turned, 0.0))
            vab[4 * i + 3] = split_rows(jnp.where(left32, 0.0, tile))

        for n in range(rows):
            c0, c1, c2, c3 = (cols_smem[k, n] for k in range(4))
            x = jnp.concatenate(
                [vab[2 * c0] + vab[2 * c1 + 1], vab[2 * c2] + vab[2 * c3 + 1]], axis=1)
            o = mm(x, kt[n])
            o = o[0:32] + o[32:64]
            ss[:, n * 128:(n + 1) * 128] = split_rows(o + swap(o))

    def forces():
        for n in range(rows):
            o = mm(ss[:, n * 128:(n + 1) * 128], kk[n])
            o = o[0:32] + o[32:64]
            for half in range(2):
                tile = o[:, half * 128:(half + 1) * 128]
                top, bottom = tile[0:16], tile[16:32]
                tp[n * 4 + 2 * half] = jnp.where(left16, top, swap(bottom))
                tp[n * 4 + 2 * half + 1] = jnp.where(left16, swap(top), bottom)

    def gather_forces(v_ref, out_ref):
        def add_up(step, total):
            for u in range(8):
                i = step * 8 + u
                total = total * csr_fs[0, i] + tp[csr_is[0, i]]
                run[i] = total
            return total

        lax.fori_loop(0, entries // 8, add_up, jnp.zeros((16, 128), F32))
        for i in range(pairs):
            lanes = slice(i * 128, (i + 1) * 128)
            a = run[csr_is[1, 2 * i]] * csr_fs[1, 2 * i]
            b = run[csr_is[1, 2 * i + 1]] * csr_fs[1, 2 * i + 1]
            tile = jnp.concatenate(
                [jnp.where(left16, a, swap(b)), jnp.where(left16, swap(a), b)], axis=0)
            out_ref[:, lanes] = tile + mass_ref[:, lanes] * v_ref[:, lanes]

    def add_jump(jump, out_ref):
        add_groups(mm(masked_groups(jump, trace_ref[...] >> 8), hot[...], NT), out_ref, out_ref)

    sent = []

    def stage(pay, index, slots, count, place, base):
        copies = []
        for j in range(1, count):
            copies.append(pltpu.make_async_remote_copy(
                src_ref=pay.at[index], dst_ref=slots.at[j - 1], send_sem=red_send.at[base + j],
                recv_sem=red_recv.at[base + j], device_id=place(j), device_id_type=MESH))
            copies[-1].start()
        sent.extend(copies)

        def finish():
            total = pay[index]
            for j, copy in enumerate(copies):
                copy.wait_recv()
                total += slots[j]
            return total

        return finish

    z_first = (me // z_size) * z_size
    span = comps + x_size + z_size

    def along_comp(j):
        return {"comp": lax.rem(mine + j, comps)}

    def along_x(j):
        return {"patch": lax.rem(me + j * z_size, patches)}

    def along_z(j):
        return {"patch": z_first + lax.rem(lax.rem(me, z_size) + j, z_size)}

    weight = pen_ref[...] * pen_other[...]
    halves_of(r_ref, 0)
    send_trace(0, 0)
    strains(r_ref)
    forces()
    gather_forces(r_ref, q_ref)
    halves_of(q_ref, 64)
    send_trace(1, 64)
    o = mm(s3[0:64], s3[0:64], NT)
    fold[32:64, 0:64] = o[0:32] + o[32:64]
    zeroth = fold[32:64]
    pay_m[0] = pack4(zeroth + pltpu.roll(zeroth, 96, 1), 0)
    m_z = stage(pay_m, 0, rz_m, z_size, along_z, 2 * span + comps + x_size)
    trace_copy(0, 0).wait_recv()
    trace_copy(0, 1).wait_recv()
    first_jump = split_rows(weight * (own[0] - part[0]))
    add_jump(first_jump, q_ref)
    halves_of(q_ref, 64)

    o = mm(s3[0:128], s3[64:128], NT)
    fold[64:96, 0:64] = o[0:32] + o[32:64]
    fold[96:128, 0:64] = o[64:96] + o[96:128]
    early = fold[64:128]
    early = early + pltpu.roll(early, 96, 1)
    pay_a[0] = jnp.concatenate([pack4(early[32 * i:32 * i + 32], 0) for i in range(2)], axis=0)
    a_z = stage(pay_a, 0, rz_a, z_size, along_z, comps + x_size)
    strains(q_ref)

    strain = ss[...]
    energy = mm(strain, strain, NT) * 0.5 + mm(split_rows(mass_ref[...] * q_ref[...]), s3[64:128], NT)
    turn = mm(first_jump, twins[...])
    trace_copy(1, 0).wait_recv()
    trace_copy(1, 1).wait_recv()
    jump = own[1] - part[1] + turn[0:32] + turn[32:64]
    energy += mm(split_rows(0.5 * weight * jump), split_rows(jump), NT)
    fold[0:32, 0:64] = energy[0:32] + energy[32:64]
    third = fold[0:32]
    third = third + pltpu.roll(third, 96, 1)
    pay_b[0] = pack4(third, 0)
    b_comp = stage(pay_b, 0, rc_b, comps, along_comp, span)

    pay_m[1] = m_z()
    m_x = stage(pay_m, 1, rx_m, x_size, along_x, 2 * span + comps)
    forces()
    gather_forces(q_ref, t_ref)
    add_jump(split_rows(weight * jump), t_ref)
    halves_of(t_ref, 128)
    pay_m[2] = m_x()
    m_comp = stage(pay_m, 2, rc_m, comps, along_comp, 2 * span)
    pay_a[1] = a_z()
    a_x = stage(pay_a, 1, rx_a, x_size, along_x, comps)
    pay_b[1] = b_comp()
    b_x = stage(pay_b, 1, rx_b, x_size, along_x, span + comps)
    pay_a[2] = a_x()
    a_comp = stage(pay_a, 2, rc_a, comps, along_comp, 0)
    pay_b[2] = b_x()
    b_z = stage(pay_b, 2, rz_b, z_size, along_z, span + comps + x_size)

    def drain(d, _):
        cell_copy(d).wait_send()
        return 0

    lax.fori_loop(1, patches, drain, 0)
    pen_copy.wait_send()
    other_copy.wait_send()
    trace_copy(0, 0).wait_send()
    trace_copy(0, 1).wait_send()
    trace_copy(1, 0).wait_send()
    trace_copy(1, 1).wait_send()

    total = a_comp()
    m0, m1, m2 = m_comp(), total[0:8], total[8:16]
    upper = unpack4(m1, 0) + unpack4(m2, 1) + unpack4(m0, 2)
    lower = unpack4(m2, 0) + unpack4(m1, 2)
    system = eliminate(jnp.concatenate([upper, lower], axis=0), 0, 32)
    lower = system[32:64] + unpack4(b_z(), 1)
    system = eliminate(jnp.concatenate([system[0:32], lower], axis=0), 32, 64)
    mixed = jnp.concatenate([system[0:32], system[0:32], system[32:64], system[32:64]], axis=0)
    weights_ref[...] = split_rows(jnp.transpose(mixed)[64:96])
    for copy in sent:
        copy.wait_send()


def finish(weights_ref, s3, r_ref, sol_hbm, res_hbm, sol, res, sems):
    weights = weights_ref[...]
    dofs = sol.shape[1]
    width = dofs // 4
    copies = []
    for part in range(4):
        for h in range(width // GROUP):
            lanes = slice(part * width + h * GROUP, part * width + (h + 1) * GROUP)
            o = mm(weights, s3[0:128, lanes])
            sol[:, lanes] = o[0:32] + o[32:64]
            o = mm(weights, s3[64:192, lanes])
            res[:, lanes] = r_ref[:, lanes] - (o[0:32] + o[32:64])
        lanes = pl.ds(part * width, width)
        for i, (src, dst) in enumerate(((sol, sol_hbm), (res, res_hbm))):
            copies.append(pltpu.make_async_copy(src.at[:, lanes], dst.at[:, lanes], sems.at[part, i]))
            copies[-1].start()
    for copy in copies:
        copy.wait()


def shards(z_size, load_cases, mass_diag, stiffness, block_cols, trace_dofs, penalty, cell_partials, cell_owner, cell_dof):
    cases, dofs = load_cases.shape
    rows = stiffness.shape[0]
    traces, ncell = trace_dofs.shape[0], cell_dof.shape[0]
    patches, comps = lax.axis_size("patch"), lax.axis_size("comp")
    groups = dofs // GROUP
    entries = rows * 4
    vm = pl.BlockSpec(memory_space=pltpu.VMEM)
    hbm = pl.BlockSpec(memory_space=pltpu.HBM)
    field = jax.ShapeDtypeStruct((cases, dofs), F32)
    x_size = patches // z_size
    stages = comps + x_size + z_size

    def sums(tall):
        return [
            pltpu.VMEM((3, tall, 128), F32),
            pltpu.VMEM((comps - 1, tall, 128), F32),
            pltpu.VMEM((x_size - 1, tall, 128), F32),
            pltpu.VMEM((z_size - 1, tall, 128), F32),
        ]

    right_side, parts, weights = pl.pallas_call(
        functools.partial(kernel, z_size),
        out_shape=(
            field, jax.ShapeDtypeStruct((6 * cases, dofs), BF16), jax.ShapeDtypeStruct((2 * cases, 128), BF16)),
        in_specs=[hbm] * 9,
        out_specs=(vm, vm, vm),
        scratch_shapes=[
            pltpu.VMEM((cases, dofs), F32),
            pltpu.VMEM((1, dofs), F32),
            pltpu.VMEM(stiffness.shape, F32),
            pltpu.VMEM((4, rows), I32),
            pltpu.SMEM((4, rows), I32),
            pltpu.VMEM((1, traces), I32),
            pltpu.VMEM((1, traces), F32),
            pltpu.VMEM((cases, ncell), F32),
            pltpu.VMEM((1, ncell), I32),
            pltpu.VMEM((1, ncell), I32),
            pltpu.VMEM((rows, 128, 256), BF16),
            pltpu.VMEM((rows, 256, 128), BF16),
            pltpu.VMEM((patches, 17, 128), F32),
            pltpu.VMEM((patches, 17, 128), F32),
            pltpu.VMEM((4, 128), I32),
            pltpu.VMEM((2, GROUP), I32),
            pltpu.VMEM((2, GROUP), F32),
            pltpu.SMEM((2, GROUP), I32),
            pltpu.SMEM((2, GROUP), F32),
            pltpu.VMEM((GROUP, traces), BF16),
            pltpu.VMEM((2, cases, traces), F32),
            pltpu.VMEM((2, cases, traces), F32),
            pltpu.VMEM((1, traces), F32),
            pltpu.VMEM((1, traces), I32),
            pltpu.VMEM((traces, traces), BF16),
            pltpu.VMEM((cases, dofs), F32),
            pltpu.VMEM((cases, dofs), F32),
            pltpu.VMEM((2 * rows, 64, 128), BF16),
            pltpu.VMEM((64, rows * 128), BF16),
            pltpu.VMEM((entries, 16, 128), F32),
            pltpu.VMEM((entries, 16, 128), F32),
            pltpu.VMEM((4 * cases, 128), F32),
            *sums(16),
            *sums(8),
            *sums(8),
            pltpu.SemaphoreType.DMA((12,)),
            pltpu.SemaphoreType.DMA((patches,)),
            pltpu.SemaphoreType.DMA((patches,)),
            pltpu.SemaphoreType.DMA((3, 2)),
            pltpu.SemaphoreType.DMA((3, 2)),
            pltpu.SemaphoreType.DMA((3 * stages,)),
            pltpu.SemaphoreType.DMA((3 * stages,)),
        ],
        compiler_params=pltpu.CompilerParams(
            collective_id=0, has_side_effects=True, vmem_limit_bytes=40 * 1024 * 1024),
    )(
        *(pltpu.with_memory_space_constraint(x, pltpu.HBM) for x in (
            load_cases, mass_diag.reshape(1, -1), stiffness, block_cols.T, trace_dofs.reshape(1, -1),
            penalty.reshape(1, -1), cell_partials, cell_owner.reshape(1, -1), cell_dof.reshape(1, -1)))
    )
    return pl.pallas_call(
        finish,
        out_shape=(field, field),
        in_specs=[vm, vm, vm],
        out_specs=(hbm, hbm),
        scratch_shapes=[
            pltpu.VMEM((cases, dofs), F32),
            pltpu.VMEM((cases, dofs), F32),
            pltpu.SemaphoreType.DMA((4, 2)),
        ],
        compiler_params=pltpu.CompilerParams(vmem_limit_bytes=8 * 1024 * 1024),
    )(weights, parts, right_side)


def solution(mesh):
    patches = mesh.shape["patch"]
    z_size = 8 if patches == 32 else patches // 2
    both = ("comp", "patch")
    return jax.shard_map(
        functools.partial(shards, z_size),
        mesh=mesh,
        in_specs=(
            P(None, both), P(both), P(both, None, None), P(both, None), P(both), P(both), P(None, both),
            P(both, None), P(both),
        ),
        out_specs=(P(None, both), P(None, both)),
        check_vma=False,
    )
```

```python
import functools

import jax
import jax.numpy as jnp
from jax import lax
from jax.experimental import pallas as pl
from jax.experimental.pallas import tpu as pltpu
from jax.sharding import PartitionSpec as P

CAP = 64
GROUP = 256
F32, BF16, I32 = jnp.float32, jnp.bfloat16, jnp.int32
NT = (((1,), (1,)), ((), ()))
NN = (((1,), (0,)), ((), ()))
MESH = pl.DeviceIdType.MESH


def mm(a, b, dims=NN):
    return lax.dot_general(a, b, dims, preferred_element_type=F32)


def split(x):
    hi = x.astype(BF16)
    return hi, (x - hi.astype(F32)).astype(BF16)


def split_rows(x):
    return jnp.concatenate(split(x), axis=0)


def iota(shape, dim):
    return lax.broadcasted_iota(I32, shape, dim)


def ones_where(mask):
    return jnp.where(mask, 1.0, 0.0)


def swap(x):
    return pltpu.roll(x, 64, 1)


def pack4(x, slot):
    band = iota((8, 128), 1) >> 5
    out = jnp.zeros((8, 128), F32)
    for g in range(4):
        out = jnp.where(band == g, pltpu.roll(x[8 * g:8 * g + 8], (32 * (g - slot)) % 128, 1), out)
    return out


def unpack4(x, slot):
    band = iota((8, 128), 1) >> 5
    return jnp.concatenate(
        [jnp.where(band == slot, pltpu.roll(x, (32 * (slot - g)) % 128, 1), 0.0) for g in range(4)], axis=0)


def eliminate(system, first, last):
    place = iota((64, 128), 0)
    for start in range(first, last, 8):
        wide = [jnp.broadcast_to(system[:, start + j:start + j + 1], (64, 128)) for j in range(8)]
        for j in range(8):
            k = start + j
            here = place == k
            inverse = 1.0 / wide[j][k:k + 1]
            factor = wide[j] * inverse
            row = system[k:k + 1]
            system = jnp.where(here, row * inverse, system - factor * row)
            for i in range(j + 1, 8):
                entry = wide[i][k:k + 1]
                wide[i] = jnp.where(here, entry * inverse, wide[i] - factor * entry)
    return system


def kernel(
    z_size, load_hbm, mass_hbm, stiff_hbm, cols_hbm, trace_hbm, pen_hbm, cells_hbm, owner_hbm,
    cdof_hbm, r_ref, s3, weights_ref,
    load, mass_ref, stiff, cols_ref, cols_smem, trace_ref, pen_ref, cells_ref, owner_ref, cdof_ref,
    kk, kt, send, recv, colp, csr_i, csr_f, csr_is, csr_fs, hot, own, part, pen_other, trace_other, twins,
    q_ref, t_ref, vab, ss, tp, run, fold, pay_a, rc_a, rx_a, rz_a, pay_b, rc_b, rx_b, rz_b, pay_m, rc_m, rx_m, rz_m,
    in_sem, a2a_send, a2a_recv, tr_send, tr_recv, red_send, red_recv,
):
    patches, comps = lax.axis_size("patch"), lax.axis_size("comp")
    me, mine = lax.axis_index("patch"), lax.axis_index("comp")
    cases, dofs = load.shape
    groups = dofs // GROUP
    ncell = cells_ref.shape[1]
    traces = trace_ref.shape[1]
    chunks = traces // GROUP
    rows = stiff.shape[0]
    entries = rows * 4
    spare = 64 - rows
    pairs = rows // 2
    left = iota((1, 128), 1) < 64
    left16 = iota((16, 128), 1) < 64
    left32 = iota((32, 128), 1) < 64

    get_stiff = pltpu.make_async_copy(stiff_hbm, stiff, in_sem.at[0])
    get_load = pltpu.make_async_copy(load_hbm, load, in_sem.at[1])
    small = [
        pltpu.make_async_copy(src, dst, in_sem.at[4 + i]) for i, (src, dst) in enumerate((
            (owner_hbm, owner_ref), (cdof_hbm, cdof_ref), (cells_hbm, cells_ref), (cols_hbm, cols_ref),
            (cols_hbm, cols_smem), (trace_hbm, trace_ref), (pen_hbm, pen_ref), (mass_hbm, mass_ref)))
    ]

    for copy in small:
        copy.start()
    barrier = pltpu.get_barrier_semaphore()

    for d in range(1, patches):
        pl.semaphore_signal(barrier, inc=1, device_id={"patch": lax.rem(me + d, patches)}, device_id_type=MESH)
    for d in range(1, comps):
        pl.semaphore_signal(barrier, inc=1, device_id={"comp": lax.rem(mine + d, comps)}, device_id_type=MESH)
    get_stiff.start()
    get_load.start()

    tri = ones_where(iota((ncell, ncell), 0) < iota((ncell, ncell), 1)).astype(BF16)
    for copy in small[0:3]:
        copy.wait()

    owner = owner_ref[...]
    hit = owner == iota((patches, ncell), 0)
    before = mm(ones_where(hit).astype(BF16), tri)
    pos = jnp.sum(jnp.where(hit, before, 0.0), axis=0, keepdims=True).astype(I32)
    slot = (owner & 3) * CAP + pos
    slot_hot = ones_where(iota((GROUP, ncell), 0) == slot).astype(BF16)
    cdof = cdof_ref[...]
    row16 = iota((16, ncell), 0)
    dof_rows = jnp.where(row16 == 0, cdof >> 8, jnp.where(row16 == 1, cdof & 255, 0)).astype(F32)
    cell_hi, cell_lo = split(cells_ref[...])
    cell_rows = jnp.concatenate([cell_hi, cell_lo, dof_rows.astype(BF16)], axis=0)
    masked = []
    for g in range(patches // 4):
        mask = jnp.broadcast_to(ones_where((owner >> 2) == g), (16, ncell)).astype(BF16)
        masked.append(cell_rows * jnp.concatenate([mask] * 5, axis=0))
    packed = mm(jnp.concatenate(masked, axis=0), slot_hot, NT)
    for g in range(patches // 4):
        values = packed[g * 80:g * 80 + 32] + packed[g * 80 + 32:g * 80 + 64]
        places = packed[g * 80 + 64:g * 80 + 72]
        for half in range(2):
            tile = values[:, half * 128:(half + 1) * 128]
            top, bottom = tile[0:16], tile[16:32]
            place = places[:, half * 128:(half + 1) * 128]
            place_hi, place_lo = place[0:1], place[1:2]
            even = g * 4 + half * 2
            send[even, 0:16] = jnp.where(left16, top, swap(bottom))
            send[even + 1, 0:16] = jnp.where(left16, swap(top), bottom)
            send[even, 16:17] = jnp.where(left, place_hi, swap(place_lo))
            send[even + 1, 16:17] = jnp.where(left, swap(place_hi), place_lo)
    recv[0] = send[me]

    for copy in small[3:]:
        copy.wait()

    pl.semaphore_wait(barrier, patches + comps - 2)

    other = lax.rem(me + patches // 2, patches)

    def cell_copy(d):
        to = lax.rem(me + d, patches)
        return pltpu.make_async_remote_copy(
            src_ref=send.at[to], dst_ref=recv.at[d], send_sem=a2a_send.at[d], recv_sem=a2a_recv.at[d],
            device_id={"patch": to}, device_id_type=MESH,
        )

    pen_copy = pltpu.make_async_remote_copy(
        src_ref=pen_ref, dst_ref=pen_other, send_sem=a2a_send.at[0], recv_sem=a2a_recv.at[0],
        device_id={"patch": other}, device_id_type=MESH,
    )
    other_copy = pltpu.make_async_remote_copy(
        src_ref=trace_ref, dst_ref=trace_other, send_sem=tr_send.at[2, 0], recv_sem=tr_recv.at[2, 0],
        device_id={"patch": other}, device_id_type=MESH,
    )
    x_size = patches // z_size
    pen_copy.start()
    other_copy.start()
    far_first = [x_size // 2] + list(range(1, x_size // 2)) + list(range(x_size // 2 + 1, x_size)) + [0]
    for x in far_first:
        for z in range(z_size):
            if x or z:
                cell_copy(x * z_size + z).start()

    i0, i1 = iota((GROUP, GROUP), 0), iota((GROUP, GROUP), 1)
    colp[...] = jnp.full((4, 128), 255, I32)
    colp[:, 0:rows] = cols_ref[...]
    quad = colp[...]
    turned = pltpu.roll(quad, 64, 1)
    col = jnp.concatenate(
        [jnp.where(left, quad[0:1], turned[1:2]), jnp.where(left, quad[2:3], turned[3:4])], axis=1)
    col_of = jnp.transpose(jnp.broadcast_to(col, (GROUP, GROUP)))
    ahead = (col_of < col) | ((col_of == col) & (i0 < i1))
    rank = jnp.sum(jnp.where(ahead, 1, 0), axis=0, keepdims=True)
    at_rank = jnp.transpose(jnp.broadcast_to(rank, (GROUP, GROUP))) == i1
    order = jnp.sum(jnp.where(at_rank, i0, 0), axis=0, keepdims=True)
    ocol = jnp.sum(jnp.where(at_rank, col_of, 0), axis=0, keepdims=True)
    upto = jnp.sum(jnp.where(col_of <= i1, 1, 0), axis=0, keepdims=True)
    same = jnp.sum(jnp.where(col_of == i1, 1, 0), axis=0, keepdims=True)
    lane = iota((1, GROUP), 1)
    csr_i[0:1, :] = jnp.minimum((order & 63) * 4 + (order >> 6), entries - 1)
    csr_i[1:2, :] = jnp.clip(upto - 1, 0, entries - 1)
    csr_f[0:1, :] = ones_where((ocol == pltpu.roll(ocol, 1, 1)) & (lane > 0))
    csr_f[1:2, :] = ones_where(same > 0)
    put_i = pltpu.make_async_copy(csr_i, csr_is, in_sem.at[2])
    put_f = pltpu.make_async_copy(csr_f, csr_fs, in_sem.at[3])
    put_i.start()
    put_f.start()

    for c in range(chunks):
        lanes = slice(c * GROUP, (c + 1) * GROUP)
        hot[:, lanes] = ones_where(i0 == trace_ref[:, lanes] & 255).astype(BF16)

    get_stiff.wait()

    def halve(n, _):
        hi, lo = split(stiff[n])
        kk[n, 0:64] = hi
        kk[n, 64:128] = lo
        return 0

    lax.fori_loop(0, rows, halve, 0)
    for n in range(rows):
        kt[n] = jnp.transpose(kk[n])
    fold[...] = jnp.zeros((128, 128), F32)
    put_i.wait()
    put_f.wait()

    pen_copy.wait_recv()
    other_copy.wait_recv()
    for c in range(chunks):
        lanes = slice(c * GROUP, (c + 1) * GROUP)
        mine_of = jnp.transpose(jnp.broadcast_to(trace_ref[:, lanes], (GROUP, GROUP)))
        other_of = jnp.transpose(jnp.broadcast_to(trace_other[:, lanes], (GROUP, GROUP)))
        for e in range(chunks):
            across = slice(e * GROUP, (e + 1) * GROUP)
            twins[lanes, across] = (
                ones_where(mine_of == trace_ref[:, across]) + ones_where(other_of == trace_other[:, across])
            ).astype(BF16)
    get_load.wait()

    def masked_groups(data, high):
        parts = []
        for h in range(groups):
            mask = jnp.broadcast_to(ones_where(high == h), (16, data.shape[1])).astype(BF16)
            parts.append(data * jnp.concatenate([mask] * 4, axis=0))
        return jnp.concatenate(parts, axis=0)

    def add_groups(total, base_ref, out_ref):
        for h in range(groups):
            lanes = slice(h * GROUP, (h + 1) * GROUP)
            out_ref[:, lanes] = base_ref[:, lanes] + total[h * 64:h * 64 + 32] + total[h * 64 + 32:h * 64 + 64]

    def arrive(d, _):
        cell_copy(d).wait_recv()
        return 0

    def place(steps, base_ref):
        for x in steps:
            lax.fori_loop(max(1, x * z_size), (x + 1) * z_size, arrive, 0)
        data, highs, lows = [], [], []
        for x in steps:
            for d in range(x * z_size, (x + 1) * z_size, 2):
                a, b = recv[d], recv[d + 1]
                at, bt, ap, bp = a[0:16], b[0:16], a[16:17], b[16:17]
                data.append(split_rows(jnp.concatenate(
                    [jnp.where(left16, at, swap(bt)), jnp.where(left16, swap(at), bt)], axis=0)))
                highs.append(jnp.where(left, ap, swap(bp)).astype(I32))
                lows.append(jnp.where(left, swap(ap), bp).astype(I32))
        rows_of = iota((GROUP, 128), 0)
        low_hot = jnp.concatenate([ones_where(rows_of == low).astype(BF16) for low in lows], axis=1)
        data = masked_groups(jnp.concatenate(data, axis=1), jnp.concatenate(highs, axis=1))
        add_groups(mm(data, low_hot, NT), base_ref, r_ref)

    place(far_first[:x_size // 2], load)
    place(far_first[x_size // 2:], r_ref)

    def trace_copy(turn, half):
        lanes = pl.ds(half * (traces // 2), traces // 2)
        return pltpu.make_async_remote_copy(
            src_ref=own.at[turn, :, lanes], dst_ref=part.at[turn, :, lanes], send_sem=tr_send.at[turn, half],
            recv_sem=tr_recv.at[turn, half], device_id={"patch": other}, device_id_type=MESH,
        )

    def halves_of(v_ref, base):
        for h in range(groups):
            lanes = slice(h * GROUP, (h + 1) * GROUP)
            s3[base:base + 64, lanes] = split_rows(v_ref[:, lanes])

    def send_trace(turn, base):
        stacked = jnp.concatenate([s3[base:base + 64, h * GROUP:(h + 1) * GROUP] for h in range(groups)], axis=0)
        for c in range(chunks):
            lanes = slice(c * GROUP, (c + 1) * GROUP)
            picked = mm(stacked, hot[:, lanes])
            high = trace_ref[:, lanes] >> 8
            total = jnp.zeros((32, GROUP), F32)
            for h in range(groups):
                total = jnp.where(high == h, picked[h * 64:h * 64 + 32] + picked[h * 64 + 32:h * 64 + 64], total)
            own[turn, :, lanes] = total
            if turn == 0 and c + 1 == chunks // 2:
                trace_copy(turn, 0).start()
        if turn == 1:
            trace_copy(turn, 0).start()
        trace_copy(turn, 1).start()

    def strains(v_ref):
        for i in range(pairs):
            tile = v_ref[:, i * 128:(i + 1) * 128]
            turned = swap(tile)
            vab[4 * i] = split_rows(jnp.where(left32, tile, 0.0))
            vab[4 * i + 1] = split_rows(jnp.where(left32, 0.0, turned))
            vab[4 * i + 2] = split_rows(jnp.where(left32, turned, 0.0))
            vab[4 * i + 3] = split_rows(jnp.where(left32, 0.0, tile))

        for n in range(rows):
            c0, c1, c2, c3 = (cols_smem[k, n] for k in range(4))
            x = jnp.concatenate(
                [vab[2 * c0] + vab[2 * c1 + 1], vab[2 * c2] + vab[2 * c3 + 1]], axis=1)
            o = mm(x, kt[n])
            o = o[0:32] + o[32:64]
            ss[:, n * 128:(n + 1) * 128] = split_rows(o + swap(o))

    def forces():
        for n in range(rows):
            o = mm(ss[:, n * 128:(n + 1) * 128], kk[n])
            o = o[0:32] + o[32:64]
            for half in range(2):
                tile = o[:, half * 128:(half + 1) * 128]
                top, bottom = tile[0:16], tile[16:32]
                tp[n * 4 + 2 * half] = jnp.where(left16, top, swap(bottom))
                tp[n * 4 + 2 * half + 1] = jnp.where(left16, swap(top), bottom)

    def gather_forces(v_ref, out_ref):
        def add_up(step, total):
            for u in range(8):
                i = step * 8 + u
                total = total * csr_fs[0, i] + tp[csr_is[0, i]]
                run[i] = total
            return total

        lax.fori_loop(0, entries // 8, add_up, jnp.zeros((16, 128), F32))
        for i in range(pairs):
            lanes = slice(i * 128, (i + 1) * 128)
            a = run[csr_is[1, 2 * i]] * csr_fs[1, 2 * i]
            b = run[csr_is[1, 2 * i + 1]] * csr_fs[1, 2 * i + 1]
            tile = jnp.concatenate(
                [jnp.where(left16, a, swap(b)), jnp.where(left16, swap(a), b)], axis=0)
            out_ref[:, lanes] = tile + mass_ref[:, lanes] * v_ref[:, lanes]

    def add_jump(jump, out_ref):
        add_groups(mm(masked_groups(jump, trace_ref[...] >> 8), hot[...], NT), out_ref, out_ref)

    sent = []

    def stage(pay, index, slots, count, place, base):
        copies = []
        for j in range(1, count):
            copies.append(pltpu.make_async_remote_copy(
                src_ref=pay.at[index], dst_ref=slots.at[j - 1], send_sem=red_send.at[base + j],
                recv_sem=red_recv.at[base + j], device_id=place(j), device_id_type=MESH))
            copies[-1].start()
        sent.extend(copies)

        def finish():
            total = pay[index]
            for j, copy in enumerate(copies):
                copy.wait_recv()
                total += slots[j]
            return total

        return finish

    z_first = (me // z_size) * z_size
    span = comps + x_size + z_size

    def along_comp(j):
        return {"comp": lax.rem(mine + j, comps)}

    def along_x(j):
        return {"patch": lax.rem(me + j * z_size, patches)}

    def along_z(j):
        return {"patch": z_first + lax.rem(lax.rem(me, z_size) + j, z_size)}

    weight = pen_ref[...] * pen_other[...]
    halves_of(r_ref, 0)
    send_trace(0, 0)
    strains(r_ref)
    forces()
    gather_forces(r_ref, q_ref)
    halves_of(q_ref, 64)
    send_trace(1, 64)
    o = mm(s3[0:64], s3[0:64], NT)
    fold[32:64, 0:64] = o[0:32] + o[32:64]
    zeroth = fold[32:64]
    pay_m[0] = pack4(zeroth + pltpu.roll(zeroth, 96, 1), 0)
    m_z = stage(pay_m, 0, rz_m, z_size, along_z, 2 * span + comps + x_size)
    trace_copy(0, 0).wait_recv()
    trace_copy(0, 1).wait_recv()
    first_jump = split_rows(weight * (own[0] - part[0]))
    add_jump(first_jump, q_ref)
    halves_of(q_ref, 64)

    o = mm(s3[0:128], s3[64:128], NT)
    fold[64:96, 0:64] = o[0:32] + o[32:64]
    fold[96:128, 0:64] = o[64:96] + o[96:128]
    early = fold[64:128]
    early = early + pltpu.roll(early, 96, 1)
    pay_a[0] = jnp.concatenate([pack4(early[32 * i:32 * i + 32], 0) for i in range(2)], axis=0)
    a_z = stage(pay_a, 0, rz_a, z_size, along_z, comps + x_size)
    strains(q_ref)

    strain = ss[...]
    energy = mm(strain, strain, NT) * 0.5 + mm(split_rows(mass_ref[...] * q_ref[...]), s3[64:128], NT)
    turn = mm(first_jump, twins[...])
    trace_copy(1, 0).wait_recv()
    trace_copy(1, 1).wait_recv()
    jump = own[1] - part[1] + turn[0:32] + turn[32:64]
    energy += mm(split_rows(0.5 * weight * jump), split_rows(jump), NT)
    fold[0:32, 0:64] = energy[0:32] + energy[32:64]
    third = fold[0:32]
    third = third + pltpu.roll(third, 96, 1)
    pay_b[0] = pack4(third, 0)
    b_comp = stage(pay_b, 0, rc_b, comps, along_comp, span)

    pay_m[1] = m_z()
    m_x = stage(pay_m, 1, rx_m, x_size, along_x, 2 * span + comps)
    forces()
    gather_forces(q_ref, t_ref)
    add_jump(split_rows(weight * jump), t_ref)
    halves_of(t_ref, 128)
    pay_a[1] = a_z()
    a_x = stage(pay_a, 1, rx_a, x_size, along_x, comps)
    pay_b[1] = b_comp()
    b_x = stage(pay_b, 1, rx_b, x_size, along_x, span + comps)
    pay_m[2] = m_x()
    m_comp = stage(pay_m, 2, rc_m, comps, along_comp, 2 * span)
    pay_a[2] = a_x()
    a_comp = stage(pay_a, 2, rc_a, comps, along_comp, 0)
    pay_b[2] = b_x()
    b_z = stage(pay_b, 2, rz_b, z_size, along_z, span + comps + x_size)

    def drain(d, _):
        cell_copy(d).wait_send()
        return 0

    lax.fori_loop(1, patches, drain, 0)
    pen_copy.wait_send()
    other_copy.wait_send()
    trace_copy(0, 0).wait_send()
    trace_copy(0, 1).wait_send()
    trace_copy(1, 0).wait_send()
    trace_copy(1, 1).wait_send()

    total = a_comp()
    m0, m1, m2 = m_comp(), total[0:8], total[8:16]
    upper = unpack4(m1, 0) + unpack4(m2, 1) + unpack4(m0, 2)
    lower = unpack4(m2, 0) + unpack4(m1, 2)
    system = eliminate(jnp.concatenate([upper, lower], axis=0), 0, 32)
    lower = system[32:64] + unpack4(b_z(), 1)
    system = eliminate(jnp.concatenate([system[0:32], lower], axis=0), 32, 64)
    mixed = jnp.concatenate([system[0:32], system[0:32], system[32:64], system[32:64]], axis=0)
    weights_ref[...] = split_rows(jnp.transpose(mixed)[64:96])
    for copy in sent:
        copy.wait_send()


def finish(weights_ref, s3, r_ref, sol_hbm, res_hbm, sol, res, sems):
    weights = weights_ref[...]
    dofs = sol.shape[1]
    width = dofs // 4
    copies = []
    for part in range(4):
        for h in range(width // GROUP):
            lanes = slice(part * width + h * GROUP, part * width + (h + 1) * GROUP)
            o = mm(weights, s3[0:128, lanes])
            sol[:, lanes] = o[0:32] + o[32:64]
            o = mm(weights, s3[64:192, lanes])
            res[:, lanes] = r_ref[:, lanes] - (o[0:32] + o[32:64])
        lanes = pl.ds(part * width, width)
        for i, (src, dst) in enumerate(((sol, sol_hbm), (res, res_hbm))):
            copies.append(pltpu.make_async_copy(src.at[:, lanes], dst.at[:, lanes], sems.at[part, i]))
            copies[-1].start()
    for copy in copies:
        copy.wait()


def shards(z_size, load_cases, mass_diag, stiffness, block_cols, trace_dofs, penalty, cell_partials, cell_owner, cell_dof):
    cases, dofs = load_cases.shape
    rows = stiffness.shape[0]
    traces, ncell = trace_dofs.shape[0], cell_dof.shape[0]
    patches, comps = lax.axis_size("patch"), lax.axis_size("comp")
    groups = dofs // GROUP
    entries = rows * 4
    vm = pl.BlockSpec(memory_space=pltpu.VMEM)
    hbm = pl.BlockSpec(memory_space=pltpu.HBM)
    field = jax.ShapeDtypeStruct((cases, dofs), F32)
    x_size = patches // z_size
    stages = comps + x_size + z_size

    def sums(tall):
        return [
            pltpu.VMEM((3, tall, 128), F32),
            pltpu.VMEM((comps - 1, tall, 128), F32),
            pltpu.VMEM((x_size - 1, tall, 128), F32),
            pltpu.VMEM((z_size - 1, tall, 128), F32),
        ]

    right_side, parts, weights = pl.pallas_call(
        functools.partial(kernel, z_size),
        out_shape=(
            field, jax.ShapeDtypeStruct((6 * cases, dofs), BF16), jax.ShapeDtypeStruct((2 * cases, 128), BF16)),
        in_specs=[hbm] * 9,
        out_specs=(vm, vm, vm),
        scratch_shapes=[
            pltpu.VMEM((cases, dofs), F32),
            pltpu.VMEM((1, dofs), F32),
            pltpu.VMEM(stiffness.shape, F32),
            pltpu.VMEM((4, rows), I32),
            pltpu.SMEM((4, rows), I32),
            pltpu.VMEM((1, traces), I32),
            pltpu.VMEM((1, traces), F32),
            pltpu.VMEM((cases, ncell), F32),
            pltpu.VMEM((1, ncell), I32),
            pltpu.VMEM((1, ncell), I32),
            pltpu.VMEM((rows, 128, 256), BF16),
            pltpu.VMEM((rows, 256, 128), BF16),
            pltpu.VMEM((patches, 17, 128), F32),
            pltpu.VMEM((patches, 17, 128), F32),
            pltpu.VMEM((4, 128), I32),
            pltpu.VMEM((2, GROUP), I32),
            pltpu.VMEM((2, GROUP), F32),
            pltpu.SMEM((2, GROUP), I32),
            pltpu.SMEM((2, GROUP), F32),
            pltpu.VMEM((GROUP, traces), BF16),
            pltpu.VMEM((2, cases, traces), F32),
            pltpu.VMEM((2, cases, traces), F32),
            pltpu.VMEM((1, traces), F32),
            pltpu.VMEM((1, traces), I32),
            pltpu.VMEM((traces, traces), BF16),
            pltpu.VMEM((cases, dofs), F32),
            pltpu.VMEM((cases, dofs), F32),
            pltpu.VMEM((2 * rows, 64, 128), BF16),
            pltpu.VMEM((64, rows * 128), BF16),
            pltpu.VMEM((entries, 16, 128), F32),
            pltpu.VMEM((entries, 16, 128), F32),
            pltpu.VMEM((4 * cases, 128), F32),
            *sums(16),
            *sums(8),
            *sums(8),
            pltpu.SemaphoreType.DMA((12,)),
            pltpu.SemaphoreType.DMA((patches,)),
            pltpu.SemaphoreType.DMA((patches,)),
            pltpu.SemaphoreType.DMA((3, 2)),
            pltpu.SemaphoreType.DMA((3, 2)),
            pltpu.SemaphoreType.DMA((3 * stages,)),
            pltpu.SemaphoreType.DMA((3 * stages,)),
        ],
        compiler_params=pltpu.CompilerParams(
            collective_id=0, has_side_effects=True, vmem_limit_bytes=40 * 1024 * 1024),
    )(
        *(pltpu.with_memory_space_constraint(x, pltpu.HBM) for x in (
            load_cases, mass_diag.reshape(1, -1), stiffness, block_cols.T, trace_dofs.reshape(1, -1),
            penalty.reshape(1, -1), cell_partials, cell_owner.reshape(1, -1), cell_dof.reshape(1, -1)))
    )
    return pl.pallas_call(
        finish,
        out_shape=(field, field),
        in_specs=[vm, vm, vm],
        out_specs=(hbm, hbm),
        scratch_shapes=[
            pltpu.VMEM((cases, dofs), F32),
            pltpu.VMEM((cases, dofs), F32),
            pltpu.SemaphoreType.DMA((4, 2)),
        ],
        compiler_params=pltpu.CompilerParams(vmem_limit_bytes=8 * 1024 * 1024),
    )(weights, parts, right_side)


def solution(mesh):
    patches = mesh.shape["patch"]
    z_size = 8 if patches == 32 else patches // 2
    both = ("comp", "patch")
    return jax.shard_map(
        functools.partial(shards, z_size),
        mesh=mesh,
        in_specs=(
            P(None, both), P(both), P(both, None, None), P(both, None), P(both), P(both), P(None, both),
            P(both, None), P(both),
        ),
        out_specs=(P(None, both), P(None, both)),
        check_vma=False,
    )
```

```python
import functools

import jax
import jax.numpy as jnp
from jax import lax
from jax.experimental import pallas as pl
from jax.experimental.pallas import tpu as pltpu
from jax.sharding import PartitionSpec as P

CAP = 64
GROUP = 256
F32, BF16, I32 = jnp.float32, jnp.bfloat16, jnp.int32
NT = (((1,), (1,)), ((), ()))
NN = (((1,), (0,)), ((), ()))
MESH = pl.DeviceIdType.MESH


def mm(a, b, dims=NN):
    return lax.dot_general(a, b, dims, preferred_element_type=F32)


def split(x):
    hi = x.astype(BF16)
    return hi, (x - hi.astype(F32)).astype(BF16)


def split_rows(x):
    return jnp.concatenate(split(x), axis=0)


def iota(shape, dim):
    return lax.broadcasted_iota(I32, shape, dim)


def ones_where(mask):
    return jnp.where(mask, 1.0, 0.0)


def swap(x):
    return pltpu.roll(x, 64, 1)


def pack4(x, slot):
    band = iota((8, 128), 1) >> 5
    out = jnp.zeros((8, 128), F32)
    for g in range(4):
        out = jnp.where(band == g, pltpu.roll(x[8 * g:8 * g + 8], (32 * (g - slot)) % 128, 1), out)
    return out


def unpack4(x, slot):
    band = iota((8, 128), 1) >> 5
    return jnp.concatenate(
        [jnp.where(band == slot, pltpu.roll(x, (32 * (slot - g)) % 128, 1), 0.0) for g in range(4)], axis=0)


def eliminate(system, first, last):
    place = iota((64, 128), 0)
    for start in range(first, last, 8):
        wide = [jnp.broadcast_to(system[:, start + j:start + j + 1], (64, 128)) for j in range(8)]
        for j in range(8):
            k = start + j
            here = place == k
            inverse = 1.0 / wide[j][k:k + 1]
            factor = wide[j] * inverse
            row = system[k:k + 1]
            system = jnp.where(here, row * inverse, system - factor * row)
            for i in range(j + 1, 8):
                entry = wide[i][k:k + 1]
                wide[i] = jnp.where(here, entry * inverse, wide[i] - factor * entry)
    return system


def kernel(
    z_size, load_hbm, mass_hbm, stiff_hbm, cols_hbm, trace_hbm, pen_hbm, cells_hbm, owner_hbm,
    cdof_hbm, r_ref, s3, weights_ref,
    load, mass_ref, stiff, cols_ref, cols_smem, trace_ref, pen_ref, cells_ref, owner_ref, cdof_ref,
    kk, kt, send, recv, colp, csr_i, csr_f, csr_is, csr_fs, hot, own, part, pen_other, trace_other, twins,
    q_ref, t_ref, vab, ss, tp, run, fold, pay_a, rc_a, rx_a, rz_a, pay_b, rc_b, rx_b, rz_b, pay_m, rc_m, rx_m, rz_m,
    in_sem, a2a_send, a2a_recv, tr_send, tr_recv, red_send, red_recv,
):
    patches, comps = lax.axis_size("patch"), lax.axis_size("comp")
    me, mine = lax.axis_index("patch"), lax.axis_index("comp")
    cases, dofs = load.shape
    groups = dofs // GROUP
    ncell = cells_ref.shape[1]
    traces = trace_ref.shape[1]
    chunks = traces // GROUP
    rows = stiff.shape[0]
    entries = rows * 4
    spare = 64 - rows
    pairs = rows // 2
    left = iota((1, 128), 1) < 64
    left16 = iota((16, 128), 1) < 64
    left32 = iota((32, 128), 1) < 64

    get_stiff = pltpu.make_async_copy(stiff_hbm, stiff, in_sem.at[0])
    get_load = pltpu.make_async_copy(load_hbm, load, in_sem.at[1])
    small = [
        pltpu.make_async_copy(src, dst, in_sem.at[4 + i]) for i, (src, dst) in enumerate((
            (owner_hbm, owner_ref), (cdof_hbm, cdof_ref), (cells_hbm, cells_ref), (cols_hbm, cols_ref),
            (cols_hbm, cols_smem), (trace_hbm, trace_ref), (pen_hbm, pen_ref), (mass_hbm, mass_ref)))
    ]

    for copy in small:
        copy.start()
    barrier = pltpu.get_barrier_semaphore()

    for d in range(1, patches):
        pl.semaphore_signal(barrier, inc=1, device_id={"patch": lax.rem(me + d, patches)}, device_id_type=MESH)
    for d in range(1, comps):
        pl.semaphore_signal(barrier, inc=1, device_id={"comp": lax.rem(mine + d, comps)}, device_id_type=MESH)
    get_stiff.start()
    get_load.start()

    tri = ones_where(iota((ncell, ncell), 0) < iota((ncell, ncell), 1)).astype(BF16)
    for copy in small[0:3]:
        copy.wait()

    owner = owner_ref[...]
    hit = owner == iota((patches, ncell), 0)
    before = mm(ones_where(hit).astype(BF16), tri)
    pos = jnp.sum(jnp.where(hit, before, 0.0), axis=0, keepdims=True).astype(I32)
    slot = (owner & 3) * CAP + pos
    slot_hot = ones_where(iota((GROUP, ncell), 0) == slot).astype(BF16)
    cdof = cdof_ref[...]
    row16 = iota((16, ncell), 0)
    dof_rows = jnp.where(row16 == 0, cdof >> 8, jnp.where(row16 == 1, cdof & 255, 0)).astype(F32)
    cell_hi, cell_lo = split(cells_ref[...])
    cell_rows = jnp.concatenate([cell_hi, cell_lo, dof_rows.astype(BF16)], axis=0)
    masked = []
    for g in range(patches // 4):
        mask = jnp.broadcast_to(ones_where((owner >> 2) == g), (16, ncell)).astype(BF16)
        masked.append(cell_rows * jnp.concatenate([mask] * 5, axis=0))
    packed = mm(jnp.concatenate(masked, axis=0), slot_hot, NT)
    for g in range(patches // 4):
        values = packed[g * 80:g * 80 + 32] + packed[g * 80 + 32:g * 80 + 64]
        places = packed[g * 80 + 64:g * 80 + 72]
        for half in range(2):
            tile = values[:, half * 128:(half + 1) * 128]
            top, bottom = tile[0:16], tile[16:32]
            place = places[:, half * 128:(half + 1) * 128]
            place_hi, place_lo = place[0:1], place[1:2]
            even = g * 4 + half * 2
            send[even, 0:16] = jnp.where(left16, top, swap(bottom))
            send[even + 1, 0:16] = jnp.where(left16, swap(top), bottom)
            send[even, 16:17] = jnp.where(left, place_hi, swap(place_lo))
            send[even + 1, 16:17] = jnp.where(left, swap(place_hi), place_lo)
    recv[0] = send[me]

    for copy in small[3:]:
        copy.wait()

    pl.semaphore_wait(barrier, patches + comps - 2)

    other = lax.rem(me + patches // 2, patches)

    def cell_copy(d):
        to = lax.rem(me + d, patches)
        return pltpu.make_async_remote_copy(
            src_ref=send.at[to], dst_ref=recv.at[d], send_sem=a2a_send.at[d], recv_sem=a2a_recv.at[d],
            device_id={"patch": to}, device_id_type=MESH,
        )

    pen_copy = pltpu.make_async_remote_copy(
        src_ref=pen_ref, dst_ref=pen_other, send_sem=a2a_send.at[0], recv_sem=a2a_recv.at[0],
        device_id={"patch": other}, device_id_type=MESH,
    )
    other_copy = pltpu.make_async_remote_copy(
        src_ref=trace_ref, dst_ref=trace_other, send_sem=tr_send.at[2, 0], recv_sem=tr_recv.at[2, 0],
        device_id={"patch": other}, device_id_type=MESH,
    )
    x_size = patches // z_size
    pen_copy.start()
    other_copy.start()
    far_first = [x_size // 2] + list(range(1, x_size // 2)) + list(range(x_size // 2 + 1, x_size)) + [0]
    for x in far_first:
        for z in range(z_size):
            if x or z:
                cell_copy(x * z_size + z).start()

    i0, i1 = iota((GROUP, GROUP), 0), iota((GROUP, GROUP), 1)
    colp[...] = jnp.full((4, 128), 255, I32)
    colp[:, 0:rows] = cols_ref[...]
    quad = colp[...]
    turned = pltpu.roll(quad, 64, 1)
    col = jnp.concatenate(
        [jnp.where(left, quad[0:1], turned[1:2]), jnp.where(left, quad[2:3], turned[3:4])], axis=1)
    col_of = jnp.transpose(jnp.broadcast_to(col, (GROUP, GROUP)))
    ahead = (col_of < col) | ((col_of == col) & (i0 < i1))
    rank = jnp.sum(jnp.where(ahead, 1, 0), axis=0, keepdims=True)
    at_rank = jnp.transpose(jnp.broadcast_to(rank, (GROUP, GROUP))) == i1
    order = jnp.sum(jnp.where(at_rank, i0, 0), axis=0, keepdims=True)
    ocol = jnp.sum(jnp.where(at_rank, col_of, 0), axis=0, keepdims=True)
    upto = jnp.sum(jnp.where(col_of <= i1, 1, 0), axis=0, keepdims=True)
    same = jnp.sum(jnp.where(col_of == i1, 1, 0), axis=0, keepdims=True)
    lane = iota((1, GROUP), 1)
    csr_i[0:1, :] = jnp.minimum((order & 63) * 4 + (order >> 6), entries - 1)
    csr_i[1:2, :] = jnp.clip(upto - 1, 0, entries - 1)
    csr_f[0:1, :] = ones_where((ocol == pltpu.roll(ocol, 1, 1)) & (lane > 0))
    csr_f[1:2, :] = ones_where(same > 0)
    put_i = pltpu.make_async_copy(csr_i, csr_is, in_sem.at[2])
    put_f = pltpu.make_async_copy(csr_f, csr_fs, in_sem.at[3])
    put_i.start()
    put_f.start()

    for c in range(chunks):
        lanes = slice(c * GROUP, (c + 1) * GROUP)
        hot[:, lanes] = ones_where(i0 == trace_ref[:, lanes] & 255).astype(BF16)

    get_stiff.wait()

    def halve(n, _):
        hi, lo = split(stiff[n])
        kk[n, 0:64] = hi
        kk[n, 64:128] = lo
        return 0

    lax.fori_loop(0, rows, halve, 0)
    for n in range(rows):
        kt[n] = jnp.transpose(kk[n])
    fold[...] = jnp.zeros((128, 128), F32)
    put_i.wait()
    put_f.wait()

    pen_copy.wait_recv()
    other_copy.wait_recv()
    for c in range(chunks):
        lanes = slice(c * GROUP, (c + 1) * GROUP)
        mine_of = jnp.transpose(jnp.broadcast_to(trace_ref[:, lanes], (GROUP, GROUP)))
        other_of = jnp.transpose(jnp.broadcast_to(trace_other[:, lanes], (GROUP, GROUP)))
        for e in range(chunks):
            across = slice(e * GROUP, (e + 1) * GROUP)
            twins[lanes, across] = (
                ones_where(mine_of == trace_ref[:, across]) + ones_where(other_of == trace_other[:, across])
            ).astype(BF16)
    get_load.wait()

    def masked_groups(data, high):
        parts = []
        for h in range(groups):
            mask = jnp.broadcast_to(ones_where(high == h), (16, data.shape[1])).astype(BF16)
            parts.append(data * jnp.concatenate([mask] * 4, axis=0))
        return jnp.concatenate(parts, axis=0)

    def add_groups(total, base_ref, out_ref):
        for h in range(groups):
            lanes = slice(h * GROUP, (h + 1) * GROUP)
            out_ref[:, lanes] = base_ref[:, lanes] + total[h * 64:h * 64 + 32] + total[h * 64 + 32:h * 64 + 64]

    def arrive(d, _):
        cell_copy(d).wait_recv()
        return 0

    def place(steps, base_ref):
        for x in steps:
            lax.fori_loop(max(1, x * z_size), (x + 1) * z_size, arrive, 0)
        data, highs, lows = [], [], []
        for x in steps:
            for d in range(x * z_size, (x + 1) * z_size, 2):
                a, b = recv[d], recv[d + 1]
                at, bt, ap, bp = a[0:16], b[0:16], a[16:17], b[16:17]
                data.append(split_rows(jnp.concatenate(
                    [jnp.where(left16, at, swap(bt)), jnp.where(left16, swap(at), bt)], axis=0)))
                highs.append(jnp.where(left, ap, swap(bp)).astype(I32))
                lows.append(jnp.where(left, swap(ap), bp).astype(I32))
        rows_of = iota((GROUP, 128), 0)
        low_hot = jnp.concatenate([ones_where(rows_of == low).astype(BF16) for low in lows], axis=1)
        data = masked_groups(jnp.concatenate(data, axis=1), jnp.concatenate(highs, axis=1))
        add_groups(mm(data, low_hot, NT), base_ref, r_ref)

    place(far_first[:x_size // 2], load)
    place(far_first[x_size // 2:], r_ref)

    def trace_copy(turn, half):
        lanes = pl.ds(half * (traces // 2), traces // 2)
        return pltpu.make_async_remote_copy(
            src_ref=own.at[turn, :, lanes], dst_ref=part.at[turn, :, lanes], send_sem=tr_send.at[turn, half],
            recv_sem=tr_recv.at[turn, half], device_id={"patch": other}, device_id_type=MESH,
        )

    def halves_of(v_ref, base):
        for h in range(groups):
            lanes = slice(h * GROUP, (h + 1) * GROUP)
            s3[base:base + 64, lanes] = split_rows(v_ref[:, lanes])

    def send_trace(turn, base):
        stacked = jnp.concatenate([s3[base:base + 64, h * GROUP:(h + 1) * GROUP] for h in range(groups)], axis=0)
        for c in range(chunks):
            lanes = slice(c * GROUP, (c + 1) * GROUP)
            picked = mm(stacked, hot[:, lanes])
            high = trace_ref[:, lanes] >> 8
            total = jnp.zeros((32, GROUP), F32)
            for h in range(groups):
                total = jnp.where(high == h, picked[h * 64:h * 64 + 32] + picked[h * 64 + 32:h * 64 + 64], total)
            own[turn, :, lanes] = total
            if turn == 0 and c + 1 == chunks // 2:
                trace_copy(turn, 0).start()
        if turn == 1:
            trace_copy(turn, 0).start()
        trace_copy(turn, 1).start()

    def strains(v_ref):
        for i in range(pairs):
            tile = v_ref[:, i * 128:(i + 1) * 128]
            turned = swap(tile)
            vab[4 * i] = split_rows(jnp.where(left32, tile, 0.0))
            vab[4 * i + 1] = split_rows(jnp.where(left32, 0.0, turned))
            vab[4 * i + 2] = split_rows(jnp.where(left32, turned, 0.0))
            vab[4 * i + 3] = split_rows(jnp.where(left32, 0.0, tile))

        for n in range(rows):
            c0, c1, c2, c3 = (cols_smem[k, n] for k in range(4))
            x = jnp.concatenate(
                [vab[2 * c0] + vab[2 * c1 + 1], vab[2 * c2] + vab[2 * c3 + 1]], axis=1)
            o = mm(x, kt[n])
            o = o[0:32] + o[32:64]
            ss[:, n * 128:(n + 1) * 128] = split_rows(o + swap(o))

    def forces():
        for n in range(rows):
            o = mm(ss[:, n * 128:(n + 1) * 128], kk[n])
            o = o[0:32] + o[32:64]
            for half in range(2):
                tile = o[:, half * 128:(half + 1) * 128]
                top, bottom = tile[0:16], tile[16:32]
                tp[n * 4 + 2 * half] = jnp.where(left16, top, swap(bottom))
                tp[n * 4 + 2 * half + 1] = jnp.where(left16, swap(top), bottom)

    def gather_forces(v_ref, out_ref):
        def add_up(step, total):
            for u in range(8):
                i = step * 8 + u
                total = total * csr_fs[0, i] + tp[csr_is[0, i]]
                run[i] = total
            return total

        lax.fori_loop(0, entries // 8, add_up, jnp.zeros((16, 128), F32))
        for i in range(pairs):
            lanes = slice(i * 128, (i + 1) * 128)
            a = run[csr_is[1, 2 * i]] * csr_fs[1, 2 * i]
            b = run[csr_is[1, 2 * i + 1]] * csr_fs[1, 2 * i + 1]
            tile = jnp.concatenate(
                [jnp.where(left16, a, swap(b)), jnp.where(left16, swap(a), b)], axis=0)
            out_ref[:, lanes] = tile + mass_ref[:, lanes] * v_ref[:, lanes]

    def add_jump(jump, out_ref):
        add_groups(mm(masked_groups(jump, trace_ref[...] >> 8), hot[...], NT), out_ref, out_ref)

    sent = []

    def stage(pay, index, slots, count, place, base):
        copies = []
        for j in range(1, count):
            copies.append(pltpu.make_async_remote_copy(
                src_ref=pay.at[index], dst_ref=slots.at[j - 1], send_sem=red_send.at[base + j],
                recv_sem=red_recv.at[base + j], device_id=place(j), device_id_type=MESH))
        for j in sorted(range(1, count), key=lambda j: -min(j, count - j)):
            copies[j - 1].start()
        sent.extend(copies)

        def finish():
            total = pay[index]
            for j, copy in enumerate(copies):
                copy.wait_recv()
                total += slots[j]
            return total

        return finish

    z_first = (me // z_size) * z_size
    span = comps + x_size + z_size

    def along_comp(j):
        return {"comp": lax.rem(mine + j, comps)}

    def along_x(j):
        return {"patch": lax.rem(me + j * z_size, patches)}

    def along_z(j):
        return {"patch": z_first + lax.rem(lax.rem(me, z_size) + j, z_size)}

    weight = pen_ref[...] * pen_other[...]
    halves_of(r_ref, 0)
    send_trace(0, 0)
    strains(r_ref)
    forces()
    gather_forces(r_ref, q_ref)
    halves_of(q_ref, 64)
    send_trace(1, 64)
    o = mm(s3[0:64], s3[0:64], NT)
    fold[32:64, 0:64] = o[0:32] + o[32:64]
    zeroth = fold[32:64]
    pay_m[0] = pack4(zeroth + pltpu.roll(zeroth, 96, 1), 0)
    m_z = stage(pay_m, 0, rz_m, z_size, along_z, 2 * span + comps + x_size)
    trace_copy(0, 0).wait_recv()
    trace_copy(0, 1).wait_recv()
    first_jump = split_rows(weight * (own[0] - part[0]))
    add_jump(first_jump, q_ref)
    halves_of(q_ref, 64)

    o = mm(s3[0:128], s3[64:128], NT)
    fold[64:96, 0:64] = o[0:32] + o[32:64]
    fold[96:128, 0:64] = o[64:96] + o[96:128]
    early = fold[64:128]
    early = early + pltpu.roll(early, 96, 1)
    pay_a[0] = jnp.concatenate([pack4(early[32 * i:32 * i + 32], 0) for i in range(2)], axis=0)
    a_z = stage(pay_a, 0, rz_a, z_size, along_z, comps + x_size)
    strains(q_ref)

    strain = ss[...]
    energy = mm(strain, strain, NT) * 0.5 + mm(split_rows(mass_ref[...] * q_ref[...]), s3[64:128], NT)
    turn = mm(first_jump, twins[...])
    trace_copy(1, 0).wait_recv()
    trace_copy(1, 1).wait_recv()
    jump = own[1] - part[1] + turn[0:32] + turn[32:64]
    energy += mm(split_rows(0.5 * weight * jump), split_rows(jump), NT)
    fold[0:32, 0:64] = energy[0:32] + energy[32:64]
    third = fold[0:32]
    third = third + pltpu.roll(third, 96, 1)
    pay_b[0] = pack4(third, 0)
    b_comp = stage(pay_b, 0, rc_b, comps, along_comp, span)

    pay_m[1] = m_z()
    m_x = stage(pay_m, 1, rx_m, x_size, along_x, 2 * span + comps)
    forces()
    gather_forces(q_ref, t_ref)
    add_jump(split_rows(weight * jump), t_ref)
    halves_of(t_ref, 128)
    pay_a[1] = a_z()
    a_x = stage(pay_a, 1, rx_a, x_size, along_x, comps)
    pay_b[1] = b_comp()
    b_x = stage(pay_b, 1, rx_b, x_size, along_x, span + comps)
    pay_m[2] = m_x()
    m_comp = stage(pay_m, 2, rc_m, comps, along_comp, 2 * span)
    pay_a[2] = a_x()
    a_comp = stage(pay_a, 2, rc_a, comps, along_comp, 0)
    pay_b[2] = b_x()
    b_z = stage(pay_b, 2, rz_b, z_size, along_z, span + comps + x_size)

    def drain(d, _):
        cell_copy(d).wait_send()
        return 0

    lax.fori_loop(1, patches, drain, 0)
    pen_copy.wait_send()
    other_copy.wait_send()
    trace_copy(0, 0).wait_send()
    trace_copy(0, 1).wait_send()
    trace_copy(1, 0).wait_send()
    trace_copy(1, 1).wait_send()

    total = a_comp()
    m0, m1, m2 = m_comp(), total[0:8], total[8:16]
    upper = unpack4(m1, 0) + unpack4(m2, 1) + unpack4(m0, 2)
    lower = unpack4(m2, 0) + unpack4(m1, 2)
    system = eliminate(jnp.concatenate([upper, lower], axis=0), 0, 32)
    lower = system[32:64] + unpack4(b_z(), 1)
    system = eliminate(jnp.concatenate([system[0:32], lower], axis=0), 32, 64)
    mixed = jnp.concatenate([system[0:32], system[0:32], system[32:64], system[32:64]], axis=0)
    weights_ref[...] = split_rows(jnp.transpose(mixed)[64:96])
    for copy in sent:
        copy.wait_send()


def finish(weights_ref, s3, r_ref, sol_hbm, res_hbm, sol, res, sems):
    weights = weights_ref[...]
    dofs = sol.shape[1]
    width = dofs // 4
    copies = []
    for part in range(4):
        for h in range(width // GROUP):
            lanes = slice(part * width + h * GROUP, part * width + (h + 1) * GROUP)
            o = mm(weights, s3[0:128, lanes])
            sol[:, lanes] = o[0:32] + o[32:64]
            o = mm(weights, s3[64:192, lanes])
            res[:, lanes] = r_ref[:, lanes] - (o[0:32] + o[32:64])
        lanes = pl.ds(part * width, width)
        for i, (src, dst) in enumerate(((sol, sol_hbm), (res, res_hbm))):
            copies.append(pltpu.make_async_copy(src.at[:, lanes], dst.at[:, lanes], sems.at[part, i]))
            copies[-1].start()
    for copy in copies:
        copy.wait()


def shards(z_size, load_cases, mass_diag, stiffness, block_cols, trace_dofs, penalty, cell_partials, cell_owner, cell_dof):
    cases, dofs = load_cases.shape
    rows = stiffness.shape[0]
    traces, ncell = trace_dofs.shape[0], cell_dof.shape[0]
    patches, comps = lax.axis_size("patch"), lax.axis_size("comp")
    groups = dofs // GROUP
    entries = rows * 4
    vm = pl.BlockSpec(memory_space=pltpu.VMEM)
    hbm = pl.BlockSpec(memory_space=pltpu.HBM)
    field = jax.ShapeDtypeStruct((cases, dofs), F32)
    x_size = patches // z_size
    stages = comps + x_size + z_size

    def sums(tall):
        return [
            pltpu.VMEM((3, tall, 128), F32),
            pltpu.VMEM((comps - 1, tall, 128), F32),
            pltpu.VMEM((x_size - 1, tall, 128), F32),
            pltpu.VMEM((z_size - 1, tall, 128), F32),
        ]

    right_side, parts, weights = pl.pallas_call(
        functools.partial(kernel, z_size),
        out_shape=(
            field, jax.ShapeDtypeStruct((6 * cases, dofs), BF16), jax.ShapeDtypeStruct((2 * cases, 128), BF16)),
        in_specs=[hbm] * 9,
        out_specs=(vm, vm, vm),
        scratch_shapes=[
            pltpu.VMEM((cases, dofs), F32),
            pltpu.VMEM((1, dofs), F32),
            pltpu.VMEM(stiffness.shape, F32),
            pltpu.VMEM((4, rows), I32),
            pltpu.SMEM((4, rows), I32),
            pltpu.VMEM((1, traces), I32),
            pltpu.VMEM((1, traces), F32),
            pltpu.VMEM((cases, ncell), F32),
            pltpu.VMEM((1, ncell), I32),
            pltpu.VMEM((1, ncell), I32),
            pltpu.VMEM((rows, 128, 256), BF16),
            pltpu.VMEM((rows, 256, 128), BF16),
            pltpu.VMEM((patches, 17, 128), F32),
            pltpu.VMEM((patches, 17, 128), F32),
            pltpu.VMEM((4, 128), I32),
            pltpu.VMEM((2, GROUP), I32),
            pltpu.VMEM((2, GROUP), F32),
            pltpu.SMEM((2, GROUP), I32),
            pltpu.SMEM((2, GROUP), F32),
            pltpu.VMEM((GROUP, traces), BF16),
            pltpu.VMEM((2, cases, traces), F32),
            pltpu.VMEM((2, cases, traces), F32),
            pltpu.VMEM((1, traces), F32),
            pltpu.VMEM((1, traces), I32),
            pltpu.VMEM((traces, traces), BF16),
            pltpu.VMEM((cases, dofs), F32),
            pltpu.VMEM((cases, dofs), F32),
            pltpu.VMEM((2 * rows, 64, 128), BF16),
            pltpu.VMEM((64, rows * 128), BF16),
            pltpu.VMEM((entries, 16, 128), F32),
            pltpu.VMEM((entries, 16, 128), F32),
            pltpu.VMEM((4 * cases, 128), F32),
            *sums(16),
            *sums(8),
            *sums(8),
            pltpu.SemaphoreType.DMA((12,)),
            pltpu.SemaphoreType.DMA((patches,)),
            pltpu.SemaphoreType.DMA((patches,)),
            pltpu.SemaphoreType.DMA((3, 2)),
            pltpu.SemaphoreType.DMA((3, 2)),
            pltpu.SemaphoreType.DMA((3 * stages,)),
            pltpu.SemaphoreType.DMA((3 * stages,)),
        ],
        compiler_params=pltpu.CompilerParams(
            collective_id=0, has_side_effects=True, vmem_limit_bytes=40 * 1024 * 1024),
    )(
        *(pltpu.with_memory_space_constraint(x, pltpu.HBM) for x in (
            load_cases, mass_diag.reshape(1, -1), stiffness, block_cols.T, trace_dofs.reshape(1, -1),
            penalty.reshape(1, -1), cell_partials, cell_owner.reshape(1, -1), cell_dof.reshape(1, -1)))
    )
    return pl.pallas_call(
        finish,
        out_shape=(field, field),
        in_specs=[vm, vm, vm],
        out_specs=(hbm, hbm),
        scratch_shapes=[
            pltpu.VMEM((cases, dofs), F32),
            pltpu.VMEM((cases, dofs), F32),
            pltpu.SemaphoreType.DMA((4, 2)),
        ],
        compiler_params=pltpu.CompilerParams(vmem_limit_bytes=8 * 1024 * 1024),
    )(weights, parts, right_side)


def solution(mesh):
    patches = mesh.shape["patch"]
    z_size = 8 if patches == 32 else patches // 2
    both = ("comp", "patch")
    return jax.shard_map(
        functools.partial(shards, z_size),
        mesh=mesh,
        in_specs=(
            P(None, both), P(both), P(both, None, None), P(both, None), P(both), P(both), P(None, both),
            P(both, None), P(both),
        ),
        out_specs=(P(None, both), P(None, both)),
        check_vma=False,
    )
```
